256 devices in a mesh: tile: 64 (over y, x_hi, z), freq: 4 (over x_lo, core).
Axes of the slice: x: 4 (x_hi: 2, x_lo: 2; x = x_hi * 2 + x_lo), y: 4, z: 8, core: 2. Of those that a mesh axis runs over, the one named last changes fastest.
Arguments:
- source_field: float32 [2, 8, 1536, 1024], P(None, 'freq', 'tile'), may hold values from -6 to 6
- receiver_field: float32 [2, 8, 1536, 1024], P(None, 'freq', 'tile'), may hold values from -6 to 6
- slowness: float32 [2, 1536, 1024], P(None, 'tile', 'freq'), may hold values from 0.5 to 1
- frequency: float32 [8], P('freq'), may hold values from 0.5 to 2
- order_table: int32 [2, 8], P(None, 'freq'), may hold values from 2 to 4, as said below
- filter_coeffs: float32 [2, 5, 3], replicated, may hold values from -2 to 2
- aperture: int32 [64], replicated, may hold values from 8 to 24, as said below
Outputs:
- image_out: float32 [2, 1536, 1024], P(None, 'tile', 'freq')
- receiver_out: float32 [2, 8, 1536, 1024], P(None, 'freq', 'tile')
The draws below stay inside these ranges and needn't reach their ends.
Inputs may be any that keep to these rules, and one draw needn't show every extreme that they name: Tile t holds aperture[t] grid rows; the entries sum to 1024, and some tile holds exactly 24. `order_table`: the order 4 occurs in every draw.
All inputs are finite; a program needn't handle non-finite values.
Results may differ from the reference program's by a relative error of at most 0.0003.
Values sent between devices are 32-bit elements; how exact they have to be, the bound alone decides.
A program may use at most 64 MiB of HBM per device.

```python
import math
import jax
import jax.numpy as jnp
from jax import lax

ROWS = 16
NY = 1024
ORDER = 4
POWERS = 3
NDEPTH = 2
CAP = 24
NX = 1024
FREQS = 8
N_TILE = 64


def draw_aperture(key, part):
    tile_count = NX // ROWS
    half_rows = ROWS // 2
    shifts = jax.random.randint(key, (tile_count,), 0, half_rows + 1)
    shifts = shifts.at[0].set(half_rows).at[1].set(0)
    return (ROWS + shifts - jnp.roll(shifts, -1)).astype(jnp.int32)


def draw_order_table(key, part):
    order_draw = jax.random.randint(key, (NDEPTH, FREQS), 2, ORDER + 1)
    order_draw = order_draw.at[0, 0].set(ORDER).at[NDEPTH - 1, FREQS - 1].set(2)
    return order_draw.astype(jnp.int32)


def block_levels(own_key, extent, cuts, smallest, high):
    def one(axis_at, parts):
        heights = jax.random.uniform(jax.random.fold_in(jax.random.fold_in(own_key, 6), axis_at), (parts,), jnp.float32, smallest / len(cuts), high / len(cuts))
        return jnp.repeat(jnp.exp(heights), extent[axis_at] // parts).reshape((-1,) + (1,) * (len(extent) - axis_at - 1))

    factor_of = one(*cuts[0])
    for cut in cuts[1:]:
        factor_of = factor_of * one(*cut)
    return factor_of


def scatter_about(key, extent, scale, reach, shards=(), held_as=jnp.bfloat16):
    gain = block_levels(key, extent, shards, -0.22, 0.18) if shards else 1.0
    array = jax.random.normal(key, extent, jnp.float32) * scale * gain
    return jnp.minimum(jnp.maximum(array, -reach), reach).astype(held_as)


def setup_inputs(seed: int = 0) -> dict:
    arg_keys = jax.random.split(jax.random.key(seed), 8)
    source_field = scatter_about(arg_keys[0], (2, FREQS, N_TILE * CAP, NY), 1.0, 6.0, ((1, 4), (2, 64)), jnp.float32)
    receiver_field = scatter_about(arg_keys[1], (2, FREQS, N_TILE * CAP, NY), 1.0, 6.0, ((1, 4), (2, 64)), jnp.float32)
    slowness = jnp.clip(jnp.exp(math.log(1.0) - 0.6931472 * jax.random.uniform(arg_keys[2], (NDEPTH, N_TILE * CAP, NY), jnp.float32) ** block_levels(arg_keys[2], (NDEPTH, N_TILE * CAP, NY), ((1, 64), (2, 4)), -0.2, 0.2)), 0.5, 1.0)
    frequency = jnp.clip(jnp.exp(math.log(2.0) - 1.3862944 * jax.random.uniform(arg_keys[3], (FREQS,), jnp.float32) ** block_levels(arg_keys[3], (FREQS,), ((0, 4),), -0.2, 0.2)), 0.5, 2.0)
    order_table = draw_order_table(jax.random.fold_in(arg_keys[7], 71), 0)
    filter_coeffs = scatter_about(arg_keys[5], (2, ORDER + 1, POWERS), 0.15, 2.0, (), jnp.float32)
    aperture = draw_aperture(jax.random.fold_in(arg_keys[7], 71), 0)
    return {"source_field": source_field, "receiver_field": receiver_field, "slowness": slowness, "frequency": frequency, "order_table": order_table, "filter_coeffs": filter_coeffs, "aperture": aperture}


def mcclellan(values):
    lead = [(0, 0)] * (values.ndim - 2)
    padded_x = jnp.pad(values, lead + [(1, 1), (0, 0)])
    blur_rows = 0.25 * (padded_x[..., :-2, :] + padded_x[..., 2:, :]) + 0.5 * values
    padded_cols = jnp.pad(blur_rows, lead + [(0, 0), (1, 1)])
    blur_cols = 0.25 * (padded_cols[..., :-2] + padded_cols[..., 2:]) + 0.5 * blur_rows
    return 2.0 * blur_cols - values


def weighted(term_index, cheb_term, wavenumber, coeffs, active):
    powers = coeffs.shape[2]
    coef_re = coeffs[0, term_index, powers - 1] + 0.0 * wavenumber
    coef_im = coeffs[1, term_index, powers - 1] + 0.0 * wavenumber
    for power_index in range(powers - 2, -1, -1):
        coef_re = coef_re * wavenumber + coeffs[0, term_index, power_index]
        coef_im = coef_im * wavenumber + coeffs[1, term_index, power_index]
    coef_re = coef_re * active
    coef_im = coef_im * active
    src_re = coef_re * cheb_term[0, 0] + coef_im * cheb_term[0, 1]
    src_im = coef_re * cheb_term[0, 1] - coef_im * cheb_term[0, 0]
    rec_re = coef_re * cheb_term[1, 0] - coef_im * cheb_term[1, 1]
    rec_im = coef_re * cheb_term[1, 1] + coef_im * cheb_term[1, 0]
    return jnp.stack([jnp.stack([src_re, src_im]), jnp.stack([rec_re, rec_im])])


def reference(source_field, receiver_field, slowness, frequency, order_table, filter_coeffs, aperture):
    starts = (jnp.cumsum(aperture) - aperture).astype(jnp.int32)
    global_row = jnp.arange(NX, dtype=jnp.int32)
    owner_tile = jnp.sum((global_row[:, None] >= starts[None, 1:]).astype(jnp.int32), axis=1).astype(jnp.int32)
    slot_index = (owner_tile * CAP + global_row - starts[owner_tile]).astype(jnp.int32)
    fields = jnp.stack([source_field[:, :, slot_index, :], receiver_field[:, :, slot_index, :]])
    fields = jnp.transpose(fields, (2, 0, 1, 3, 4))
    planes = slowness[:, slot_index, :]
    orders = jnp.transpose(order_table, (1, 0))

    def one_frequency(inputs):
        state, angular, order_column = inputs
        images = []
        for depth_index in range(NDEPTH):
            wavenumber = angular * planes[depth_index]
            previous = state
            current = mcclellan(state)
            result = weighted(0, previous, wavenumber, filter_coeffs, (order_column[depth_index] >= 0).astype(jnp.float32))
            result = result + weighted(1, current, wavenumber, filter_coeffs, (order_column[depth_index] >= 1).astype(jnp.float32))
            for term_index in range(2, ORDER + 1):
                following = 2.0 * mcclellan(current) - previous
                result = result + weighted(term_index, following, wavenumber, filter_coeffs, (order_column[depth_index] >= term_index).astype(jnp.float32))
                previous, current = current, following
            state = result
            images.append(state[0, 0] * state[1, 0] + state[0, 1] * state[1, 1])
        return jnp.stack(images), state[1]

    image_terms, receivers = lax.map(one_frequency, (fields, frequency, orders))
    image_sum = jnp.sum(image_terms, axis=0)
    stored = N_TILE * CAP
    image_out = jnp.zeros((NDEPTH, stored, NY), jnp.float32).at[:, slot_index, :].set(image_sum)
    receivers = jnp.transpose(receivers, (1, 0, 2, 3))
    receiver_out = jnp.zeros((2, receivers.shape[1], stored, NY), jnp.float32).at[:, :, slot_index, :].set(receivers)
    return image_out, receiver_out
```

```python
import functools

import jax
import jax.numpy as jnp
from jax import lax
from jax.experimental import pallas as pl
from jax.experimental.pallas import tpu as pltpu
from jax.sharding import PartitionSpec as P

ORDER = 4
NDEPTH = 2
HALO = 4
LEAD = 8
SPARE = 8


def passed_along(value, axis, steps):
    count = lax.axis_size(axis)
    initial, last = (max(0, -steps), min(count, count - steps))
    return lax.ppermute(value, axis, [(source, source + steps) for source in range(initial, last)])


def depth_kernel(ints, flts, ext_ref, slow_ref, out_ref, img_ref, tb):
    _, _, nf, ext_rows, ncol = ext_ref.shape
    own = out_ref.shape[3]
    powers = 3
    ap = ints[0]
    has_above = ints[1] > 0
    has_below = ints[2] > 0
    rows = lax.broadcasted_iota(jnp.int32, (ext_rows, ncol), 0)
    valid = (
        ((rows >= LEAD - HALO) & (rows < LEAD) & has_above)
        | ((rows >= LEAD) & (rows < LEAD + ap))
        | ((rows >= LEAD + ap) & (rows < LEAD + HALO + ap) & has_below)
    )
    cols = lax.broadcasted_iota(jnp.int32, (ext_rows, ncol), 1)
    left_ok = jnp.abs(pltpu.roll(cols, 1, 1) - cols) == 1
    right_ok = jnp.abs(pltpu.roll(cols, ncol - 1, 1) - cols) == 1
    live = lax.broadcasted_iota(jnp.int32, (own, ncol), 0) < ap

    def spread(v):
        blur_rows = 0.25 * (pltpu.roll(v, 1, 0) + pltpu.roll(v, ext_rows - 1, 0)) + 0.5 * v
        side = jnp.where(left_ok, pltpu.roll(blur_rows, 1, 1), 0.0) + jnp.where(
            right_ok, pltpu.roll(blur_rows, ncol - 1, 1), 0.0
        )
        blur_cols = 0.25 * side + 0.5 * blur_rows
        return 2.0 * blur_cols - v

    for f in range(nf):
        wavenumber = flts[f] * slow_ref[...]

        def coefficient(n):
            base = nf
            coef_re = flts[base + n * powers + powers - 1] + 0.0 * wavenumber
            coef_im = flts[base + (ORDER + 1) * powers + n * powers + powers - 1] + 0.0 * wavenumber
            for m in range(powers - 2, -1, -1):
                coef_re = coef_re * wavenumber + flts[base + n * powers + m]
                coef_im = coef_im * wavenumber + flts[base + (ORDER + 1) * powers + n * powers + m]
            active = ints[3 + f * (ORDER + 1) + n].astype(jnp.float32)
            return coef_re * active, coef_im * active

        def accumulate(n, slot):
            coef_re, coef_im = coefficient(n)
            s_re = tb[slot, 0, LEAD:LEAD + own, :]
            s_im = tb[slot, 1, LEAD:LEAD + own, :]
            r_re = tb[slot, 2, LEAD:LEAD + own, :]
            r_im = tb[slot, 3, LEAD:LEAD + own, :]
            terms = (
                coef_re * s_re + coef_im * s_im,
                coef_re * s_im - coef_im * s_re,
                coef_re * r_re - coef_im * r_im,
                coef_re * r_im + coef_im * r_re,
            )
            for p in range(4):
                if n == 0:
                    out_ref[p // 2, p % 2, f] = terms[p]
                else:
                    out_ref[p // 2, p % 2, f] = out_ref[p // 2, p % 2, f] + terms[p]

        for p in range(4):
            tb[0, p] = jnp.where(valid, ext_ref[p // 2, p % 2, f], 0.0)
        accumulate(0, 0)
        for n in range(1, ORDER + 1):
            cur, prev, nxt = (n - 1) % 3, (n - 2) % 3, n % 3
            for p in range(4):
                g = spread(tb[cur, p])
                if n > 1:
                    g = 2.0 * g - tb[prev, p]
                tb[nxt, p] = jnp.where(valid, g, 0.0)
            accumulate(n, nxt)

        for p in range(4):
            out_ref[p // 2, p % 2, f] = jnp.where(live, out_ref[p // 2, p % 2, f], 0.0)
        term = out_ref[0, 0, f] * out_ref[1, 0, f] + out_ref[0, 1, f] * out_ref[1, 1, f]
        if f == 0:
            img_ref[...] = term
        else:
            img_ref[...] = img_ref[...] + term


def depth_step(ints, flts, ext, slow, own):
    nfield, nc, nf, ext_rows, ncol = ext.shape
    vmem = pltpu.MemorySpace.VMEM
    smem = pltpu.MemorySpace.SMEM
    elements = nfield * nc * nf * ext_rows * ncol
    return pl.pallas_call(
        depth_kernel,
        out_shape=(
            jax.ShapeDtypeStruct((nfield, nc, nf, own, ncol), jnp.float32),
            jax.ShapeDtypeStruct((own, ncol), jnp.float32),
        ),
        in_specs=[
            pl.BlockSpec(memory_space=smem),
            pl.BlockSpec(memory_space=smem),
            pl.BlockSpec(memory_space=vmem),
            pl.BlockSpec(memory_space=vmem),
        ],
        out_specs=(pl.BlockSpec(memory_space=vmem), pl.BlockSpec(memory_space=vmem)),
        scratch_shapes=[pltpu.VMEM((3, 4, ext_rows, ncol), jnp.float32)],
        cost_estimate=pl.CostEstimate(
            flops=elements * 100, bytes_accessed=elements * 4 * 2, transcendentals=0
        ),
    )(ints, flts, ext, slow)


def extended(fields, tile_width):
    row_axis = fields.ndim - 2
    upper_rows = lax.dynamic_slice_in_dim(fields, tile_width - HALO, HALO, row_axis)
    lower_rows = fields[..., :HALO, :]
    from_below = passed_along(upper_rows, "tile", 1)
    from_above = passed_along(lower_rows, "tile", -1)
    lead = jnp.zeros(fields.shape[:-2] + (LEAD - HALO, fields.shape[-1]), fields.dtype)
    spare = jnp.zeros(fields.shape[:-2] + (SPARE, fields.shape[-1]), fields.dtype)
    joined = jnp.concatenate([lead, from_below, fields, spare], axis=row_axis)
    return lax.dynamic_update_slice_in_dim(joined, from_above, LEAD + tile_width, row_axis)


def shards(source_field, receiver_field, slowness, frequency, order_table, filter_coeffs, aperture):
    tile_index = lax.axis_index("tile")
    tile_count = lax.axis_size("tile")
    row_count = source_field.shape[2]
    tile_width = aperture[tile_index]
    live_rows = (jnp.arange(row_count, dtype=jnp.int32) < tile_width).astype(jnp.float32)[:, None]
    fields = jnp.stack([source_field, receiver_field]) * live_rows
    planes = lax.all_gather(slowness, "freq", axis=2, tiled=True)
    flts = jnp.concatenate([frequency, filter_coeffs.reshape(-1)])
    flags = jnp.stack(
        [tile_width, (tile_index > 0).astype(jnp.int32), (tile_index < tile_count - 1).astype(jnp.int32)]
    )
    images = []
    for depth_index in range(NDEPTH):
        active = (
            jnp.arange(ORDER + 1, dtype=jnp.int32)[None, :] <= order_table[depth_index][:, None]
        ).astype(jnp.int32)
        ints = jnp.concatenate([flags, active.reshape(-1)])
        ext = extended(fields, tile_width)
        fields, image = depth_step(ints, flts, ext, planes[depth_index], row_count)
        images.append(image)
    stacked = jnp.stack(images)
    image_out = lax.psum_scatter(stacked, "freq", scatter_dimension=2, tiled=True)
    return (image_out, fields[1])


def solution(mesh):
    placed = (
        P(None, "freq", "tile", None),
        P(None, "freq", "tile", None),
        P(None, "tile", "freq"),
        P("freq"),
        P(None, "freq"),
        P(),
        P(),
    )
    return jax.shard_map(
        shards,
        mesh=mesh,
        in_specs=placed,
        out_specs=(P(None, "tile", "freq"), P(None, "freq", "tile", None)),
        check_vma=False,
    )
```

```python
import functools

import jax
import jax.numpy as jnp
from jax import lax
from jax.experimental import pallas as pl
from jax.experimental.pallas import tpu as pltpu
from jax.sharding import PartitionSpec as P

ORDER = 4
NDEPTH = 2
POWERS = 3
HALO = 8
MESH = pl.DeviceIdType.MESH
VMEM = pltpu.MemorySpace.VMEM
SMEM = pltpu.MemorySpace.SMEM


def migrate_kernel(n_tile, n_freq, ints, flts, src_ref, rec_ref, slow_ref, f_up, f_lo, s_up, s_lo,
                   rec_out, img_out, g_slow, h_sa, h_sb, h_fa, h_fb, s1, tb, send_sem, recv_sem):
    t = lax.axis_index("tile")
    f = lax.axis_index("freq")
    nc, nfl, own, ncol = src_ref.shape
    ext_rows = HALO + own + HALO
    block = slow_ref.shape[2]
    ap = ints[0]
    has_above = t > 0
    has_below = t < n_tile - 1

    g_slow[f] = slow_ref[...]

    @pl.when(t == 0)
    def _():
        h_fa[...] = jnp.zeros_like(h_fa)
        h_sa[...] = jnp.zeros_like(h_sa)

    @pl.when(t == n_tile - 1)
    def _():
        h_fb[...] = jnp.zeros_like(h_fb)
        h_sb[...] = jnp.zeros_like(h_sb)

    barrier = pltpu.get_barrier_semaphore()
    for q in range(n_freq):
        @pl.when(f != q)
        def _():
            pl.semaphore_signal(barrier, 1, device_id=(t, q), device_id_type=MESH)

        @pl.when(has_above)
        def _():
            pl.semaphore_signal(barrier, 1, device_id=(t - 1, q), device_id_type=MESH)

        @pl.when(has_below)
        def _():
            pl.semaphore_signal(barrier, 1, device_id=(t + 1, q), device_id_type=MESH)

    expected = (n_freq - 1) + n_freq * has_above.astype(jnp.int32) + n_freq * has_below.astype(jnp.int32)
    pl.semaphore_wait(barrier, expected)

    def remote(src, dst, slot_send, slot_recv, device):
        return pltpu.make_async_remote_copy(
            src_ref=src, dst_ref=dst, send_sem=send_sem.at[slot_send], recv_sem=recv_sem.at[slot_recv],
            device_id=device, device_id_type=MESH,
        )

    for q in range(n_freq):
        @pl.when(f != q)
        def _():
            remote(slow_ref, g_slow.at[f], q, f, (t, q)).start()

        @pl.when(has_below)
        def _():
            remote(s_up, h_sa.at[f], n_freq + q, n_freq + f, (t + 1, q)).start()

        @pl.when(has_above)
        def _():
            remote(s_lo, h_sb.at[f], 2 * n_freq + q, 2 * n_freq + f, (t - 1, q)).start()

    @pl.when(has_below)
    def _():
        remote(f_up, h_fa, 3 * n_freq, 3 * n_freq, (t + 1, f)).start()

    @pl.when(has_above)
    def _():
        remote(f_lo, h_fb, 3 * n_freq + 1, 3 * n_freq + 1, (t - 1, f)).start()

    for q in range(n_freq):
        @pl.when(f != q)
        def _():
            remote(slow_ref, g_slow.at[q], q, q, (t, q)).wait_send()
            remote(slow_ref, g_slow.at[q], q, q, (t, q)).wait_recv()

        @pl.when(has_below)
        def _():
            remote(s_up, h_sa.at[q], n_freq + q, n_freq + q, (t + 1, q)).wait_send()
            remote(s_lo, h_sb.at[q], 2 * n_freq + q, 2 * n_freq + q, (t + 1, q)).wait_recv()

        @pl.when(has_above)
        def _():
            remote(s_lo, h_sb.at[q], 2 * n_freq + q, 2 * n_freq + q, (t - 1, q)).wait_send()
            remote(s_up, h_sa.at[q], n_freq + q, n_freq + q, (t - 1, q)).wait_recv()

    @pl.when(has_below)
    def _():
        remote(f_up, h_fa, 3 * n_freq, 3 * n_freq, (t + 1, f)).wait_send()
        remote(f_lo, h_fb, 3 * n_freq + 1, 3 * n_freq + 1, (t + 1, f)).wait_recv()

    @pl.when(has_above)
    def _():
        remote(f_lo, h_fb, 3 * n_freq + 1, 3 * n_freq + 1, (t - 1, f)).wait_send()
        remote(f_up, h_fa, 3 * n_freq, 3 * n_freq, (t - 1, f)).wait_recv()

    rows = lax.broadcasted_iota(jnp.int32, (ext_rows, ncol), 0)
    cols = lax.broadcasted_iota(jnp.int32, (ext_rows, ncol), 1)
    left_ok = jnp.abs(pltpu.roll(cols, 1, 1) - cols) == 1
    right_ok = jnp.abs(pltpu.roll(cols, ncol - 1, 1) - cols) == 1
    forward = pltpu.roll(rows, 1, 0) == (rows + ext_rows - 1) % ext_rows
    lower_start = HALO + ap
    top_part = rows < lower_start

    def in_band(lo, hi):
        return (rows >= lo) & (rows < hi)

    valid0 = (in_band(0, HALO) & has_above) | in_band(HALO, lower_start) | (
        in_band(lower_start, lower_start + HALO) & has_below)
    reach = HALO // 2
    valid1 = (in_band(HALO - reach, HALO) & has_above) | in_band(HALO, lower_start) | (
        in_band(lower_start, lower_start + reach) & has_below)
    live = lax.broadcasted_iota(jnp.int32, (own, ncol), 0) < ap
    zeros_tail = jnp.zeros((ext_rows - HALO, ncol), jnp.float32)

    def place_lower(lower8):
        padded = jnp.concatenate([lower8, zeros_tail], axis=0)
        ahead = pltpu.roll(padded, lower_start, 0)
        behind = pltpu.roll(padded, ext_rows - lower_start, 0)
        return jnp.where(forward, ahead, behind)

    def joined(upper8, own_rows, lower8):
        top = jnp.concatenate([upper8, own_rows, jnp.zeros((HALO, ncol), jnp.float32)], axis=0)
        return jnp.where(top_part, top, place_lower(lower8))

    def columns_of(pieces):
        return jnp.concatenate(pieces, axis=1)

    slow0 = joined(
        columns_of([h_sa[q] for q in range(n_freq)]),
        columns_of([g_slow[q, 0] for q in range(n_freq)]),
        columns_of([h_sb[q] for q in range(n_freq)]),
    )
    slow0 = jnp.where(valid0, slow0, 0.0)
    slow1 = columns_of([g_slow[q, 1] for q in range(n_freq)])

    def spread(v):
        blur_rows = 0.25 * (pltpu.roll(v, 1, 0) + pltpu.roll(v, ext_rows - 1, 0)) + 0.5 * v
        side = jnp.where(left_ok, pltpu.roll(blur_rows, 1, 1), 0.0) + jnp.where(
            right_ok, pltpu.roll(blur_rows, ncol - 1, 1), 0.0)
        blur_cols = 0.25 * side + 0.5 * blur_rows
        return 2.0 * blur_cols - v

    def coefficient(depth, fi, n, wavenumber):
        base = nfl
        im = (ORDER + 1) * POWERS
        coef_re = flts[base + n * POWERS + POWERS - 1] + 0.0 * wavenumber
        coef_im = flts[base + im + n * POWERS + POWERS - 1] + 0.0 * wavenumber
        for m in range(POWERS - 2, -1, -1):
            coef_re = coef_re * wavenumber + flts[base + n * POWERS + m]
            coef_im = coef_im * wavenumber + flts[base + im + n * POWERS + m]
        active = ints[1 + depth * nfl * (ORDER + 1) + fi * (ORDER + 1) + n].astype(jnp.float32)
        return coef_re * active, coef_im * active

    def extrapolate(depth, fi, wavenumber, valid, lo, hi, write):
        for n in range(ORDER + 1):
            slot = n % 3
            if n >= 1:
                cur, prev = (n - 1) % 3, (n - 2) % 3
                for p in range(4):
                    g = spread(tb[cur, p])
                    if n > 1:
                        g = 2.0 * g - tb[prev, p]
                    tb[slot, p] = jnp.where(valid, g, 0.0)
            coef_re, coef_im = coefficient(depth, fi, n, wavenumber)
            s_re = tb[slot, 0, lo:hi, :]
            s_im = tb[slot, 1, lo:hi, :]
            r_re = tb[slot, 2, lo:hi, :]
            r_im = tb[slot, 3, lo:hi, :]
            terms = (
                coef_re * s_re + coef_im * s_im,
                coef_re * s_im - coef_im * s_re,
                coef_re * r_re - coef_im * r_im,
                coef_re * r_im + coef_im * r_re,
            )
            write(n, terms)

    fields = (src_ref, rec_ref)
    for fi in range(nfl):
        for p in range(4):
            x, c = p // 2, p % 2
            tb[0, p] = jnp.where(valid0, joined(h_fa[x, c, fi], fields[x][c, fi], h_fb[x, c, fi]), 0.0)

        def write0(n, terms, fi=fi):
            for p in range(4):
                if n == 0:
                    s1[p // 2, p % 2, fi] = terms[p]
                else:
                    s1[p // 2, p % 2, fi] = s1[p // 2, p % 2, fi] + terms[p]

        extrapolate(0, fi, flts[fi] * slow0, valid0, 0, ext_rows, write0)
        for p in range(4):
            s1[p // 2, p % 2, fi] = jnp.where(valid1, s1[p // 2, p % 2, fi], 0.0)
        mid = slice(HALO, HALO + own)
        term = s1[0, 0, fi, mid, :] * s1[1, 0, fi, mid, :] + s1[0, 1, fi, mid, :] * s1[1, 1, fi, mid, :]
        term = jnp.where(live, term, 0.0)
        if fi == 0:
            img_out[0] = term
        else:
            img_out[0] = img_out[0] + term

    for fi in range(nfl):
        for p in range(4):
            tb[0, p] = s1[p // 2, p % 2, fi]
        acc = {}

        def write1(n, terms, acc=acc):
            for p in range(4):
                acc[p] = terms[p] if n == 0 else acc[p] + terms[p]

        extrapolate(1, fi, flts[fi] * slow1, valid1, HALO, HALO + own, write1)
        result = [jnp.where(live, acc[p], 0.0) for p in range(4)]
        rec_out[0, fi] = result[2]
        rec_out[1, fi] = result[3]
        term = result[0] * result[2] + result[1] * result[3]
        if fi == 0:
            img_out[1] = term
        else:
            img_out[1] = img_out[1] + term


def scatter_kernel(n_freq, img_ref, out_ref, got, send_sem, recv_sem):
    t = lax.axis_index("tile")
    f = lax.axis_index("freq")
    block = out_ref.shape[2]
    barrier = pltpu.get_barrier_semaphore()
    for q in range(n_freq):
        @pl.when(f != q)
        def _():
            pl.semaphore_signal(barrier, 1, device_id=(t, q), device_id_type=MESH)
    pl.semaphore_wait(barrier, n_freq - 1)

    def remote(q, slot_recv, device):
        return pltpu.make_async_remote_copy(
            src_ref=img_ref.at[:, :, pl.ds(q * block, block)], dst_ref=got.at[slot_recv],
            send_sem=send_sem.at[q], recv_sem=recv_sem.at[slot_recv],
            device_id=device, device_id_type=MESH,
        )

    for q in range(n_freq):
        @pl.when(f != q)
        def _():
            remote(q, f, (t, q)).start()

    for q in range(n_freq):
        @pl.when(f != q)
        def _():
            remote(q, q, (t, q)).wait_send()
            remote(q, q, (t, q)).wait_recv()

    total = None
    for q in range(n_freq):
        mine = img_ref[:, :, q * block:(q + 1) * block]
        part = jnp.where(f == q, mine, got[q])
        total = part if total is None else total + part
    out_ref[...] = total


def shards(n_tile, n_freq, source_field, receiver_field, slowness, frequency, order_table, filter_coeffs, aperture):
    tile_index = lax.axis_index("tile")
    nc, nfl, own, ncol = source_field.shape
    tile_width = aperture[tile_index]
    f_up = jnp.stack([
        lax.dynamic_slice_in_dim(source_field, tile_width - HALO, HALO, 2),
        lax.dynamic_slice_in_dim(receiver_field, tile_width - HALO, HALO, 2),
    ])
    f_lo = jnp.stack([source_field[:, :, :HALO], receiver_field[:, :, :HALO]])
    s_up = lax.dynamic_slice_in_dim(slowness[0], tile_width - HALO, HALO, 0)
    s_lo = slowness[0, :HALO]
    active = (
        jnp.arange(ORDER + 1, dtype=jnp.int32)[None, None, :] <= order_table[:, :, None]
    ).astype(jnp.int32)
    ints = jnp.concatenate([tile_width[None], active.reshape(-1)])
    flts = jnp.concatenate([frequency, filter_coeffs.reshape(-1)])
    block = slowness.shape[2]
    ext_rows = own + 2 * HALO
    elements = nc * nfl * 2 * ext_rows * ncol * NDEPTH
    rec_out, img = pl.pallas_call(
        functools.partial(migrate_kernel, n_tile, n_freq),
        out_shape=(
            jax.ShapeDtypeStruct((nc, nfl, own, ncol), jnp.float32),
            jax.ShapeDtypeStruct((NDEPTH, own, ncol), jnp.float32),
        ),
        in_specs=[pl.BlockSpec(memory_space=SMEM)] * 2 + [pl.BlockSpec(memory_space=VMEM)] * 7,
        out_specs=(pl.BlockSpec(memory_space=VMEM), pl.BlockSpec(memory_space=VMEM)),
        scratch_shapes=[
            pltpu.VMEM((n_freq, NDEPTH, own, block), jnp.float32),
            pltpu.VMEM((n_freq, HALO, block), jnp.float32),
            pltpu.VMEM((n_freq, HALO, block), jnp.float32),
            pltpu.VMEM((2, nc, nfl, HALO, ncol), jnp.float32),
            pltpu.VMEM((2, nc, nfl, HALO, ncol), jnp.float32),
            pltpu.VMEM((2, nc, nfl, ext_rows, ncol), jnp.float32),
            pltpu.VMEM((3, 4, ext_rows, ncol), jnp.float32),
            pltpu.SemaphoreType.DMA((3 * n_freq + 2,)),
            pltpu.SemaphoreType.DMA((3 * n_freq + 2,)),
        ],
        compiler_params=pltpu.CompilerParams(collective_id=0, has_side_effects=True),
        cost_estimate=pl.CostEstimate(flops=elements * 100, bytes_accessed=elements * 4, transcendentals=0),
    )(ints, flts, source_field, receiver_field, slowness, f_up, f_lo, s_up, s_lo)
    image_out = pl.pallas_call(
        functools.partial(scatter_kernel, n_freq),
        out_shape=jax.ShapeDtypeStruct((NDEPTH, own, block), jnp.float32),
        in_specs=[pl.BlockSpec(memory_space=VMEM)],
        out_specs=pl.BlockSpec(memory_space=VMEM),
        scratch_shapes=[
            pltpu.VMEM((n_freq, NDEPTH, own, block), jnp.float32),
            pltpu.SemaphoreType.DMA((n_freq,)),
            pltpu.SemaphoreType.DMA((n_freq,)),
        ],
        compiler_params=pltpu.CompilerParams(collective_id=1, has_side_effects=True),
    )(img)
    return (image_out, rec_out)


def solution(mesh):
    placed = (
        P(None, "freq", "tile", None),
        P(None, "freq", "tile", None),
        P(None, "tile", "freq"),
        P("freq"),
        P(None, "freq"),
        P(),
        P(),
    )
    return jax.shard_map(
        functools.partial(shards, mesh.shape["tile"], mesh.shape["freq"]),
        mesh=mesh,
        in_specs=placed,
        out_specs=(P(None, "tile", "freq"), P(None, "freq", "tile", None)),
        check_vma=False,
    )
```

```python
import functools

import jax
import jax.numpy as jnp
from jax import lax
from jax.experimental import pallas as pl
from jax.experimental.pallas import tpu as pltpu
from jax.sharding import PartitionSpec as P

ORDER = 4
NDEPTH = 2
POWERS = 3
HALO = 8
MESH = pl.DeviceIdType.MESH
VMEM = pltpu.MemorySpace.VMEM
SMEM = pltpu.MemorySpace.SMEM


def migrate_kernel(n_tile, n_freq, aperture, orders, frequency, coeffs, src_ref, rec_ref, slow_ref, f_up, s_up,
                   rec_out, img_out, g_slow, h_sa, h_sb, h_fa, h_fb, s1, tb, send_sem, recv_sem):
    t = lax.axis_index("tile")
    f = lax.axis_index("freq")
    nc, nfl, own, ncol = src_ref.shape
    ext_rows = HALO + own + HALO
    block = slow_ref.shape[2]
    ap = aperture[t]
    has_above = t > 0
    has_below = t < n_tile - 1
    f_lo = (src_ref.at[:, :, pl.ds(0, HALO), :], rec_ref.at[:, :, pl.ds(0, HALO), :])
    s_lo = slow_ref.at[0, pl.ds(0, HALO), :]

    g_slow[f] = slow_ref[...]

    @pl.when(t == 0)
    def _():
        h_fa[...] = jnp.zeros_like(h_fa)
        h_sa[...] = jnp.zeros_like(h_sa)

    @pl.when(t == n_tile - 1)
    def _():
        h_fb[...] = jnp.zeros_like(h_fb)
        h_sb[...] = jnp.zeros_like(h_sb)

    barrier = pltpu.get_barrier_semaphore()
    for q in range(n_freq):
        @pl.when(f != q)
        def _():
            pl.semaphore_signal(barrier, 1, device_id=(t, q), device_id_type=MESH)

        @pl.when(has_above)
        def _():
            pl.semaphore_signal(barrier, 1, device_id=(t - 1, q), device_id_type=MESH)

        @pl.when(has_below)
        def _():
            pl.semaphore_signal(barrier, 1, device_id=(t + 1, q), device_id_type=MESH)

    expected = (n_freq - 1) + n_freq * has_above.astype(jnp.int32) + n_freq * has_below.astype(jnp.int32)
    pl.semaphore_wait(barrier, expected)

    def remote(src, dst, slot_send, slot_recv, device):
        return pltpu.make_async_remote_copy(
            src_ref=src, dst_ref=dst, send_sem=send_sem.at[slot_send], recv_sem=recv_sem.at[slot_recv],
            device_id=device, device_id_type=MESH,
        )

    for q in range(n_freq):
        @pl.when(f != q)
        def _():
            remote(slow_ref, g_slow.at[f], q, f, (t, q)).start()

        @pl.when(has_below)
        def _():
            remote(s_up, h_sa.at[f], n_freq + q, n_freq + f, (t + 1, q)).start()

        @pl.when(has_above)
        def _():
            remote(s_lo, h_sb.at[f], 2 * n_freq + q, 2 * n_freq + f, (t - 1, q)).start()

    @pl.when(has_below)
    def _():
        remote(f_up, h_fa, 3 * n_freq, 3 * n_freq, (t + 1, f)).start()

    @pl.when(has_above)
    def _():
        for x in range(2):
            remote(f_lo[x], h_fb.at[x], 3 * n_freq + 1 + x, 3 * n_freq + 1 + x, (t - 1, f)).start()

    for q in range(n_freq):
        @pl.when(f != q)
        def _():
            remote(slow_ref, g_slow.at[q], q, q, (t, q)).wait_send()
            remote(slow_ref, g_slow.at[q], q, q, (t, q)).wait_recv()

        @pl.when(has_below)
        def _():
            remote(s_up, h_sa.at[q], n_freq + q, n_freq + q, (t + 1, q)).wait_send()
            remote(s_lo, h_sb.at[q], 2 * n_freq + q, 2 * n_freq + q, (t + 1, q)).wait_recv()

        @pl.when(has_above)
        def _():
            remote(s_lo, h_sb.at[q], 2 * n_freq + q, 2 * n_freq + q, (t - 1, q)).wait_send()
            remote(s_up, h_sa.at[q], n_freq + q, n_freq + q, (t - 1, q)).wait_recv()

    @pl.when(has_below)
    def _():
        remote(f_up, h_fa, 3 * n_freq, 3 * n_freq, (t + 1, f)).wait_send()
        for x in range(2):
            remote(f_lo[x], h_fb.at[x], 3 * n_freq + 1 + x, 3 * n_freq + 1 + x, (t + 1, f)).wait_recv()

    @pl.when(has_above)
    def _():
        for x in range(2):
            remote(f_lo[x], h_fb.at[x], 3 * n_freq + 1 + x, 3 * n_freq + 1 + x, (t - 1, f)).wait_send()
        remote(f_up, h_fa, 3 * n_freq, 3 * n_freq, (t - 1, f)).wait_recv()

    rows = lax.broadcasted_iota(jnp.int32, (ext_rows, ncol), 0)
    cols = lax.broadcasted_iota(jnp.int32, (ext_rows, ncol), 1)
    left_ok = jnp.abs(pltpu.roll(cols, 1, 1) - cols) == 1
    right_ok = jnp.abs(pltpu.roll(cols, ncol - 1, 1) - cols) == 1
    forward = pltpu.roll(rows, 1, 0) == (rows + ext_rows - 1) % ext_rows
    lower_start = HALO + ap
    top_part = rows < lower_start

    def in_band(lo, hi):
        return (rows >= lo) & (rows < hi)

    valid0 = (in_band(0, HALO) & has_above) | in_band(HALO, lower_start) | (
        in_band(lower_start, lower_start + HALO) & has_below)
    reach = HALO // 2
    valid1 = (in_band(HALO - reach, HALO) & has_above) | in_band(HALO, lower_start) | (
        in_band(lower_start, lower_start + reach) & has_below)
    live = lax.broadcasted_iota(jnp.int32, (own, ncol), 0) < ap
    zeros_tail = jnp.zeros((ext_rows - HALO, ncol), jnp.float32)

    def place_lower(lower8):
        padded = jnp.concatenate([lower8, zeros_tail], axis=0)
        ahead = pltpu.roll(padded, lower_start, 0)
        behind = pltpu.roll(padded, ext_rows - lower_start, 0)
        return jnp.where(forward, ahead, behind)

    def joined(upper8, own_rows, lower8):
        top = jnp.concatenate([upper8, own_rows, jnp.zeros((HALO, ncol), jnp.float32)], axis=0)
        return jnp.where(top_part, top, place_lower(lower8))

    def columns_of(pieces):
        return jnp.concatenate(pieces, axis=1)

    slow0 = joined(
        columns_of([h_sa[q] for q in range(n_freq)]),
        columns_of([g_slow[q, 0] for q in range(n_freq)]),
        columns_of([h_sb[q] for q in range(n_freq)]),
    )
    slow0 = jnp.where(valid0, slow0, 0.0)
    slow1 = columns_of([g_slow[q, 1] for q in range(n_freq)])

    def spread(v):
        blur_rows = 0.25 * (pltpu.roll(v, 1, 0) + pltpu.roll(v, ext_rows - 1, 0)) + 0.5 * v
        side = jnp.where(left_ok, pltpu.roll(blur_rows, 1, 1), 0.0) + jnp.where(
            right_ok, pltpu.roll(blur_rows, ncol - 1, 1), 0.0)
        blur_cols = 0.25 * side + 0.5 * blur_rows
        return 2.0 * blur_cols - v

    def coefficient(depth, fi, n, wavenumber):
        im = (ORDER + 1) * POWERS
        coef_re = coeffs[n * POWERS + POWERS - 1] + 0.0 * wavenumber
        coef_im = coeffs[im + n * POWERS + POWERS - 1] + 0.0 * wavenumber
        for m in range(POWERS - 2, -1, -1):
            coef_re = coef_re * wavenumber + coeffs[n * POWERS + m]
            coef_im = coef_im * wavenumber + coeffs[im + n * POWERS + m]
        active = (orders[depth * nfl + fi] >= n).astype(jnp.float32)
        return coef_re * active, coef_im * active

    def extrapolate(depth, fi, wavenumber, valid, lo, hi, write):
        for n in range(ORDER + 1):
            slot = n % 3
            if n >= 1:
                cur, prev = (n - 1) % 3, (n - 2) % 3
                for p in range(4):
                    g = spread(tb[cur, p])
                    if n > 1:
                        g = 2.0 * g - tb[prev, p]
                    tb[slot, p] = jnp.where(valid, g, 0.0)
            coef_re, coef_im = coefficient(depth, fi, n, wavenumber)
            s_re = tb[slot, 0, lo:hi, :]
            s_im = tb[slot, 1, lo:hi, :]
            r_re = tb[slot, 2, lo:hi, :]
            r_im = tb[slot, 3, lo:hi, :]
            terms = (
                coef_re * s_re + coef_im * s_im,
                coef_re * s_im - coef_im * s_re,
                coef_re * r_re - coef_im * r_im,
                coef_re * r_im + coef_im * r_re,
            )
            write(n, terms)

    fields = (src_ref, rec_ref)
    for fi in range(nfl):
        for p in range(4):
            x, c = p // 2, p % 2
            tb[0, p] = jnp.where(valid0, joined(h_fa[x, c, fi], fields[x][c, fi], h_fb[x, c, fi]), 0.0)

        def write0(n, terms, fi=fi):
            for p in range(4):
                if n == 0:
                    s1[p // 2, p % 2, fi] = terms[p]
                else:
                    s1[p // 2, p % 2, fi] = s1[p // 2, p % 2, fi] + terms[p]

        extrapolate(0, fi, frequency[fi] * slow0, valid0, 0, ext_rows, write0)
        for p in range(4):
            s1[p // 2, p % 2, fi] = jnp.where(valid1, s1[p // 2, p % 2, fi], 0.0)
        mid = slice(HALO, HALO + own)
        term = s1[0, 0, fi, mid, :] * s1[1, 0, fi, mid, :] + s1[0, 1, fi, mid, :] * s1[1, 1, fi, mid, :]
        term = jnp.where(live, term, 0.0)
        if fi == 0:
            img_out[0] = term
        else:
            img_out[0] = img_out[0] + term

    for fi in range(nfl):
        for p in range(4):
            tb[0, p] = s1[p // 2, p % 2, fi]
        acc = {}

        def write1(n, terms, acc=acc):
            for p in range(4):
                acc[p] = terms[p] if n == 0 else acc[p] + terms[p]

        extrapolate(1, fi, frequency[fi] * slow1, valid1, HALO, HALO + own, write1)
        result = [jnp.where(live, acc[p], 0.0) for p in range(4)]
        rec_out[0, fi] = result[2]
        rec_out[1, fi] = result[3]
        term = result[0] * result[2] + result[1] * result[3]
        if fi == 0:
            img_out[1] = term
        else:
            img_out[1] = img_out[1] + term


def scatter_kernel(n_freq, img_ref, out_ref, got, send_sem, recv_sem):
    t = lax.axis_index("tile")
    f = lax.axis_index("freq")
    block = out_ref.shape[2]
    barrier = pltpu.get_barrier_semaphore()
    for q in range(n_freq):
        @pl.when(f != q)
        def _():
            pl.semaphore_signal(barrier, 1, device_id=(t, q), device_id_type=MESH)
    pl.semaphore_wait(barrier, n_freq - 1)

    def remote(q, slot_recv, device):
        return pltpu.make_async_remote_copy(
            src_ref=img_ref.at[:, :, pl.ds(q * block, block)], dst_ref=got.at[slot_recv],
            send_sem=send_sem.at[q], recv_sem=recv_sem.at[slot_recv],
            device_id=device, device_id_type=MESH,
        )

    for q in range(n_freq):
        @pl.when(f != q)
        def _():
            remote(q, f, (t, q)).start()

    for q in range(n_freq):
        @pl.when(f != q)
        def _():
            remote(q, q, (t, q)).wait_send()
            remote(q, q, (t, q)).wait_recv()

    total = None
    for q in range(n_freq):
        mine = img_ref[:, :, q * block:(q + 1) * block]
        part = jnp.where(f == q, mine, got[q])
        total = part if total is None else total + part
    out_ref[...] = total


def shards(n_tile, n_freq, source_field, receiver_field, slowness, frequency, order_table, filter_coeffs, aperture):
    tile_index = lax.axis_index("tile")
    nc, nfl, own, ncol = source_field.shape
    tile_width = aperture[tile_index]
    f_up = jnp.stack([
        lax.dynamic_slice_in_dim(source_field, tile_width - HALO, HALO, 2),
        lax.dynamic_slice_in_dim(receiver_field, tile_width - HALO, HALO, 2),
    ])
    s_up = lax.dynamic_slice_in_dim(slowness[0], tile_width - HALO, HALO, 0)
    block = slowness.shape[2]
    ext_rows = own + 2 * HALO
    elements = nc * nfl * 2 * ext_rows * ncol * NDEPTH
    rec_out, img = pl.pallas_call(
        functools.partial(migrate_kernel, n_tile, n_freq),
        out_shape=(
            jax.ShapeDtypeStruct((nc, nfl, own, ncol), jnp.float32),
            jax.ShapeDtypeStruct((NDEPTH, own, ncol), jnp.float32),
        ),
        in_specs=[pl.BlockSpec(memory_space=SMEM)] * 4 + [pl.BlockSpec(memory_space=VMEM)] * 5,
        out_specs=(pl.BlockSpec(memory_space=VMEM), pl.BlockSpec(memory_space=VMEM)),
        scratch_shapes=[
            pltpu.VMEM((n_freq, NDEPTH, own, block), jnp.float32),
            pltpu.VMEM((n_freq, HALO, block), jnp.float32),
            pltpu.VMEM((n_freq, HALO, block), jnp.float32),
            pltpu.VMEM((2, nc, nfl, HALO, ncol), jnp.float32),
            pltpu.VMEM((2, nc, nfl, HALO, ncol), jnp.float32),
            pltpu.VMEM((2, nc, nfl, ext_rows, ncol), jnp.float32),
            pltpu.VMEM((3, 4, ext_rows, ncol), jnp.float32),
            pltpu.SemaphoreType.DMA((3 * n_freq + 3,)),
            pltpu.SemaphoreType.DMA((3 * n_freq + 3,)),
        ],
        compiler_params=pltpu.CompilerParams(collective_id=0, has_side_effects=True),
        cost_estimate=pl.CostEstimate(flops=elements * 100, bytes_accessed=elements * 4, transcendentals=0),
    )(aperture, order_table.reshape(-1), frequency, filter_coeffs.reshape(-1), source_field, receiver_field, slowness, f_up, s_up)
    image_out = pl.pallas_call(
        functools.partial(scatter_kernel, n_freq),
        out_shape=jax.ShapeDtypeStruct((NDEPTH, own, block), jnp.float32),
        in_specs=[pl.BlockSpec(memory_space=VMEM)],
        out_specs=pl.BlockSpec(memory_space=VMEM),
        scratch_shapes=[
            pltpu.VMEM((n_freq, NDEPTH, own, block), jnp.float32),
            pltpu.SemaphoreType.DMA((n_freq,)),
            pltpu.SemaphoreType.DMA((n_freq,)),
        ],
        compiler_params=pltpu.CompilerParams(collective_id=1, has_side_effects=True),
    )(img)
    return (image_out, rec_out)


def solution(mesh):
    placed = (
        P(None, "freq", "tile", None),
        P(None, "freq", "tile", None),
        P(None, "tile", "freq"),
        P("freq"),
        P(None, "freq"),
        P(),
        P(),
    )
    return jax.shard_map(
        functools.partial(shards, mesh.shape["tile"], mesh.shape["freq"]),
        mesh=mesh,
        in_specs=placed,
        out_specs=(P(None, "tile", "freq"), P(None, "freq", "tile", None)),
        check_vma=False,
    )
```

```python
import functools

import jax
import jax.numpy as jnp
from jax import lax
from jax.experimental import pallas as pl
from jax.experimental.pallas import tpu as pltpu
from jax.sharding import PartitionSpec as P

ORDER = 4
NDEPTH = 2
POWERS = 3
HALO = 8
MESH = pl.DeviceIdType.MESH
VMEM = pltpu.MemorySpace.VMEM
SMEM = pltpu.MemorySpace.SMEM


def migrate_kernel(n_tile, n_freq, aperture, orders, frequency, coeffs, src_ref, rec_ref, slow_ref, f_up, s_up,
                   rec_out, image_out, g_slow, h_sa, h_sb, h_fa, h_fb, s1, tb, img_out, got, send_sem, recv_sem):
    t = lax.axis_index("tile")
    f = lax.axis_index("freq")
    nc, nfl, own, ncol = src_ref.shape
    ext_rows = HALO + own + HALO
    block = slow_ref.shape[2]
    ap = aperture[t]
    has_above = t > 0
    has_below = t < n_tile - 1
    f_lo = (src_ref.at[:, :, pl.ds(0, HALO), :], rec_ref.at[:, :, pl.ds(0, HALO), :])
    s_lo = slow_ref.at[0, pl.ds(0, HALO), :]

    g_slow[f] = slow_ref[...]

    @pl.when(t == 0)
    def _():
        h_fa[...] = jnp.zeros_like(h_fa)
        h_sa[...] = jnp.zeros_like(h_sa)

    @pl.when(t == n_tile - 1)
    def _():
        h_fb[...] = jnp.zeros_like(h_fb)
        h_sb[...] = jnp.zeros_like(h_sb)

    barrier = pltpu.get_barrier_semaphore()
    for q in range(n_freq):
        @pl.when(f != q)
        def _():
            pl.semaphore_signal(barrier, 1, device_id=(t, q), device_id_type=MESH)

        @pl.when(has_above)
        def _():
            pl.semaphore_signal(barrier, 1, device_id=(t - 1, q), device_id_type=MESH)

        @pl.when(has_below)
        def _():
            pl.semaphore_signal(barrier, 1, device_id=(t + 1, q), device_id_type=MESH)

    expected = (n_freq - 1) + n_freq * has_above.astype(jnp.int32) + n_freq * has_below.astype(jnp.int32)
    pl.semaphore_wait(barrier, expected)

    def remote(src, dst, slot_send, slot_recv, device):
        return pltpu.make_async_remote_copy(
            src_ref=src, dst_ref=dst, send_sem=send_sem.at[slot_send], recv_sem=recv_sem.at[slot_recv],
            device_id=device, device_id_type=MESH,
        )

    for q in range(n_freq):
        @pl.when(f != q)
        def _():
            remote(slow_ref, g_slow.at[f], q, f, (t, q)).start()

        @pl.when(has_below)
        def _():
            remote(s_up, h_sa.at[f], n_freq + q, n_freq + f, (t + 1, q)).start()

        @pl.when(has_above)
        def _():
            remote(s_lo, h_sb.at[f], 2 * n_freq + q, 2 * n_freq + f, (t - 1, q)).start()

    @pl.when(has_below)
    def _():
        remote(f_up, h_fa, 3 * n_freq, 3 * n_freq, (t + 1, f)).start()

    @pl.when(has_above)
    def _():
        for x in range(2):
            remote(f_lo[x], h_fb.at[x], 3 * n_freq + 1 + x, 3 * n_freq + 1 + x, (t - 1, f)).start()

    for q in range(n_freq):
        @pl.when(f != q)
        def _():
            remote(slow_ref, g_slow.at[q], q, q, (t, q)).wait_send()
            remote(slow_ref, g_slow.at[q], q, q, (t, q)).wait_recv()

        @pl.when(has_below)
        def _():
            remote(s_up, h_sa.at[q], n_freq + q, n_freq + q, (t + 1, q)).wait_send()
            remote(s_lo, h_sb.at[q], 2 * n_freq + q, 2 * n_freq + q, (t + 1, q)).wait_recv()

        @pl.when(has_above)
        def _():
            remote(s_lo, h_sb.at[q], 2 * n_freq + q, 2 * n_freq + q, (t - 1, q)).wait_send()
            remote(s_up, h_sa.at[q], n_freq + q, n_freq + q, (t - 1, q)).wait_recv()

    @pl.when(has_below)
    def _():
        remote(f_up, h_fa, 3 * n_freq, 3 * n_freq, (t + 1, f)).wait_send()
        for x in range(2):
            remote(f_lo[x], h_fb.at[x], 3 * n_freq + 1 + x, 3 * n_freq + 1 + x, (t + 1, f)).wait_recv()

    @pl.when(has_above)
    def _():
        for x in range(2):
            remote(f_lo[x], h_fb.at[x], 3 * n_freq + 1 + x, 3 * n_freq + 1 + x, (t - 1, f)).wait_send()
        remote(f_up, h_fa, 3 * n_freq, 3 * n_freq, (t - 1, f)).wait_recv()

    rows = lax.broadcasted_iota(jnp.int32, (ext_rows, ncol), 0)
    cols = lax.broadcasted_iota(jnp.int32, (ext_rows, ncol), 1)
    left_ok = jnp.abs(pltpu.roll(cols, 1, 1) - cols) == 1
    right_ok = jnp.abs(pltpu.roll(cols, ncol - 1, 1) - cols) == 1
    forward = pltpu.roll(rows, 1, 0) == (rows + ext_rows - 1) % ext_rows
    lower_start = HALO + ap
    top_part = rows < lower_start

    def in_band(lo, hi):
        return (rows >= lo) & (rows < hi)

    valid0 = (in_band(0, HALO) & has_above) | in_band(HALO, lower_start) | (
        in_band(lower_start, lower_start + HALO) & has_below)
    reach = HALO // 2
    valid1 = (in_band(HALO - reach, HALO) & has_above) | in_band(HALO, lower_start) | (
        in_band(lower_start, lower_start + reach) & has_below)
    live = lax.broadcasted_iota(jnp.int32, (own, ncol), 0) < ap
    zeros_tail = jnp.zeros((ext_rows - HALO, ncol), jnp.float32)

    def place_lower(lower8):
        padded = jnp.concatenate([lower8, zeros_tail], axis=0)
        ahead = pltpu.roll(padded, lower_start, 0)
        behind = pltpu.roll(padded, ext_rows - lower_start, 0)
        return jnp.where(forward, ahead, behind)

    def joined(upper8, own_rows, lower8):
        top = jnp.concatenate([upper8, own_rows, jnp.zeros((HALO, ncol), jnp.float32)], axis=0)
        return jnp.where(top_part, top, place_lower(lower8))

    def columns_of(pieces):
        return jnp.concatenate(pieces, axis=1)

    slow0 = joined(
        columns_of([h_sa[q] for q in range(n_freq)]),
        columns_of([g_slow[q, 0] for q in range(n_freq)]),
        columns_of([h_sb[q] for q in range(n_freq)]),
    )
    slow0 = jnp.where(valid0, slow0, 0.0)
    slow1 = columns_of([g_slow[q, 1] for q in range(n_freq)])

    def spread(v):
        blur_rows = 0.25 * (pltpu.roll(v, 1, 0) + pltpu.roll(v, ext_rows - 1, 0)) + 0.5 * v
        side = jnp.where(left_ok, pltpu.roll(blur_rows, 1, 1), 0.0) + jnp.where(
            right_ok, pltpu.roll(blur_rows, ncol - 1, 1), 0.0)
        blur_cols = 0.25 * side + 0.5 * blur_rows
        return 2.0 * blur_cols - v

    def coefficient(depth, fi, n, wavenumber):
        coef_re = coeffs[0, n, POWERS - 1] + 0.0 * wavenumber
        coef_im = coeffs[1, n, POWERS - 1] + 0.0 * wavenumber
        for m in range(POWERS - 2, -1, -1):
            coef_re = coef_re * wavenumber + coeffs[0, n, m]
            coef_im = coef_im * wavenumber + coeffs[1, n, m]
        active = (orders[depth, fi] >= n).astype(jnp.float32)
        return coef_re * active, coef_im * active

    def extrapolate(depth, fi, wavenumber, valid, lo, hi, write):
        for n in range(ORDER + 1):
            slot = n % 3
            if n >= 1:
                cur, prev = (n - 1) % 3, (n - 2) % 3
                for p in range(4):
                    g = spread(tb[cur, p])
                    if n > 1:
                        g = 2.0 * g - tb[prev, p]
                    tb[slot, p] = jnp.where(valid, g, 0.0)
            coef_re, coef_im = coefficient(depth, fi, n, wavenumber)
            s_re = tb[slot, 0, lo:hi, :]
            s_im = tb[slot, 1, lo:hi, :]
            r_re = tb[slot, 2, lo:hi, :]
            r_im = tb[slot, 3, lo:hi, :]
            terms = (
                coef_re * s_re + coef_im * s_im,
                coef_re * s_im - coef_im * s_re,
                coef_re * r_re - coef_im * r_im,
                coef_re * r_im + coef_im * r_re,
            )
            write(n, terms)

    fields = (src_ref, rec_ref)
    for fi in range(nfl):
        for p in range(4):
            x, c = p // 2, p % 2
            tb[0, p] = jnp.where(valid0, joined(h_fa[x, c, fi], fields[x][c, fi], h_fb[x, c, fi]), 0.0)

        def write0(n, terms, fi=fi):
            for p in range(4):
                if n == 0:
                    s1[p // 2, p % 2, fi] = terms[p]
                else:
                    s1[p // 2, p % 2, fi] = s1[p // 2, p % 2, fi] + terms[p]

        extrapolate(0, fi, frequency[fi] * slow0, valid0, 0, ext_rows, write0)
        for p in range(4):
            s1[p // 2, p % 2, fi] = jnp.where(valid1, s1[p // 2, p % 2, fi], 0.0)
        mid = slice(HALO, HALO + own)
        term = s1[0, 0, fi, mid, :] * s1[1, 0, fi, mid, :] + s1[0, 1, fi, mid, :] * s1[1, 1, fi, mid, :]
        term = jnp.where(live, term, 0.0)
        if fi == 0:
            img_out[0] = term
        else:
            img_out[0] = img_out[0] + term

    image_base = 3 * n_freq + 3

    def image_copy(depth, q, slot_recv, device):
        return pltpu.make_async_remote_copy(
            src_ref=img_out.at[depth, :, pl.ds(q * block, block)], dst_ref=got.at[slot_recv, depth],
            send_sem=send_sem.at[image_base + depth * n_freq + q],
            recv_sem=recv_sem.at[image_base + depth * n_freq + slot_recv],
            device_id=device, device_id_type=MESH,
        )

    def send_image(depth):
        for q in range(n_freq):
            @pl.when(f != q)
            def _():
                image_copy(depth, q, f, (t, q)).start()

    send_image(0)

    for fi in range(nfl):
        for p in range(4):
            tb[0, p] = s1[p // 2, p % 2, fi]
        acc = {}

        def write1(n, terms, acc=acc):
            for p in range(4):
                acc[p] = terms[p] if n == 0 else acc[p] + terms[p]

        extrapolate(1, fi, frequency[fi] * slow1, valid1, HALO, HALO + own, write1)
        result = [jnp.where(live, acc[p], 0.0) for p in range(4)]
        rec_out[0, fi] = result[2]
        rec_out[1, fi] = result[3]
        term = result[0] * result[2] + result[1] * result[3]
        if fi == 0:
            img_out[1] = term
        else:
            img_out[1] = img_out[1] + term

    send_image(1)
    for depth in range(NDEPTH):
        for q in range(n_freq):
            @pl.when(f != q)
            def _():
                image_copy(depth, q, q, (t, q)).wait_send()
                image_copy(depth, q, q, (t, q)).wait_recv()

    total = None
    for q in range(n_freq):
        mine = img_out[:, :, q * block:(q + 1) * block]
        part = jnp.where(f == q, mine, got[q])
        total = part if total is None else total + part
    image_out[...] = total


def shards(n_tile, n_freq, source_field, receiver_field, slowness, frequency, order_table, filter_coeffs, aperture):
    tile_index = lax.axis_index("tile")
    nc, nfl, own, ncol = source_field.shape
    tile_width = aperture[tile_index]
    f_up = jnp.stack([
        lax.dynamic_slice_in_dim(source_field, tile_width - HALO, HALO, 2),
        lax.dynamic_slice_in_dim(receiver_field, tile_width - HALO, HALO, 2),
    ])
    s_up = lax.dynamic_slice_in_dim(slowness[0], tile_width - HALO, HALO, 0)
    block = slowness.shape[2]
    ext_rows = own + 2 * HALO
    elements = nc * nfl * 2 * ext_rows * ncol * NDEPTH
    rec_out, image_out = pl.pallas_call(
        functools.partial(migrate_kernel, n_tile, n_freq),
        out_shape=(
            jax.ShapeDtypeStruct((nc, nfl, own, ncol), jnp.float32),
            jax.ShapeDtypeStruct((NDEPTH, own, block), jnp.float32),
        ),
        in_specs=[pl.BlockSpec(memory_space=SMEM)] * 4 + [pl.BlockSpec(memory_space=VMEM)] * 5,
        out_specs=(pl.BlockSpec(memory_space=VMEM), pl.BlockSpec(memory_space=VMEM)),
        scratch_shapes=[
            pltpu.VMEM((n_freq, NDEPTH, own, block), jnp.float32),
            pltpu.VMEM((n_freq, HALO, block), jnp.float32),
            pltpu.VMEM((n_freq, HALO, block), jnp.float32),
            pltpu.VMEM((2, nc, nfl, HALO, ncol), jnp.float32),
            pltpu.VMEM((2, nc, nfl, HALO, ncol), jnp.float32),
            pltpu.VMEM((2, nc, nfl, ext_rows, ncol), jnp.float32),
            pltpu.VMEM((3, 4, ext_rows, ncol), jnp.float32),
            pltpu.VMEM((NDEPTH, own, ncol), jnp.float32),
            pltpu.VMEM((n_freq, NDEPTH, own, block), jnp.float32),
            pltpu.SemaphoreType.DMA((3 * n_freq + 3 + NDEPTH * n_freq,)),
            pltpu.SemaphoreType.DMA((3 * n_freq + 3 + NDEPTH * n_freq,)),
        ],
        compiler_params=pltpu.CompilerParams(collective_id=0, has_side_effects=True),
        cost_estimate=pl.CostEstimate(flops=elements * 100, bytes_accessed=elements * 4, transcendentals=0),
    )(aperture, order_table, frequency, filter_coeffs, source_field, receiver_field, slowness, f_up, s_up)
    return (image_out, rec_out)


def solution(mesh):
    placed = (
        P(None, "freq", "tile", None),
        P(None, "freq", "tile", None),
        P(None, "tile", "freq"),
        P("freq"),
        P(None, "freq"),
        P(),
        P(),
    )
    return jax.shard_map(
        functools.partial(shards, mesh.shape["tile"], mesh.shape["freq"]),
        mesh=mesh,
        in_specs=placed,
        out_specs=(P(None, "tile", "freq"), P(None, "freq", "tile", None)),
        check_vma=False,
    )
```

```python
import functools

import jax
import jax.numpy as jnp
from jax import lax
from jax.experimental import pallas as pl
from jax.experimental.pallas import tpu as pltpu
from jax.sharding import PartitionSpec as P

ORDER = 4
NDEPTH = 2
POWERS = 3
HALO = 8
MESH = pl.DeviceIdType.MESH
VMEM = pltpu.MemorySpace.VMEM
SMEM = pltpu.MemorySpace.SMEM


def migrate_kernel(n_tile, n_freq, aperture, orders, frequency, coeffs, src_hbm, rec_hbm, slow_hbm,
                   rec_out, image_out, src_v, rec_v, g_slow, h_sa, h_sb, h_fa, h_fb, up_buf, s_up, s1, tb, img_out,
                   got, local_sem, send_sem, recv_sem):
    t = lax.axis_index("tile")
    f = lax.axis_index("freq")
    nc, nfl, own, ncol = src_v.shape
    ext_rows = HALO + own + HALO
    block = slow_hbm.shape[2]
    ap = aperture[t]
    has_above = t > 0
    has_below = t < n_tile - 1

    loads = (
        pltpu.make_async_copy(src_hbm, src_v, local_sem.at[0]),
        pltpu.make_async_copy(rec_hbm, rec_v, local_sem.at[1]),
        pltpu.make_async_copy(slow_hbm, g_slow.at[f], local_sem.at[2]),
    )
    for copy in loads:
        copy.start()

    @pl.when(t == 0)
    def _():
        h_fa[...] = jnp.zeros_like(h_fa)
        h_sa[...] = jnp.zeros_like(h_sa)

    @pl.when(t == n_tile - 1)
    def _():
        h_fb[...] = jnp.zeros_like(h_fb)
        h_sb[...] = jnp.zeros_like(h_sb)

    barrier = pltpu.get_barrier_semaphore()
    for q in range(n_freq):
        @pl.when(f != q)
        def _():
            pl.semaphore_signal(barrier, 1, device_id=(t, q), device_id_type=MESH)

        @pl.when(has_above)
        def _():
            pl.semaphore_signal(barrier, 1, device_id=(t - 1, q), device_id_type=MESH)

        @pl.when(has_below)
        def _():
            pl.semaphore_signal(barrier, 1, device_id=(t + 1, q), device_id_type=MESH)

    expected = (n_freq - 1) + n_freq * has_above.astype(jnp.int32) + n_freq * has_below.astype(jnp.int32)
    pl.semaphore_wait(barrier, expected)

    def remote(src, dst, slot_send, slot_recv, device):
        return pltpu.make_async_remote_copy(
            src_ref=src, dst_ref=dst, send_sem=send_sem.at[slot_send], recv_sem=recv_sem.at[slot_recv],
            device_id=device, device_id_type=MESH,
        )

    f_lo = (src_hbm.at[:, :, pl.ds(0, HALO), :], rec_hbm.at[:, :, pl.ds(0, HALO), :])
    s_lo = slow_hbm.at[0, pl.ds(0, HALO), :]
    for q in range(n_freq):
        @pl.when(f != q)
        def _():
            remote(slow_hbm, g_slow.at[f], q, f, (t, q)).start()

        @pl.when(has_above)
        def _():
            remote(s_lo, h_sb.at[f], 2 * n_freq + q, 2 * n_freq + f, (t - 1, q)).start()

    @pl.when(has_above)
    def _():
        for x in range(2):
            remote(f_lo[x], h_fb.at[x], 3 * n_freq + 1 + x, 3 * n_freq + 1 + x, (t - 1, f)).start()

    for copy in loads:
        copy.wait()

    own_rows = lax.broadcasted_iota(jnp.int32, (own, ncol), 0)
    own_forward = pltpu.roll(own_rows, 1, 0) == (own_rows + own - 1) % own
    lift = (own + HALO - ap) % own
    drop = ap - HALO

    def last_rows(x, forward):
        return jnp.where(forward, pltpu.roll(x, lift, 0), pltpu.roll(x, drop, 0))[:HALO]

    fields_v = (src_v, rec_v)
    for x in range(2):
        for c in range(nc):
            for fi in range(nfl):
                up_buf[x, c, fi] = last_rows(fields_v[x][c, fi], own_forward)
    s_up[...] = last_rows(g_slow[f, 0], own_forward[:, :block])

    for q in range(n_freq):
        @pl.when(has_below)
        def _():
            remote(s_up, h_sa.at[f], n_freq + q, n_freq + f, (t + 1, q)).start()

    @pl.when(has_below)
    def _():
        remote(up_buf, h_fa, 3 * n_freq, 3 * n_freq, (t + 1, f)).start()

    for q in range(n_freq):
        @pl.when(f != q)
        def _():
            remote(slow_hbm, g_slow.at[q], q, q, (t, q)).wait_send()
            remote(slow_hbm, g_slow.at[q], q, q, (t, q)).wait_recv()

        @pl.when(has_below)
        def _():
            remote(s_up, h_sa.at[q], n_freq + q, n_freq + q, (t + 1, q)).wait_send()
            remote(s_lo, h_sb.at[q], 2 * n_freq + q, 2 * n_freq + q, (t + 1, q)).wait_recv()

        @pl.when(has_above)
        def _():
            remote(s_lo, h_sb.at[q], 2 * n_freq + q, 2 * n_freq + q, (t - 1, q)).wait_send()
            remote(s_up, h_sa.at[q], n_freq + q, n_freq + q, (t - 1, q)).wait_recv()

    @pl.when(has_below)
    def _():
        remote(up_buf, h_fa, 3 * n_freq, 3 * n_freq, (t + 1, f)).wait_send()
        for x in range(2):
            remote(f_lo[x], h_fb.at[x], 3 * n_freq + 1 + x, 3 * n_freq + 1 + x, (t + 1, f)).wait_recv()

    @pl.when(has_above)
    def _():
        for x in range(2):
            remote(f_lo[x], h_fb.at[x], 3 * n_freq + 1 + x, 3 * n_freq + 1 + x, (t - 1, f)).wait_send()
        remote(up_buf, h_fa, 3 * n_freq, 3 * n_freq, (t - 1, f)).wait_recv()

    rows = lax.broadcasted_iota(jnp.int32, (ext_rows, ncol), 0)
    cols = lax.broadcasted_iota(jnp.int32, (ext_rows, ncol), 1)
    left_ok = jnp.abs(pltpu.roll(cols, 1, 1) - cols) == 1
    right_ok = jnp.abs(pltpu.roll(cols, ncol - 1, 1) - cols) == 1
    forward = pltpu.roll(rows, 1, 0) == (rows + ext_rows - 1) % ext_rows
    lower_start = HALO + ap
    top_part = rows < lower_start

    def in_band(lo, hi):
        return (rows >= lo) & (rows < hi)

    valid0 = (in_band(0, HALO) & has_above) | in_band(HALO, lower_start) | (
        in_band(lower_start, lower_start + HALO) & has_below)
    reach = HALO // 2
    valid1 = (in_band(HALO - reach, HALO) & has_above) | in_band(HALO, lower_start) | (
        in_band(lower_start, lower_start + reach) & has_below)
    live = lax.broadcasted_iota(jnp.int32, (own, ncol), 0) < ap
    zeros_tail = jnp.zeros((ext_rows - HALO, ncol), jnp.float32)

    def place_lower(lower8):
        padded = jnp.concatenate([lower8, zeros_tail], axis=0)
        ahead = pltpu.roll(padded, lower_start, 0)
        behind = pltpu.roll(padded, ext_rows - lower_start, 0)
        return jnp.where(forward, ahead, behind)

    def joined(upper8, own_rows, lower8):
        top = jnp.concatenate([upper8, own_rows, jnp.zeros((HALO, ncol), jnp.float32)], axis=0)
        return jnp.where(top_part, top, place_lower(lower8))

    def columns_of(pieces):
        return jnp.concatenate(pieces, axis=1)

    slow0 = joined(
        columns_of([h_sa[q] for q in range(n_freq)]),
        columns_of([g_slow[q, 0] for q in range(n_freq)]),
        columns_of([h_sb[q] for q in range(n_freq)]),
    )
    slow0 = jnp.where(valid0, slow0, 0.0)
    slow1 = columns_of([g_slow[q, 1] for q in range(n_freq)])

    def spread(v):
        blur_rows = 0.25 * (pltpu.roll(v, 1, 0) + pltpu.roll(v, ext_rows - 1, 0)) + 0.5 * v
        side = jnp.where(left_ok, pltpu.roll(blur_rows, 1, 1), 0.0) + jnp.where(
            right_ok, pltpu.roll(blur_rows, ncol - 1, 1), 0.0)
        blur_cols = 0.25 * side + 0.5 * blur_rows
        return 2.0 * blur_cols - v

    def coefficient(depth, fi, n, wavenumber):
        coef_re = coeffs[0, n, POWERS - 1] + 0.0 * wavenumber
        coef_im = coeffs[1, n, POWERS - 1] + 0.0 * wavenumber
        for m in range(POWERS - 2, -1, -1):
            coef_re = coef_re * wavenumber + coeffs[0, n, m]
            coef_im = coef_im * wavenumber + coeffs[1, n, m]
        active = (orders[depth, fi] >= n).astype(jnp.float32)
        return coef_re * active, coef_im * active

    def extrapolate(depth, fi, wavenumber, valid, lo, hi, write):
        for n in range(ORDER + 1):
            slot = n % 3
            if n >= 1:
                cur, prev = (n - 1) % 3, (n - 2) % 3
                for p in range(4):
                    g = spread(tb[cur, p])
                    if n > 1:
                        g = 2.0 * g - tb[prev, p]
                    tb[slot, p] = jnp.where(valid, g, 0.0)
            coef_re, coef_im = coefficient(depth, fi, n, wavenumber)
            s_re = tb[slot, 0, lo:hi, :]
            s_im = tb[slot, 1, lo:hi, :]
            r_re = tb[slot, 2, lo:hi, :]
            r_im = tb[slot, 3, lo:hi, :]
            terms = (
                coef_re * s_re + coef_im * s_im,
                coef_re * s_im - coef_im * s_re,
                coef_re * r_re - coef_im * r_im,
                coef_re * r_im + coef_im * r_re,
            )
            write(n, terms)

    fields = (src_v, rec_v)
    for fi in range(nfl):
        for p in range(4):
            x, c = p // 2, p % 2
            tb[0, p] = jnp.where(valid0, joined(h_fa[x, c, fi], fields[x][c, fi], h_fb[x, c, fi]), 0.0)

        def write0(n, terms, fi=fi):
            for p in range(4):
                if n == 0:
                    s1[p // 2, p % 2, fi] = terms[p]
                else:
                    s1[p // 2, p % 2, fi] = s1[p // 2, p % 2, fi] + terms[p]

        extrapolate(0, fi, frequency[fi] * slow0, valid0, 0, ext_rows, write0)
        for p in range(4):
            s1[p // 2, p % 2, fi] = jnp.where(valid1, s1[p // 2, p % 2, fi], 0.0)
        mid = slice(HALO, HALO + own)
        term = s1[0, 0, fi, mid, :] * s1[1, 0, fi, mid, :] + s1[0, 1, fi, mid, :] * s1[1, 1, fi, mid, :]
        term = jnp.where(live, term, 0.0)
        if fi == 0:
            img_out[0] = term
        else:
            img_out[0] = img_out[0] + term

    image_base = 3 * n_freq + 3

    def image_copy(depth, q, slot_recv, device):
        return pltpu.make_async_remote_copy(
            src_ref=img_out.at[depth, :, pl.ds(q * block, block)], dst_ref=got.at[slot_recv, depth],
            send_sem=send_sem.at[image_base + depth * n_freq + q],
            recv_sem=recv_sem.at[image_base + depth * n_freq + slot_recv],
            device_id=device, device_id_type=MESH,
        )

    def send_image(depth):
        for q in range(n_freq):
            @pl.when(f != q)
            def _():
                image_copy(depth, q, f, (t, q)).start()

    send_image(0)

    for fi in range(nfl):
        for p in range(4):
            tb[0, p] = s1[p // 2, p % 2, fi]
        acc = {}

        def write1(n, terms, acc=acc):
            for p in range(4):
                acc[p] = terms[p] if n == 0 else acc[p] + terms[p]

        extrapolate(1, fi, frequency[fi] * slow1, valid1, HALO, HALO + own, write1)
        result = [jnp.where(live, acc[p], 0.0) for p in range(4)]
        rec_out[0, fi] = result[2]
        rec_out[1, fi] = result[3]
        term = result[0] * result[2] + result[1] * result[3]
        if fi == 0:
            img_out[1] = term
        else:
            img_out[1] = img_out[1] + term

    send_image(1)
    for depth in range(NDEPTH):
        for q in range(n_freq):
            @pl.when(f != q)
            def _():
                image_copy(depth, q, q, (t, q)).wait_send()
                image_copy(depth, q, q, (t, q)).wait_recv()

    total = None
    for q in range(n_freq):
        mine = img_out[:, :, q * block:(q + 1) * block]
        part = jnp.where(f == q, mine, got[q])
        total = part if total is None else total + part
    image_out[...] = total


def shards(n_tile, n_freq, source_field, receiver_field, slowness, frequency, order_table, filter_coeffs, aperture):
    nc, nfl, own, ncol = source_field.shape
    block = slowness.shape[2]
    ext_rows = own + 2 * HALO
    elements = nc * nfl * 2 * ext_rows * ncol * NDEPTH
    rec_out, image_out = pl.pallas_call(
        functools.partial(migrate_kernel, n_tile, n_freq),
        out_shape=(
            jax.ShapeDtypeStruct((nc, nfl, own, ncol), jnp.float32),
            jax.ShapeDtypeStruct((NDEPTH, own, block), jnp.float32),
        ),
        in_specs=[pl.BlockSpec(memory_space=SMEM)] * 4 + [pl.BlockSpec(memory_space=pl.ANY)] * 3,
        out_specs=(pl.BlockSpec(memory_space=VMEM), pl.BlockSpec(memory_space=VMEM)),
        scratch_shapes=[
            pltpu.VMEM((nc, nfl, own, ncol), jnp.float32),
            pltpu.VMEM((nc, nfl, own, ncol), jnp.float32),
            pltpu.VMEM((n_freq, NDEPTH, own, block), jnp.float32),
            pltpu.VMEM((n_freq, HALO, block), jnp.float32),
            pltpu.VMEM((n_freq, HALO, block), jnp.float32),
            pltpu.VMEM((2, nc, nfl, HALO, ncol), jnp.float32),
            pltpu.VMEM((2, nc, nfl, HALO, ncol), jnp.float32),
            pltpu.VMEM((2, nc, nfl, HALO, ncol), jnp.float32),
            pltpu.VMEM((HALO, block), jnp.float32),
            pltpu.VMEM((2, nc, nfl, ext_rows, ncol), jnp.float32),
            pltpu.VMEM((3, 4, ext_rows, ncol), jnp.float32),
            pltpu.VMEM((NDEPTH, own, ncol), jnp.float32),
            pltpu.VMEM((n_freq, NDEPTH, own, block), jnp.float32),
            pltpu.SemaphoreType.DMA((3,)),
            pltpu.SemaphoreType.DMA((3 * n_freq + 3 + NDEPTH * n_freq,)),
            pltpu.SemaphoreType.DMA((3 * n_freq + 3 + NDEPTH * n_freq,)),
        ],
        compiler_params=pltpu.CompilerParams(collective_id=0, has_side_effects=True),
        cost_estimate=pl.CostEstimate(flops=elements * 100, bytes_accessed=elements * 4, transcendentals=0),
    )(aperture, order_table, frequency, filter_coeffs, source_field, receiver_field, slowness)
    return (image_out, rec_out)


def solution(mesh):
    placed = (
        P(None, "freq", "tile", None),
        P(None, "freq", "tile", None),
        P(None, "tile", "freq"),
        P("freq"),
        P(None, "freq"),
        P(),
        P(),
    )
    return jax.shard_map(
        functools.partial(shards, mesh.shape["tile"], mesh.shape["freq"]),
        mesh=mesh,
        in_specs=placed,
        out_specs=(P(None, "tile", "freq"), P(None, "freq", "tile", None)),
        check_vma=False,
    )
```

```python
import functools

import jax
import jax.numpy as jnp
from jax import lax
from jax.experimental import pallas as pl
from jax.experimental.pallas import tpu as pltpu
from jax.sharding import PartitionSpec as P

ORDER = 4
NDEPTH = 2
POWERS = 3
HALO = 8
MESH = pl.DeviceIdType.MESH
VMEM = pltpu.MemorySpace.VMEM
SMEM = pltpu.MemorySpace.SMEM


def migrate_kernel(n_tile, n_freq, aperture, orders, frequency, coeffs, src_hbm, rec_hbm, slow_hbm,
                   rec_out, image_out, src_v, rec_v, g_slow, h_sa, h_sb, h_fa, h_fb, up_buf, s_up, s1, tb, img_out,
                   got, local_sem, send_sem, recv_sem):
    t = lax.axis_index("tile")
    f = lax.axis_index("freq")
    nc, nfl, own, ncol = src_v.shape
    ext_rows = HALO + own + HALO
    block = slow_hbm.shape[2]
    ap = aperture[t]
    has_above = t > 0
    has_below = t < n_tile - 1

    loads = (
        pltpu.make_async_copy(src_hbm, src_v, local_sem.at[0]),
        pltpu.make_async_copy(rec_hbm, rec_v, local_sem.at[1]),
        pltpu.make_async_copy(slow_hbm, g_slow.at[f], local_sem.at[2]),
    )
    for copy in loads:
        copy.start()

    @pl.when(t == 0)
    def _():
        h_fa[...] = jnp.zeros_like(h_fa)
        h_sa[...] = jnp.zeros_like(h_sa)

    @pl.when(t == n_tile - 1)
    def _():
        h_fb[...] = jnp.zeros_like(h_fb)
        h_sb[...] = jnp.zeros_like(h_sb)

    barrier = pltpu.get_barrier_semaphore()
    for q in range(n_freq):
        @pl.when(f != q)
        def _():
            pl.semaphore_signal(barrier, 1, device_id=(t, q), device_id_type=MESH)

        @pl.when(has_above)
        def _():
            pl.semaphore_signal(barrier, 1, device_id=(t - 1, q), device_id_type=MESH)

        @pl.when(has_below)
        def _():
            pl.semaphore_signal(barrier, 1, device_id=(t + 1, q), device_id_type=MESH)

    expected = (n_freq - 1) + n_freq * has_above.astype(jnp.int32) + n_freq * has_below.astype(jnp.int32)
    pl.semaphore_wait(barrier, expected)

    def remote(src, dst, slot_send, slot_recv, device):
        return pltpu.make_async_remote_copy(
            src_ref=src, dst_ref=dst, send_sem=send_sem.at[slot_send], recv_sem=recv_sem.at[slot_recv],
            device_id=device, device_id_type=MESH,
        )

    f_lo = (src_hbm.at[:, :, pl.ds(0, HALO), :], rec_hbm.at[:, :, pl.ds(0, HALO), :])
    s_lo = slow_hbm.at[0, pl.ds(0, HALO), :]
    for q in range(n_freq):
        @pl.when(f != q)
        def _():
            remote(slow_hbm, g_slow.at[f], q, f, (t, q)).start()

        @pl.when(has_above)
        def _():
            remote(s_lo, h_sb.at[f], 2 * n_freq + q, 2 * n_freq + f, (t - 1, q)).start()

    field_base = 3 * n_freq

    def lower_copy(x, fi, device):
        return remote(f_lo[x].at[:, fi], h_fb.at[x, :, fi], field_base + 2 + 2 * x + fi,
                      field_base + 2 + 2 * x + fi, device)

    def upper_copy(fi, device):
        return remote(up_buf.at[:, :, fi], h_fa.at[:, :, fi], field_base + fi, field_base + fi, device)

    for fi in range(2):
        @pl.when(has_above)
        def _():
            for x in range(2):
                lower_copy(x, fi, (t - 1, f)).start()

    for copy in loads:
        copy.wait()

    own_rows = lax.broadcasted_iota(jnp.int32, (own, ncol), 0)
    own_forward = pltpu.roll(own_rows, 1, 0) == (own_rows + own - 1) % own
    lift = (own + HALO - ap) % own
    drop = ap - HALO

    def last_rows(x, forward):
        return jnp.where(forward, pltpu.roll(x, lift, 0), pltpu.roll(x, drop, 0))[:HALO]

    s_up[...] = last_rows(g_slow[f, 0], own_forward[:, :block])
    for q in range(n_freq):
        @pl.when(has_below)
        def _():
            remote(s_up, h_sa.at[f], n_freq + q, n_freq + f, (t + 1, q)).start()

    fields_v = (src_v, rec_v)
    for fi in range(nfl):
        for x in range(2):
            for c in range(nc):
                up_buf[x, c, fi] = last_rows(fields_v[x][c, fi], own_forward)

        @pl.when(has_below)
        def _():
            upper_copy(fi, (t + 1, f)).start()

    for q in range(n_freq):
        @pl.when(f != q)
        def _():
            remote(slow_hbm, g_slow.at[q], q, q, (t, q)).wait_send()
            remote(slow_hbm, g_slow.at[q], q, q, (t, q)).wait_recv()

        @pl.when(has_below)
        def _():
            remote(s_up, h_sa.at[q], n_freq + q, n_freq + q, (t + 1, q)).wait_send()
            remote(s_lo, h_sb.at[q], 2 * n_freq + q, 2 * n_freq + q, (t + 1, q)).wait_recv()

        @pl.when(has_above)
        def _():
            remote(s_lo, h_sb.at[q], 2 * n_freq + q, 2 * n_freq + q, (t - 1, q)).wait_send()
            remote(s_up, h_sa.at[q], n_freq + q, n_freq + q, (t - 1, q)).wait_recv()

    def await_fields(fi):
        @pl.when(has_below)
        def _():
            upper_copy(fi, (t + 1, f)).wait_send()
            for x in range(2):
                lower_copy(x, fi, (t + 1, f)).wait_recv()

        @pl.when(has_above)
        def _():
            for x in range(2):
                lower_copy(x, fi, (t - 1, f)).wait_send()
            upper_copy(fi, (t - 1, f)).wait_recv()

    rows = lax.broadcasted_iota(jnp.int32, (ext_rows, ncol), 0)
    cols = lax.broadcasted_iota(jnp.int32, (ext_rows, ncol), 1)
    left_ok = jnp.abs(pltpu.roll(cols, 1, 1) - cols) == 1
    right_ok = jnp.abs(pltpu.roll(cols, ncol - 1, 1) - cols) == 1
    forward = pltpu.roll(rows, 1, 0) == (rows + ext_rows - 1) % ext_rows
    lower_start = HALO + ap
    top_part = rows < lower_start

    def in_band(lo, hi):
        return (rows >= lo) & (rows < hi)

    valid0 = (in_band(0, HALO) & has_above) | in_band(HALO, lower_start) | (
        in_band(lower_start, lower_start + HALO) & has_below)
    reach = HALO // 2
    valid1 = (in_band(HALO - reach, HALO) & has_above) | in_band(HALO, lower_start) | (
        in_band(lower_start, lower_start + reach) & has_below)
    live = lax.broadcasted_iota(jnp.int32, (own, ncol), 0) < ap
    zeros_tail = jnp.zeros((ext_rows - HALO, ncol), jnp.float32)

    def place_lower(lower8):
        padded = jnp.concatenate([lower8, zeros_tail], axis=0)
        ahead = pltpu.roll(padded, lower_start, 0)
        behind = pltpu.roll(padded, ext_rows - lower_start, 0)
        return jnp.where(forward, ahead, behind)

    def joined(upper8, own_rows, lower8):
        top = jnp.concatenate([upper8, own_rows, jnp.zeros((HALO, ncol), jnp.float32)], axis=0)
        return jnp.where(top_part, top, place_lower(lower8))

    def columns_of(pieces):
        return jnp.concatenate(pieces, axis=1)

    slow0 = joined(
        columns_of([h_sa[q] for q in range(n_freq)]),
        columns_of([g_slow[q, 0] for q in range(n_freq)]),
        columns_of([h_sb[q] for q in range(n_freq)]),
    )
    slow0 = jnp.where(valid0, slow0, 0.0)
    slow1 = columns_of([g_slow[q, 1] for q in range(n_freq)])

    def spread(v):
        blur_rows = 0.25 * (pltpu.roll(v, 1, 0) + pltpu.roll(v, ext_rows - 1, 0)) + 0.5 * v
        side = jnp.where(left_ok, pltpu.roll(blur_rows, 1, 1), 0.0) + jnp.where(
            right_ok, pltpu.roll(blur_rows, ncol - 1, 1), 0.0)
        blur_cols = 0.25 * side + 0.5 * blur_rows
        return 2.0 * blur_cols - v

    def coefficient(depth, fi, n, wavenumber):
        coef_re = coeffs[0, n, POWERS - 1] + 0.0 * wavenumber
        coef_im = coeffs[1, n, POWERS - 1] + 0.0 * wavenumber
        for m in range(POWERS - 2, -1, -1):
            coef_re = coef_re * wavenumber + coeffs[0, n, m]
            coef_im = coef_im * wavenumber + coeffs[1, n, m]
        active = (orders[depth, fi] >= n).astype(jnp.float32)
        return coef_re * active, coef_im * active

    def extrapolate(depth, fi, wavenumber, valid, lo, hi, write):
        for n in range(ORDER + 1):
            slot = n % 3
            if n >= 1:
                cur, prev = (n - 1) % 3, (n - 2) % 3
                for p in range(4):
                    g = spread(tb[cur, p])
                    if n > 1:
                        g = 2.0 * g - tb[prev, p]
                    tb[slot, p] = jnp.where(valid, g, 0.0)
            coef_re, coef_im = coefficient(depth, fi, n, wavenumber)
            s_re = tb[slot, 0, lo:hi, :]
            s_im = tb[slot, 1, lo:hi, :]
            r_re = tb[slot, 2, lo:hi, :]
            r_im = tb[slot, 3, lo:hi, :]
            terms = (
                coef_re * s_re + coef_im * s_im,
                coef_re * s_im - coef_im * s_re,
                coef_re * r_re - coef_im * r_im,
                coef_re * r_im + coef_im * r_re,
            )
            write(n, terms)

    fields = (src_v, rec_v)
    for fi in range(nfl):
        await_fields(fi)
        for p in range(4):
            x, c = p // 2, p % 2
            tb[0, p] = jnp.where(valid0, joined(h_fa[x, c, fi], fields[x][c, fi], h_fb[x, c, fi]), 0.0)

        def write0(n, terms, fi=fi):
            for p in range(4):
                if n == 0:
                    s1[p // 2, p % 2, fi] = terms[p]
                else:
                    s1[p // 2, p % 2, fi] = s1[p // 2, p % 2, fi] + terms[p]

        extrapolate(0, fi, frequency[fi] * slow0, valid0, 0, ext_rows, write0)
        for p in range(4):
            s1[p // 2, p % 2, fi] = jnp.where(valid1, s1[p // 2, p % 2, fi], 0.0)
        mid = slice(HALO, HALO + own)
        term = s1[0, 0, fi, mid, :] * s1[1, 0, fi, mid, :] + s1[0, 1, fi, mid, :] * s1[1, 1, fi, mid, :]
        term = jnp.where(live, term, 0.0)
        if fi == 0:
            img_out[0] = term
        else:
            img_out[0] = img_out[0] + term

    image_base = 3 * n_freq + 6

    def image_copy(depth, q, slot_recv, device):
        return pltpu.make_async_remote_copy(
            src_ref=img_out.at[depth, :, pl.ds(q * block, block)], dst_ref=got.at[slot_recv, depth],
            send_sem=send_sem.at[image_base + depth * n_freq + q],
            recv_sem=recv_sem.at[image_base + depth * n_freq + slot_recv],
            device_id=device, device_id_type=MESH,
        )

    def send_image(depth):
        for q in range(n_freq):
            @pl.when(f != q)
            def _():
                image_copy(depth, q, f, (t, q)).start()

    send_image(0)

    for fi in range(nfl):
        for p in range(4):
            tb[0, p] = s1[p // 2, p % 2, fi]
        acc = {}

        def write1(n, terms, acc=acc):
            for p in range(4):
                acc[p] = terms[p] if n == 0 else acc[p] + terms[p]

        extrapolate(1, fi, frequency[fi] * slow1, valid1, HALO, HALO + own, write1)
        result = [jnp.where(live, acc[p], 0.0) for p in range(4)]
        rec_out[0, fi] = result[2]
        rec_out[1, fi] = result[3]
        term = result[0] * result[2] + result[1] * result[3]
        if fi == 0:
            img_out[1] = term
        else:
            img_out[1] = img_out[1] + term

    send_image(1)
    for depth in range(NDEPTH):
        for q in range(n_freq):
            @pl.when(f != q)
            def _():
                image_copy(depth, q, q, (t, q)).wait_send()
                image_copy(depth, q, q, (t, q)).wait_recv()

    total = None
    for q in range(n_freq):
        mine = img_out[:, :, q * block:(q + 1) * block]
        part = jnp.where(f == q, mine, got[q])
        total = part if total is None else total + part
    image_out[...] = total


def shards(n_tile, n_freq, source_field, receiver_field, slowness, frequency, order_table, filter_coeffs, aperture):
    nc, nfl, own, ncol = source_field.shape
    block = slowness.shape[2]
    ext_rows = own + 2 * HALO
    elements = nc * nfl * 2 * ext_rows * ncol * NDEPTH
    rec_out, image_out = pl.pallas_call(
        functools.partial(migrate_kernel, n_tile, n_freq),
        out_shape=(
            jax.ShapeDtypeStruct((nc, nfl, own, ncol), jnp.float32),
            jax.ShapeDtypeStruct((NDEPTH, own, block), jnp.float32),
        ),
        in_specs=[pl.BlockSpec(memory_space=SMEM)] * 4 + [pl.BlockSpec(memory_space=pl.ANY)] * 3,
        out_specs=(pl.BlockSpec(memory_space=VMEM), pl.BlockSpec(memory_space=VMEM)),
        scratch_shapes=[
            pltpu.VMEM((nc, nfl, own, ncol), jnp.float32),
            pltpu.VMEM((nc, nfl, own, ncol), jnp.float32),
            pltpu.VMEM((n_freq, NDEPTH, own, block), jnp.float32),
            pltpu.VMEM((n_freq, HALO, block), jnp.float32),
            pltpu.VMEM((n_freq, HALO, block), jnp.float32),
            pltpu.VMEM((2, nc, nfl, HALO, ncol), jnp.float32),
            pltpu.VMEM((2, nc, nfl, HALO, ncol), jnp.float32),
            pltpu.VMEM((2, nc, nfl, HALO, ncol), jnp.float32),
            pltpu.VMEM((HALO, block), jnp.float32),
            pltpu.VMEM((2, nc, nfl, ext_rows, ncol), jnp.float32),
            pltpu.VMEM((3, 4, ext_rows, ncol), jnp.float32),
            pltpu.VMEM((NDEPTH, own, ncol), jnp.float32),
            pltpu.VMEM((n_freq, NDEPTH, own, block), jnp.float32),
            pltpu.SemaphoreType.DMA((3,)),
            pltpu.SemaphoreType.DMA((3 * n_freq + 6 + NDEPTH * n_freq,)),
            pltpu.SemaphoreType.DMA((3 * n_freq + 6 + NDEPTH * n_freq,)),
        ],
        compiler_params=pltpu.CompilerParams(collective_id=0, has_side_effects=True),
        cost_estimate=pl.CostEstimate(flops=elements * 100, bytes_accessed=elements * 4, transcendentals=0),
    )(aperture, order_table, frequency, filter_coeffs, source_field, receiver_field, slowness)
    return (image_out, rec_out)


def solution(mesh):
    placed = (
        P(None, "freq", "tile", None),
        P(None, "freq", "tile", None),
        P(None, "tile", "freq"),
        P("freq"),
        P(None, "freq"),
        P(),
        P(),
    )
    return jax.shard_map(
        functools.partial(shards, mesh.shape["tile"], mesh.shape["freq"]),
        mesh=mesh,
        in_specs=placed,
        out_specs=(P(None, "tile", "freq"), P(None, "freq", "tile", None)),
        check_vma=False,
    )
```

```python
import functools

import jax
import jax.numpy as jnp
from jax import lax
from jax.experimental import pallas as pl
from jax.experimental.pallas import tpu as pltpu
from jax.sharding import PartitionSpec as P

ORDER = 4
NDEPTH = 2
POWERS = 3
HALO = 8
MESH = pl.DeviceIdType.MESH
VMEM = pltpu.MemorySpace.VMEM
SMEM = pltpu.MemorySpace.SMEM


def migrate_kernel(n_tile, n_freq, period, aperture, orders, frequency, coeffs, src_hbm, rec_hbm, slow_hbm,
                   rec_out, image_out, src_v, rec_v, g_slow, h_sa, h_sb, h_fa, h_fb, up_buf, s_up, s1, tb, img_out,
                   got, rl_up, rl_lo, local_sem, send_sem, recv_sem):
    t = lax.axis_index("tile")
    f = lax.axis_index("freq")
    nc, nfl, own, ncol = src_v.shape
    ext_rows = HALO + own + HALO
    block = slow_hbm.shape[2]
    ap = aperture[t]
    has_above = t > 0
    has_below = t < n_tile - 1
    partner = (f + n_freq // 2) % n_freq
    if period:
        up_cross = has_below & (t % period == period - 1)
        lo_cross = has_above & (t % period == 0)
    else:
        up_cross = t < 0
        lo_cross = t < 0
    up_direct = has_below & jnp.logical_not(up_cross)
    lo_direct = has_above & jnp.logical_not(lo_cross)

    loads = (
        pltpu.make_async_copy(src_hbm, src_v, local_sem.at[0]),
        pltpu.make_async_copy(rec_hbm, rec_v, local_sem.at[1]),
        pltpu.make_async_copy(slow_hbm, g_slow.at[f], local_sem.at[2]),
    )
    for copy in loads:
        copy.start()

    @pl.when(t == 0)
    def _():
        h_fa[...] = jnp.zeros_like(h_fa)
        h_sa[...] = jnp.zeros_like(h_sa)

    @pl.when(t == n_tile - 1)
    def _():
        h_fb[...] = jnp.zeros_like(h_fb)
        h_sb[...] = jnp.zeros_like(h_sb)

    barrier = pltpu.get_barrier_semaphore()
    for q in range(n_freq):
        @pl.when(f != q)
        def _():
            pl.semaphore_signal(barrier, 1, device_id=(t, q), device_id_type=MESH)

        @pl.when(has_above)
        def _():
            pl.semaphore_signal(barrier, 1, device_id=(t - 1, q), device_id_type=MESH)

        @pl.when(has_below)
        def _():
            pl.semaphore_signal(barrier, 1, device_id=(t + 1, q), device_id_type=MESH)

    expected = (n_freq - 1) + n_freq * has_above.astype(jnp.int32) + n_freq * has_below.astype(jnp.int32)
    pl.semaphore_wait(barrier, expected)

    def remote(src, dst, slot_send, slot_recv, device):
        return pltpu.make_async_remote_copy(
            src_ref=src, dst_ref=dst, send_sem=send_sem.at[slot_send], recv_sem=recv_sem.at[slot_recv],
            device_id=device, device_id_type=MESH,
        )

    f_lo = (src_hbm.at[:, :, pl.ds(0, HALO), :], rec_hbm.at[:, :, pl.ds(0, HALO), :])
    s_lo = slow_hbm.at[0, pl.ds(0, HALO), :]
    for q in range(n_freq):
        @pl.when(f != q)
        def _():
            remote(slow_hbm, g_slow.at[f], q, f, (t, q)).start()

        @pl.when(has_above)
        def _():
            remote(s_lo, h_sb.at[f], 2 * n_freq + q, 2 * n_freq + f, (t - 1, q)).start()

    field_base = 3 * n_freq
    relay_base = 3 * n_freq + 6 + NDEPTH * n_freq

    def lower_copy(x, fi, device):
        return remote(f_lo[x].at[:, fi], h_fb.at[x, :, fi], field_base + 2 + 2 * x + fi,
                      field_base + 2 + 2 * x + fi, device)

    def upper_copy(fi, device):
        return remote(up_buf.at[:, :, fi], h_fa.at[:, :, fi], field_base + fi, field_base + fi, device)

    def lower_to_relay(x, fi, device):
        return remote(f_lo[x].at[:, fi], rl_lo.at[x, :, fi], field_base + 2 + 2 * x + fi,
                      relay_base + 2 + 2 * x + fi, device)

    def upper_to_relay(fi, device):
        return remote(up_buf.at[:, :, fi], rl_up.at[:, :, fi], field_base + fi, relay_base + fi, device)

    def lower_forward(x, fi, device):
        return remote(rl_lo.at[x, :, fi], h_fb.at[x, :, fi], relay_base + 6 + 2 + 2 * x + fi,
                      field_base + 2 + 2 * x + fi, device)

    def upper_forward(fi, device):
        return remote(rl_up.at[:, :, fi], h_fa.at[:, :, fi], relay_base + 6 + fi, field_base + fi, device)

    for fi in range(2):
        @pl.when(lo_direct)
        def _():
            for x in range(2):
                lower_copy(x, fi, (t - 1, f)).start()

        @pl.when(lo_cross)
        def _():
            for x in range(2):
                lower_to_relay(x, fi, (t - 1, partner)).start()

    for copy in loads:
        copy.wait()

    own_rows = lax.broadcasted_iota(jnp.int32, (own, ncol), 0)
    own_forward = pltpu.roll(own_rows, 1, 0) == (own_rows + own - 1) % own
    lift = (own + HALO - ap) % own
    drop = ap - HALO

    def last_rows(x, forward):
        return jnp.where(forward, pltpu.roll(x, lift, 0), pltpu.roll(x, drop, 0))[:HALO]

    s_up[...] = last_rows(g_slow[f, 0], own_forward[:, :block])
    for q in range(n_freq):
        @pl.when(has_below)
        def _():
            remote(s_up, h_sa.at[f], n_freq + q, n_freq + f, (t + 1, q)).start()

    fields_v = (src_v, rec_v)
    for fi in range(nfl):
        for x in range(2):
            for c in range(nc):
                up_buf[x, c, fi] = last_rows(fields_v[x][c, fi], own_forward)

        @pl.when(up_direct)
        def _():
            upper_copy(fi, (t + 1, f)).start()

        @pl.when(up_cross)
        def _():
            upper_to_relay(fi, (t + 1, partner)).start()

    for fi in range(nfl):
        @pl.when(lo_cross)
        def _():
            upper_to_relay(fi, (t - 1, partner)).wait_recv()
            upper_forward(fi, (t, partner)).start()

        @pl.when(up_cross)
        def _():
            for x in range(2):
                lower_to_relay(x, fi, (t + 1, partner)).wait_recv()
                lower_forward(x, fi, (t, partner)).start()

    for q in range(n_freq):
        @pl.when(f != q)
        def _():
            remote(slow_hbm, g_slow.at[q], q, q, (t, q)).wait_send()
            remote(slow_hbm, g_slow.at[q], q, q, (t, q)).wait_recv()

        @pl.when(has_below)
        def _():
            remote(s_up, h_sa.at[q], n_freq + q, n_freq + q, (t + 1, q)).wait_send()
            remote(s_lo, h_sb.at[q], 2 * n_freq + q, 2 * n_freq + q, (t + 1, q)).wait_recv()

        @pl.when(has_above)
        def _():
            remote(s_lo, h_sb.at[q], 2 * n_freq + q, 2 * n_freq + q, (t - 1, q)).wait_send()
            remote(s_up, h_sa.at[q], n_freq + q, n_freq + q, (t - 1, q)).wait_recv()

    def await_fields(fi):
        @pl.when(lo_cross)
        def _():
            upper_forward(fi, (t, partner)).wait_send()

        @pl.when(up_cross)
        def _():
            for x in range(2):
                lower_forward(x, fi, (t, partner)).wait_send()

        @pl.when(has_below)
        def _():
            upper_copy(fi, (t + 1, f)).wait_send()
            for x in range(2):
                lower_copy(x, fi, (t + 1, f)).wait_recv()

        @pl.when(has_above)
        def _():
            for x in range(2):
                lower_copy(x, fi, (t - 1, f)).wait_send()
            upper_copy(fi, (t - 1, f)).wait_recv()

    rows = lax.broadcasted_iota(jnp.int32, (ext_rows, ncol), 0)
    cols = lax.broadcasted_iota(jnp.int32, (ext_rows, ncol), 1)
    left_ok = jnp.abs(pltpu.roll(cols, 1, 1) - cols) == 1
    right_ok = jnp.abs(pltpu.roll(cols, ncol - 1, 1) - cols) == 1
    forward = pltpu.roll(rows, 1, 0) == (rows + ext_rows - 1) % ext_rows
    lower_start = HALO + ap
    top_part = rows < lower_start

    def in_band(lo, hi):
        return (rows >= lo) & (rows < hi)

    valid0 = (in_band(0, HALO) & has_above) | in_band(HALO, lower_start) | (
        in_band(lower_start, lower_start + HALO) & has_below)
    reach = HALO // 2
    valid1 = (in_band(HALO - reach, HALO) & has_above) | in_band(HALO, lower_start) | (
        in_band(lower_start, lower_start + reach) & has_below)
    live = lax.broadcasted_iota(jnp.int32, (own, ncol), 0) < ap
    zeros_tail = jnp.zeros((ext_rows - HALO, ncol), jnp.float32)

    def place_lower(lower8):
        padded = jnp.concatenate([lower8, zeros_tail], axis=0)
        ahead = pltpu.roll(padded, lower_start, 0)
        behind = pltpu.roll(padded, ext_rows - lower_start, 0)
        return jnp.where(forward, ahead, behind)

    def joined(upper8, own_rows, lower8):
        top = jnp.concatenate([upper8, own_rows, jnp.zeros((HALO, ncol), jnp.float32)], axis=0)
        return jnp.where(top_part, top, place_lower(lower8))

    def columns_of(pieces):
        return jnp.concatenate(pieces, axis=1)

    slow0 = joined(
        columns_of([h_sa[q] for q in range(n_freq)]),
        columns_of([g_slow[q, 0] for q in range(n_freq)]),
        columns_of([h_sb[q] for q in range(n_freq)]),
    )
    slow0 = jnp.where(valid0, slow0, 0.0)
    slow1 = columns_of([g_slow[q, 1] for q in range(n_freq)])

    def spread(v):
        blur_rows = 0.25 * (pltpu.roll(v, 1, 0) + pltpu.roll(v, ext_rows - 1, 0)) + 0.5 * v
        side = jnp.where(left_ok, pltpu.roll(blur_rows, 1, 1), 0.0) + jnp.where(
            right_ok, pltpu.roll(blur_rows, ncol - 1, 1), 0.0)
        blur_cols = 0.25 * side + 0.5 * blur_rows
        return 2.0 * blur_cols - v

    def coefficient(depth, fi, n, wavenumber):
        coef_re = coeffs[0, n, POWERS - 1] + 0.0 * wavenumber
        coef_im = coeffs[1, n, POWERS - 1] + 0.0 * wavenumber
        for m in range(POWERS - 2, -1, -1):
            coef_re = coef_re * wavenumber + coeffs[0, n, m]
            coef_im = coef_im * wavenumber + coeffs[1, n, m]
        active = (orders[depth, fi] >= n).astype(jnp.float32)
        return coef_re * active, coef_im * active

    def extrapolate(depth, fi, wavenumber, valid, lo, hi, write):
        for n in range(ORDER + 1):
            slot = n % 3
            if n >= 1:
                cur, prev = (n - 1) % 3, (n - 2) % 3
                for p in range(4):
                    g = spread(tb[cur, p])
                    if n > 1:
                        g = 2.0 * g - tb[prev, p]
                    tb[slot, p] = jnp.where(valid, g, 0.0)
            coef_re, coef_im = coefficient(depth, fi, n, wavenumber)
            s_re = tb[slot, 0, lo:hi, :]
            s_im = tb[slot, 1, lo:hi, :]
            r_re = tb[slot, 2, lo:hi, :]
            r_im = tb[slot, 3, lo:hi, :]
            terms = (
                coef_re * s_re + coef_im * s_im,
                coef_re * s_im - coef_im * s_re,
                coef_re * r_re - coef_im * r_im,
                coef_re * r_im + coef_im * r_re,
            )
            write(n, terms)

    fields = (src_v, rec_v)
    for fi in range(nfl):
        await_fields(fi)
        for p in range(4):
            x, c = p // 2, p % 2
            tb[0, p] = jnp.where(valid0, joined(h_fa[x, c, fi], fields[x][c, fi], h_fb[x, c, fi]), 0.0)

        def write0(n, terms, fi=fi):
            for p in range(4):
                if n == 0:
                    s1[p // 2, p % 2, fi] = terms[p]
                else:
                    s1[p // 2, p % 2, fi] = s1[p // 2, p % 2, fi] + terms[p]

        extrapolate(0, fi, frequency[fi] * slow0, valid0, 0, ext_rows, write0)
        for p in range(4):
            s1[p // 2, p % 2, fi] = jnp.where(valid1, s1[p // 2, p % 2, fi], 0.0)
        mid = slice(HALO, HALO + own)
        term = s1[0, 0, fi, mid, :] * s1[1, 0, fi, mid, :] + s1[0, 1, fi, mid, :] * s1[1, 1, fi, mid, :]
        term = jnp.where(live, term, 0.0)
        if fi == 0:
            img_out[0] = term
        else:
            img_out[0] = img_out[0] + term

    image_base = 3 * n_freq + 6

    def image_copy(depth, q, slot_recv, device):
        return pltpu.make_async_remote_copy(
            src_ref=img_out.at[depth, :, pl.ds(q * block, block)], dst_ref=got.at[slot_recv, depth],
            send_sem=send_sem.at[image_base + depth * n_freq + q],
            recv_sem=recv_sem.at[image_base + depth * n_freq + slot_recv],
            device_id=device, device_id_type=MESH,
        )

    def send_image(depth):
        for q in range(n_freq):
            @pl.when(f != q)
            def _():
                image_copy(depth, q, f, (t, q)).start()

    send_image(0)

    for fi in range(nfl):
        for p in range(4):
            tb[0, p] = s1[p // 2, p % 2, fi]
        acc = {}

        def write1(n, terms, acc=acc):
            for p in range(4):
                acc[p] = terms[p] if n == 0 else acc[p] + terms[p]

        extrapolate(1, fi, frequency[fi] * slow1, valid1, HALO, HALO + own, write1)
        result = [jnp.where(live, acc[p], 0.0) for p in range(4)]
        rec_out[0, fi] = result[2]
        rec_out[1, fi] = result[3]
        term = result[0] * result[2] + result[1] * result[3]
        if fi == 0:
            img_out[1] = term
        else:
            img_out[1] = img_out[1] + term

    send_image(1)
    for depth in range(NDEPTH):
        for q in range(n_freq):
            @pl.when(f != q)
            def _():
                image_copy(depth, q, q, (t, q)).wait_send()
                image_copy(depth, q, q, (t, q)).wait_recv()

    total = None
    for q in range(n_freq):
        mine = img_out[:, :, q * block:(q + 1) * block]
        part = jnp.where(f == q, mine, got[q])
        total = part if total is None else total + part
    image_out[...] = total


def shards(n_tile, n_freq, period, source_field, receiver_field, slowness, frequency, order_table, filter_coeffs, aperture):
    nc, nfl, own, ncol = source_field.shape
    block = slowness.shape[2]
    ext_rows = own + 2 * HALO
    elements = nc * nfl * 2 * ext_rows * ncol * NDEPTH
    rec_out, image_out = pl.pallas_call(
        functools.partial(migrate_kernel, n_tile, n_freq, period),
        out_shape=(
            jax.ShapeDtypeStruct((nc, nfl, own, ncol), jnp.float32),
            jax.ShapeDtypeStruct((NDEPTH, own, block), jnp.float32),
        ),
        in_specs=[pl.BlockSpec(memory_space=SMEM)] * 4 + [pl.BlockSpec(memory_space=pl.ANY)] * 3,
        out_specs=(pl.BlockSpec(memory_space=VMEM), pl.BlockSpec(memory_space=VMEM)),
        scratch_shapes=[
            pltpu.VMEM((nc, nfl, own, ncol), jnp.float32),
            pltpu.VMEM((nc, nfl, own, ncol), jnp.float32),
            pltpu.VMEM((n_freq, NDEPTH, own, block), jnp.float32),
            pltpu.VMEM((n_freq, HALO, block), jnp.float32),
            pltpu.VMEM((n_freq, HALO, block), jnp.float32),
            pltpu.VMEM((2, nc, nfl, HALO, ncol), jnp.float32),
            pltpu.VMEM((2, nc, nfl, HALO, ncol), jnp.float32),
            pltpu.VMEM((2, nc, nfl, HALO, ncol), jnp.float32),
            pltpu.VMEM((HALO, block), jnp.float32),
            pltpu.VMEM((2, nc, nfl, ext_rows, ncol), jnp.float32),
            pltpu.VMEM((3, 4, ext_rows, ncol), jnp.float32),
            pltpu.VMEM((NDEPTH, own, ncol), jnp.float32),
            pltpu.VMEM((n_freq, NDEPTH, own, block), jnp.float32),
            pltpu.VMEM((2, nc, nfl, HALO, ncol), jnp.float32),
            pltpu.VMEM((2, nc, nfl, HALO, ncol), jnp.float32),
            pltpu.SemaphoreType.DMA((3,)),
            pltpu.SemaphoreType.DMA((3 * n_freq + 6 + NDEPTH * n_freq + 12,)),
            pltpu.SemaphoreType.DMA((3 * n_freq + 6 + NDEPTH * n_freq + 12,)),
        ],
        compiler_params=pltpu.CompilerParams(collective_id=0, has_side_effects=True),
        cost_estimate=pl.CostEstimate(flops=elements * 100, bytes_accessed=elements * 4, transcendentals=0),
    )(aperture, order_table, frequency, filter_coeffs, source_field, receiver_field, slowness)
    return (image_out, rec_out)


def relay_period(mesh):
    devices = mesh.devices
    n_tile, n_freq = devices.shape
    if n_freq % 2:
        return 0
    try:
        xs = [[d.coords[0] for d in row] for row in devices]
        cores = [[d.core_on_chip for d in row] for row in devices]
        ring = max(max(r) for r in xs) + 1
    except AttributeError:
        return 0
    crossing = []
    for t in range(n_tile - 1):
        gaps = {min((xs[t][q] - xs[t + 1][q]) % ring, (xs[t + 1][q] - xs[t][q]) % ring) for q in range(n_freq)}
        crossing.append(gaps == {2})
    if not any(crossing):
        return 0
    period = crossing.index(True) + 1
    if crossing != [t % period == period - 1 for t in range(n_tile - 1)]:
        return 0
    for t in range(n_tile):
        for q in range(n_freq):
            p = (q + n_freq // 2) % n_freq
            if cores[t][p] != cores[t][q] or xs[t][p] == xs[t][q]:
                return 0
    return period


def solution(mesh):
    placed = (
        P(None, "freq", "tile", None),
        P(None, "freq", "tile", None),
        P(None, "tile", "freq"),
        P("freq"),
        P(None, "freq"),
        P(),
        P(),
    )
    return jax.shard_map(
        functools.partial(shards, mesh.shape["tile"], mesh.shape["freq"], relay_period(mesh)),
        mesh=mesh,
        in_specs=placed,
        out_specs=(P(None, "tile", "freq"), P(None, "freq", "tile", None)),
        check_vma=False,
    )
```

```python
import functools

import jax
import jax.numpy as jnp
from jax import lax
from jax.experimental import pallas as pl
from jax.experimental.pallas import tpu as pltpu
from jax.sharding import PartitionSpec as P

ORDER = 4
NDEPTH = 2
POWERS = 3
HALO = 8
MESH = pl.DeviceIdType.MESH
VMEM = pltpu.MemorySpace.VMEM
SMEM = pltpu.MemorySpace.SMEM


def migrate_kernel(n_tile, n_freq, aperture, orders, frequency, coeffs_hbm, src_hbm, rec_hbm, slow_hbm,
                   rec_out, image_out, src_v, rec_v, g_slow, h_sa, h_sb, h_fa, h_fb, up_buf, s_up, s1, tb, img_out,
                   got, coeffs, cf0, cf1, local_sem, send_sem, recv_sem):
    t = lax.axis_index("tile")
    f = lax.axis_index("freq")
    nc, nfl, own, ncol = src_v.shape
    ext_rows = HALO + own + HALO
    block = slow_hbm.shape[2]
    ap = aperture[t]
    has_above = t > 0
    has_below = t < n_tile - 1

    loads = (
        pltpu.make_async_copy(src_hbm, src_v, local_sem.at[0]),
        pltpu.make_async_copy(rec_hbm, rec_v, local_sem.at[1]),
        pltpu.make_async_copy(slow_hbm, g_slow.at[f], local_sem.at[2]),
        pltpu.make_async_copy(coeffs_hbm, coeffs, local_sem.at[3]),
    )
    for copy in loads:
        copy.start()

    @pl.when(t == 0)
    def _():
        h_fa[...] = jnp.zeros_like(h_fa)
        h_sa[...] = jnp.zeros_like(h_sa)

    @pl.when(t == n_tile - 1)
    def _():
        h_fb[...] = jnp.zeros_like(h_fb)
        h_sb[...] = jnp.zeros_like(h_sb)

    barrier = pltpu.get_barrier_semaphore()
    for q in range(n_freq):
        @pl.when(f != q)
        def _():
            pl.semaphore_signal(barrier, 1, device_id=(t, q), device_id_type=MESH)

        @pl.when(has_above)
        def _():
            pl.semaphore_signal(barrier, 1, device_id=(t - 1, q), device_id_type=MESH)

        @pl.when(has_below)
        def _():
            pl.semaphore_signal(barrier, 1, device_id=(t + 1, q), device_id_type=MESH)

    expected = (n_freq - 1) + n_freq * has_above.astype(jnp.int32) + n_freq * has_below.astype(jnp.int32)

    for copy in loads:
        copy.wait()

    own_rows = lax.broadcasted_iota(jnp.int32, (own, ncol), 0)
    own_forward = pltpu.roll(own_rows, 1, 0) == (own_rows + own - 1) % own
    lift = (own + HALO - ap) % own
    drop = ap - HALO

    def last_rows(x, forward):
        return jnp.where(forward, pltpu.roll(x, lift, 0), pltpu.roll(x, drop, 0))[:HALO]

    s_up[...] = last_rows(g_slow[f, 0], own_forward[:, :block])
    fields_v = (src_v, rec_v)
    for fi in range(nfl):
        for x in range(2):
            for c in range(nc):
                up_buf[x, c, fi] = last_rows(fields_v[x][c, fi], own_forward)

    pl.semaphore_wait(barrier, expected)

    def remote(src, dst, slot_send, slot_recv, device):
        return pltpu.make_async_remote_copy(
            src_ref=src, dst_ref=dst, send_sem=send_sem.at[slot_send], recv_sem=recv_sem.at[slot_recv],
            device_id=device, device_id_type=MESH,
        )

    f_lo = (src_hbm.at[:, :, pl.ds(0, HALO), :], rec_hbm.at[:, :, pl.ds(0, HALO), :])
    s_lo = slow_hbm.at[0, pl.ds(0, HALO), :]
    for q in range(n_freq):
        @pl.when(f != q)
        def _():
            remote(slow_hbm, g_slow.at[f], q, f, (t, q)).start()

        @pl.when(has_above)
        def _():
            remote(s_lo, h_sb.at[f], 2 * n_freq + q, 2 * n_freq + f, (t - 1, q)).start()

    field_base = 3 * n_freq

    def lower_copy(x, fi, device):
        return remote(f_lo[x].at[:, fi], h_fb.at[x, :, fi], field_base + 2 + 2 * x + fi,
                      field_base + 2 + 2 * x + fi, device)

    def upper_copy(fi, device):
        return remote(up_buf.at[:, :, fi], h_fa.at[:, :, fi], field_base + fi, field_base + fi, device)

    for fi in range(2):
        @pl.when(has_above)
        def _():
            for x in range(2):
                lower_copy(x, fi, (t - 1, f)).start()

    for q in range(n_freq):
        @pl.when(has_below)
        def _():
            remote(s_up, h_sa.at[f], n_freq + q, n_freq + f, (t + 1, q)).start()

    for fi in range(nfl):
        @pl.when(has_below)
        def _():
            upper_copy(fi, (t + 1, f)).start()

    for q in range(n_freq):
        @pl.when(f != q)
        def _():
            remote(slow_hbm, g_slow.at[q], q, q, (t, q)).wait_send()
            remote(slow_hbm, g_slow.at[q], q, q, (t, q)).wait_recv()

        @pl.when(has_below)
        def _():
            remote(s_up, h_sa.at[q], n_freq + q, n_freq + q, (t + 1, q)).wait_send()
            remote(s_lo, h_sb.at[q], 2 * n_freq + q, 2 * n_freq + q, (t + 1, q)).wait_recv()

        @pl.when(has_above)
        def _():
            remote(s_lo, h_sb.at[q], 2 * n_freq + q, 2 * n_freq + q, (t - 1, q)).wait_send()
            remote(s_up, h_sa.at[q], n_freq + q, n_freq + q, (t - 1, q)).wait_recv()

    def await_fields(fi):
        @pl.when(has_below)
        def _():
            upper_copy(fi, (t + 1, f)).wait_send()
            for x in range(2):
                lower_copy(x, fi, (t + 1, f)).wait_recv()

        @pl.when(has_above)
        def _():
            for x in range(2):
                lower_copy(x, fi, (t - 1, f)).wait_send()
            upper_copy(fi, (t - 1, f)).wait_recv()

    rows = lax.broadcasted_iota(jnp.int32, (ext_rows, ncol), 0)
    cols = lax.broadcasted_iota(jnp.int32, (ext_rows, ncol), 1)
    left_ok = jnp.abs(pltpu.roll(cols, 1, 1) - cols) == 1
    right_ok = jnp.abs(pltpu.roll(cols, ncol - 1, 1) - cols) == 1
    forward = pltpu.roll(rows, 1, 0) == (rows + ext_rows - 1) % ext_rows
    lower_start = HALO + ap
    top_part = rows < lower_start

    def in_band(lo, hi):
        return (rows >= lo) & (rows < hi)

    valid0 = (in_band(0, HALO) & has_above) | in_band(HALO, lower_start) | (
        in_band(lower_start, lower_start + HALO) & has_below)
    reach = HALO // 2
    valid1 = (in_band(HALO - reach, HALO) & has_above) | in_band(HALO, lower_start) | (
        in_band(lower_start, lower_start + reach) & has_below)
    live = lax.broadcasted_iota(jnp.int32, (own, ncol), 0) < ap
    zeros_tail = jnp.zeros((ext_rows - HALO, ncol), jnp.float32)

    def place_lower(lower8):
        padded = jnp.concatenate([lower8, zeros_tail], axis=0)
        ahead = pltpu.roll(padded, lower_start, 0)
        behind = pltpu.roll(padded, ext_rows - lower_start, 0)
        return jnp.where(forward, ahead, behind)

    def joined(upper8, own_rows, lower8):
        top = jnp.concatenate([upper8, own_rows, jnp.zeros((HALO, ncol), jnp.float32)], axis=0)
        return jnp.where(top_part, top, place_lower(lower8))

    def columns_of(pieces):
        return jnp.concatenate(pieces, axis=1)

    slow0 = joined(
        columns_of([h_sa[q] for q in range(n_freq)]),
        columns_of([g_slow[q, 0] for q in range(n_freq)]),
        columns_of([h_sb[q] for q in range(n_freq)]),
    )
    slow0 = jnp.where(valid0, slow0, 0.0)
    slow1 = columns_of([g_slow[q, 1] for q in range(n_freq)])

    def spread(v):
        blur_rows = 0.25 * (pltpu.roll(v, 1, 0) + pltpu.roll(v, ext_rows - 1, 0)) + 0.5 * v
        side = jnp.where(left_ok, pltpu.roll(blur_rows, 1, 1), 0.0) + jnp.where(
            right_ok, pltpu.roll(blur_rows, ncol - 1, 1), 0.0)
        blur_cols = 0.25 * side + 0.5 * blur_rows
        return 2.0 * blur_cols - v

    def coefficient_of(depth, fi, n, wavenumber):
        coef_re = coeffs[0, n, POWERS - 1] + 0.0 * wavenumber
        coef_im = coeffs[1, n, POWERS - 1] + 0.0 * wavenumber
        for m in range(POWERS - 2, -1, -1):
            coef_re = coef_re * wavenumber + coeffs[0, n, m]
            coef_im = coef_im * wavenumber + coeffs[1, n, m]
        active = (orders[depth, fi] >= n).astype(jnp.float32)
        return coef_re * active, coef_im * active

    for fi in range(nfl):
        for n in range(ORDER + 1):
            cf0[fi, n, 0], cf0[fi, n, 1] = coefficient_of(0, fi, n, frequency[fi] * slow0)
            cf1[fi, n, 0], cf1[fi, n, 1] = coefficient_of(1, fi, n, frequency[fi] * slow1)

    def coefficient(depth, fi, n, wavenumber):
        table = cf0 if depth == 0 else cf1
        return table[fi, n, 0], table[fi, n, 1]

    def extrapolate(depth, fi, wavenumber, valid, lo, hi, write):
        for n in range(ORDER + 1):
            slot = n % 3
            if n >= 1:
                cur, prev = (n - 1) % 3, (n - 2) % 3
                for p in range(4):
                    g = spread(tb[cur, p])
                    if n > 1:
                        g = 2.0 * g - tb[prev, p]
                    tb[slot, p] = jnp.where(valid, g, 0.0)
            coef_re, coef_im = coefficient(depth, fi, n, wavenumber)
            s_re = tb[slot, 0, lo:hi, :]
            s_im = tb[slot, 1, lo:hi, :]
            r_re = tb[slot, 2, lo:hi, :]
            r_im = tb[slot, 3, lo:hi, :]
            terms = (
                coef_re * s_re + coef_im * s_im,
                coef_re * s_im - coef_im * s_re,
                coef_re * r_re - coef_im * r_im,
                coef_re * r_im + coef_im * r_re,
            )
            write(n, terms)

    fields = (src_v, rec_v)
    for fi in range(nfl):
        await_fields(fi)
        for p in range(4):
            x, c = p // 2, p % 2
            tb[0, p] = jnp.where(valid0, joined(h_fa[x, c, fi], fields[x][c, fi], h_fb[x, c, fi]), 0.0)

        def write0(n, terms, fi=fi):
            for p in range(4):
                if n == 0:
                    s1[p // 2, p % 2, fi] = terms[p]
                else:
                    s1[p // 2, p % 2, fi] = s1[p // 2, p % 2, fi] + terms[p]

        extrapolate(0, fi, frequency[fi] * slow0, valid0, 0, ext_rows, write0)
        for p in range(4):
            s1[p // 2, p % 2, fi] = jnp.where(valid1, s1[p // 2, p % 2, fi], 0.0)
        mid = slice(HALO, HALO + own)
        term = s1[0, 0, fi, mid, :] * s1[1, 0, fi, mid, :] + s1[0, 1, fi, mid, :] * s1[1, 1, fi, mid, :]
        term = jnp.where(live, term, 0.0)
        if fi == 0:
            img_out[0] = term
        else:
            img_out[0] = img_out[0] + term

    image_base = 3 * n_freq + 6

    def image_copy(depth, q, slot_recv, device):
        return pltpu.make_async_remote_copy(
            src_ref=img_out.at[depth, :, pl.ds(q * block, block)], dst_ref=got.at[slot_recv, depth],
            send_sem=send_sem.at[image_base + depth * n_freq + q],
            recv_sem=recv_sem.at[image_base + depth * n_freq + slot_recv],
            device_id=device, device_id_type=MESH,
        )

    def send_image(depth):
        for q in range(n_freq):
            @pl.when(f != q)
            def _():
                image_copy(depth, q, f, (t, q)).start()

    send_image(0)

    for fi in range(nfl):
        for p in range(4):
            tb[0, p] = s1[p // 2, p % 2, fi]
        acc = {}

        def write1(n, terms, acc=acc):
            for p in range(4):
                acc[p] = terms[p] if n == 0 else acc[p] + terms[p]

        extrapolate(1, fi, frequency[fi] * slow1, valid1, HALO, HALO + own, write1)
        result = [jnp.where(live, acc[p], 0.0) for p in range(4)]
        rec_out[0, fi] = result[2]
        rec_out[1, fi] = result[3]
        term = result[0] * result[2] + result[1] * result[3]
        if fi == 0:
            img_out[1] = term
        else:
            img_out[1] = img_out[1] + term

    send_image(1)
    for depth in range(NDEPTH):
        for q in range(n_freq):
            @pl.when(f != q)
            def _():
                image_copy(depth, q, q, (t, q)).wait_send()
                image_copy(depth, q, q, (t, q)).wait_recv()

    total = None
    for q in range(n_freq):
        mine = img_out[:, :, q * block:(q + 1) * block]
        part = jnp.where(f == q, mine, got[q])
        total = part if total is None else total + part
    image_out[...] = total


def shards(n_tile, n_freq, source_field, receiver_field, slowness, frequency, order_table, filter_coeffs, aperture):
    nc, nfl, own, ncol = source_field.shape
    block = slowness.shape[2]
    ext_rows = own + 2 * HALO
    elements = nc * nfl * 2 * ext_rows * ncol * NDEPTH
    rec_out, image_out = pl.pallas_call(
        functools.partial(migrate_kernel, n_tile, n_freq),
        out_shape=(
            jax.ShapeDtypeStruct((nc, nfl, own, ncol), jnp.float32),
            jax.ShapeDtypeStruct((NDEPTH, own, block), jnp.float32),
        ),
        in_specs=[pl.BlockSpec(memory_space=SMEM)] * 3 + [pl.BlockSpec(memory_space=pl.ANY)] * 4,
        out_specs=(pl.BlockSpec(memory_space=VMEM), pl.BlockSpec(memory_space=VMEM)),
        scratch_shapes=[
            pltpu.VMEM((nc, nfl, own, ncol), jnp.float32),
            pltpu.VMEM((nc, nfl, own, ncol), jnp.float32),
            pltpu.VMEM((n_freq, NDEPTH, own, block), jnp.float32),
            pltpu.VMEM((n_freq, HALO, block), jnp.float32),
            pltpu.VMEM((n_freq, HALO, block), jnp.float32),
            pltpu.VMEM((2, nc, nfl, HALO, ncol), jnp.float32),
            pltpu.VMEM((2, nc, nfl, HALO, ncol), jnp.float32),
            pltpu.VMEM((2, nc, nfl, HALO, ncol), jnp.float32),
            pltpu.VMEM((HALO, block), jnp.float32),
            pltpu.VMEM((2, nc, nfl, ext_rows, ncol), jnp.float32),
            pltpu.VMEM((3, 4, ext_rows, ncol), jnp.float32),
            pltpu.VMEM((NDEPTH, own, ncol), jnp.float32),
            pltpu.VMEM((n_freq, NDEPTH, own, block), jnp.float32),
            pltpu.SMEM(filter_coeffs.shape, jnp.float32),
            pltpu.VMEM((nfl, ORDER + 1, 2, ext_rows, ncol), jnp.float32),
            pltpu.VMEM((nfl, ORDER + 1, 2, own, ncol), jnp.float32),
            pltpu.SemaphoreType.DMA((4,)),
            pltpu.SemaphoreType.DMA((3 * n_freq + 6 + NDEPTH * n_freq,)),
            pltpu.SemaphoreType.DMA((3 * n_freq + 6 + NDEPTH * n_freq,)),
        ],
        compiler_params=pltpu.CompilerParams(collective_id=0, has_side_effects=True),
        cost_estimate=pl.CostEstimate(flops=elements * 100, bytes_accessed=elements * 4, transcendentals=0),
    )(aperture, order_table, frequency, filter_coeffs, source_field, receiver_field, slowness)
    return (image_out, rec_out)


def solution(mesh):
    placed = (
        P(None, "freq", "tile", None),
        P(None, "freq", "tile", None),
        P(None, "tile", "freq"),
        P("freq"),
        P(None, "freq"),
        P(),
        P(),
    )
    return jax.shard_map(
        functools.partial(shards, mesh.shape["tile"], mesh.shape["freq"]),
        mesh=mesh,
        in_specs=placed,
        out_specs=(P(None, "tile", "freq"), P(None, "freq", "tile", None)),
        check_vma=False,
    )
```

```python
import functools

import jax
import jax.numpy as jnp
from jax import lax
from jax.experimental import pallas as pl
from jax.experimental.pallas import tpu as pltpu
from jax.sharding import PartitionSpec as P

ORDER = 4
NDEPTH = 2
POWERS = 3
HALO = 8
PAD = 8
MESH = pl.DeviceIdType.MESH
VMEM = pltpu.MemorySpace.VMEM
SMEM = pltpu.MemorySpace.SMEM


def migrate_kernel(n_tile, n_freq, aperture, orders, frequency, coeffs_hbm, src_hbm, rec_hbm, slow_hbm,
                   rec_out, image_out, src_v, rec_v, g_slow, h_sa, h_sb, h_fa, h_fb, up_buf, s_up, s1, tb, img_out,
                   got, coeffs, cf0, cf1, vmask, acc1, local_sem, send_sem, recv_sem):
    t = lax.axis_index("tile")
    f = lax.axis_index("freq")
    nc, nfl, own, ncol = src_v.shape
    ext_rows = HALO + own + HALO
    block = slow_hbm.shape[2]
    ap = aperture[t]
    has_above = t > 0
    has_below = t < n_tile - 1

    loads = (
        pltpu.make_async_copy(src_hbm, src_v, local_sem.at[0]),
        pltpu.make_async_copy(rec_hbm, rec_v, local_sem.at[1]),
        pltpu.make_async_copy(slow_hbm, g_slow.at[f], local_sem.at[2]),
        pltpu.make_async_copy(coeffs_hbm, coeffs, local_sem.at[3]),
    )
    for copy in loads:
        copy.start()

    @pl.when(t == 0)
    def _():
        h_fa[...] = jnp.zeros_like(h_fa)
        h_sa[...] = jnp.zeros_like(h_sa)

    @pl.when(t == n_tile - 1)
    def _():
        h_fb[...] = jnp.zeros_like(h_fb)
        h_sb[...] = jnp.zeros_like(h_sb)

    barrier = pltpu.get_barrier_semaphore()
    for q in range(n_freq):
        @pl.when(f != q)
        def _():
            pl.semaphore_signal(barrier, 1, device_id=(t, q), device_id_type=MESH)

        @pl.when(has_above)
        def _():
            pl.semaphore_signal(barrier, 1, device_id=(t - 1, q), device_id_type=MESH)

        @pl.when(has_below)
        def _():
            pl.semaphore_signal(barrier, 1, device_id=(t + 1, q), device_id_type=MESH)

    expected = (n_freq - 1) + n_freq * has_above.astype(jnp.int32) + n_freq * has_below.astype(jnp.int32)

    for copy in loads:
        copy.wait()

    own_rows = lax.broadcasted_iota(jnp.int32, (own, ncol), 0)
    own_forward = pltpu.roll(own_rows, 1, 0) == (own_rows + own - 1) % own
    lift = (own + HALO - ap) % own
    drop = ap - HALO

    def last_rows(x, forward):
        return jnp.where(forward, pltpu.roll(x, lift, 0), pltpu.roll(x, drop, 0))[:HALO]

    s_up[...] = last_rows(g_slow[f, 0], own_forward[:, :block])
    fields_v = (src_v, rec_v)
    for fi in range(nfl):
        for x in range(2):
            for c in range(nc):
                up_buf[x, c, fi] = last_rows(fields_v[x][c, fi], own_forward)

    pl.semaphore_wait(barrier, expected)

    def remote(src, dst, slot_send, slot_recv, device):
        return pltpu.make_async_remote_copy(
            src_ref=src, dst_ref=dst, send_sem=send_sem.at[slot_send], recv_sem=recv_sem.at[slot_recv],
            device_id=device, device_id_type=MESH,
        )

    f_lo = (src_hbm.at[:, :, pl.ds(0, HALO), :], rec_hbm.at[:, :, pl.ds(0, HALO), :])
    s_lo = slow_hbm.at[0, pl.ds(0, HALO), :]
    for q in range(n_freq):
        @pl.when(f != q)
        def _():
            remote(slow_hbm, g_slow.at[f], q, f, (t, q)).start()

        @pl.when(has_above)
        def _():
            remote(s_lo, h_sb.at[f], 2 * n_freq + q, 2 * n_freq + f, (t - 1, q)).start()

    field_base = 3 * n_freq

    def lower_copy(x, fi, device):
        return remote(f_lo[x].at[:, fi], h_fb.at[x, :, fi], field_base + 2 + 2 * x + fi,
                      field_base + 2 + 2 * x + fi, device)

    def upper_copy(fi, device):
        return remote(up_buf.at[:, :, fi], h_fa.at[:, :, fi], field_base + fi, field_base + fi, device)

    for fi in range(2):
        @pl.when(has_above)
        def _():
            for x in range(2):
                lower_copy(x, fi, (t - 1, f)).start()

    for q in range(n_freq):
        @pl.when(has_below)
        def _():
            remote(s_up, h_sa.at[f], n_freq + q, n_freq + f, (t + 1, q)).start()

    for fi in range(nfl):
        @pl.when(has_below)
        def _():
            upper_copy(fi, (t + 1, f)).start()

    for q in range(n_freq):
        @pl.when(f != q)
        def _():
            remote(slow_hbm, g_slow.at[q], q, q, (t, q)).wait_send()
            remote(slow_hbm, g_slow.at[q], q, q, (t, q)).wait_recv()

        @pl.when(has_below)
        def _():
            remote(s_up, h_sa.at[q], n_freq + q, n_freq + q, (t + 1, q)).wait_send()
            remote(s_lo, h_sb.at[q], 2 * n_freq + q, 2 * n_freq + q, (t + 1, q)).wait_recv()

        @pl.when(has_above)
        def _():
            remote(s_lo, h_sb.at[q], 2 * n_freq + q, 2 * n_freq + q, (t - 1, q)).wait_send()
            remote(s_up, h_sa.at[q], n_freq + q, n_freq + q, (t - 1, q)).wait_recv()

    def await_fields(fi):
        @pl.when(has_below)
        def _():
            upper_copy(fi, (t + 1, f)).wait_send()
            for x in range(2):
                lower_copy(x, fi, (t + 1, f)).wait_recv()

        @pl.when(has_above)
        def _():
            for x in range(2):
                lower_copy(x, fi, (t - 1, f)).wait_send()
            upper_copy(fi, (t - 1, f)).wait_recv()

    rows = lax.broadcasted_iota(jnp.int32, (ext_rows, ncol), 0)
    cols = lax.broadcasted_iota(jnp.int32, (ext_rows, ncol), 1)
    left_ok = jnp.abs(pltpu.roll(cols, 1, 1) - cols) == 1
    right_ok = jnp.abs(pltpu.roll(cols, ncol - 1, 1) - cols) == 1
    forward = pltpu.roll(rows, 1, 0) == (rows + ext_rows - 1) % ext_rows
    lower_start = HALO + ap
    top_part = rows < lower_start

    def in_band(lo, hi):
        return (rows >= lo) & (rows < hi)

    valid0 = (in_band(0, HALO) & has_above) | in_band(HALO, lower_start) | (
        in_band(lower_start, lower_start + HALO) & has_below)
    reach = HALO // 2
    valid1 = (in_band(HALO - reach, HALO) & has_above) | in_band(HALO, lower_start) | (
        in_band(lower_start, lower_start + reach) & has_below)
    live = lax.broadcasted_iota(jnp.int32, (own, ncol), 0) < ap
    zeros_tail = jnp.zeros((ext_rows - HALO, ncol), jnp.float32)

    def place_lower(lower8):
        padded = jnp.concatenate([lower8, zeros_tail], axis=0)
        ahead = pltpu.roll(padded, lower_start, 0)
        behind = pltpu.roll(padded, ext_rows - lower_start, 0)
        return jnp.where(forward, ahead, behind)

    def joined(upper8, own_rows, lower8):
        top = jnp.concatenate([upper8, own_rows, jnp.zeros((HALO, ncol), jnp.float32)], axis=0)
        return jnp.where(top_part, top, place_lower(lower8))

    def columns_of(pieces):
        return jnp.concatenate(pieces, axis=1)

    slow0 = joined(
        columns_of([h_sa[q] for q in range(n_freq)]),
        columns_of([g_slow[q, 0] for q in range(n_freq)]),
        columns_of([h_sb[q] for q in range(n_freq)]),
    )
    slow0 = jnp.where(valid0, slow0, 0.0)
    slow1 = columns_of([g_slow[q, 1] for q in range(n_freq)])

    def coefficient_of(depth, fi, n, wavenumber):
        coef_re = coeffs[0, n, POWERS - 1] + 0.0 * wavenumber
        coef_im = coeffs[1, n, POWERS - 1] + 0.0 * wavenumber
        for m in range(POWERS - 2, -1, -1):
            coef_re = coef_re * wavenumber + coeffs[0, n, m]
            coef_im = coef_im * wavenumber + coeffs[1, n, m]
        active = (orders[depth, fi] >= n).astype(jnp.float32)
        return coef_re * active, coef_im * active

    for fi in range(nfl):
        for n in range(ORDER + 1):
            cf0[fi, n, 0], cf0[fi, n, 1] = coefficient_of(0, fi, n, frequency[fi] * slow0)
            cf1[fi, n, 0], cf1[fi, n, 1] = coefficient_of(1, fi, n, frequency[fi] * slow1)

    def coefficient(depth, fi, n, wavenumber):
        table = cf0 if depth == 0 else cf1
        return table[fi, n, 0], table[fi, n, 1]

    lane = lax.broadcasted_iota(jnp.int32, (8, ncol), 1)
    left8 = jnp.abs(pltpu.roll(lane, 1, 1) - lane) == 1
    right8 = jnp.abs(pltpu.roll(lane, ncol - 1, 1) - lane) == 1
    tiles = ext_rows // 8
    vmask[0] = jnp.where(valid0, 1.0, 0.0)
    vmask[1] = jnp.where(valid1, 1.0, 0.0)
    pad_zeros = jnp.zeros((PAD, ncol), jnp.float32)
    for slot in range(3):
        for p in range(4):
            tb[slot, p, 0:PAD] = pad_zeros
            tb[slot, p, PAD + ext_rows:PAD + ext_rows + PAD] = pad_zeros

    def step_tile(depth, n, p, rt):
        cur, prev, slot = (n - 1) % 3, (n - 2) % 3, n % 3
        base = PAD + 8 * rt
        v = tb[cur, p, base:base + 8]
        pair = tb[cur, p, pl.ds(base - 1, 8)] + tb[cur, p, pl.ds(base + 1, 8)]
        blur = 0.25 * pair + 0.5 * v
        side = jnp.where(left8, pltpu.roll(blur, 1, 1), 0.0) + jnp.where(
            right8, pltpu.roll(blur, ncol - 1, 1), 0.0)
        if n == 1:
            g = 0.5 * side + blur - v
        else:
            g = side + 0.5 * pair - v - tb[prev, p, base:base + 8]
        g = g * vmask[depth, 8 * rt:8 * rt + 8]
        tb[slot, p, base:base + 8] = g
        return g

    def extrapolate(depth, fi, acc_tiles, write):
        table = cf0 if depth == 0 else cf1
        for n in range(ORDER + 1):
            slot = n % 3
            for rt in range(tiles):
                for x in range(2):
                    if n >= 1:
                        t_re = step_tile(depth, n, 2 * x, rt)
                        t_im = step_tile(depth, n, 2 * x + 1, rt)
                    else:
                        t_re = tb[slot, 2 * x, PAD + 8 * rt:PAD + 8 * rt + 8]
                        t_im = tb[slot, 2 * x + 1, PAD + 8 * rt:PAD + 8 * rt + 8]
                    if rt not in acc_tiles:
                        continue
                    row0 = 8 * (rt - acc_tiles[0])
                    coef_re = table[fi, n, 0, row0:row0 + 8]
                    coef_im = table[fi, n, 1, row0:row0 + 8]
                    if x == 0:
                        terms = (coef_re * t_re + coef_im * t_im, coef_re * t_im - coef_im * t_re)
                    else:
                        terms = (coef_re * t_re - coef_im * t_im, coef_re * t_im + coef_im * t_re)
                    write(n, x, row0, terms)

    fields = (src_v, rec_v)
    for fi in range(nfl):
        await_fields(fi)
        for p in range(4):
            x, c = p // 2, p % 2
            tb[0, p, PAD:PAD + ext_rows] = jnp.where(
                valid0, joined(h_fa[x, c, fi], fields[x][c, fi], h_fb[x, c, fi]), 0.0)

        def write0(n, x, row0, terms, fi=fi):
            for c in range(2):
                if n == 0:
                    s1[x, c, fi, row0:row0 + 8] = terms[c]
                else:
                    s1[x, c, fi, row0:row0 + 8] = s1[x, c, fi, row0:row0 + 8] + terms[c]

        extrapolate(0, fi, tuple(range(tiles)), write0)
        for p in range(4):
            s1[p // 2, p % 2, fi] = jnp.where(valid1, s1[p // 2, p % 2, fi], 0.0)
        mid = slice(HALO, HALO + own)
        term = s1[0, 0, fi, mid, :] * s1[1, 0, fi, mid, :] + s1[0, 1, fi, mid, :] * s1[1, 1, fi, mid, :]
        term = jnp.where(live, term, 0.0)
        if fi == 0:
            img_out[0] = term
        else:
            img_out[0] = img_out[0] + term

    image_base = 3 * n_freq + 6

    def image_copy(depth, q, slot_recv, device):
        return pltpu.make_async_remote_copy(
            src_ref=img_out.at[depth, :, pl.ds(q * block, block)], dst_ref=got.at[slot_recv, depth],
            send_sem=send_sem.at[image_base + depth * n_freq + q],
            recv_sem=recv_sem.at[image_base + depth * n_freq + slot_recv],
            device_id=device, device_id_type=MESH,
        )

    def send_image(depth):
        for q in range(n_freq):
            @pl.when(f != q)
            def _():
                image_copy(depth, q, f, (t, q)).start()

    send_image(0)

    for fi in range(nfl):
        for p in range(4):
            tb[0, p, PAD:PAD + ext_rows] = s1[p // 2, p % 2, fi]

        def write1(n, x, row0, terms):
            for c in range(2):
                if n == 0:
                    acc1[2 * x + c, row0:row0 + 8] = terms[c]
                else:
                    acc1[2 * x + c, row0:row0 + 8] = acc1[2 * x + c, row0:row0 + 8] + terms[c]

        extrapolate(1, fi, tuple(range(HALO // 8, (HALO + own) // 8)), write1)
        result = [jnp.where(live, acc1[p], 0.0) for p in range(4)]
        rec_out[0, fi] = result[2]
        rec_out[1, fi] = result[3]
        term = result[0] * result[2] + result[1] * result[3]
        if fi == 0:
            img_out[1] = term
        else:
            img_out[1] = img_out[1] + term

    send_image(1)
    for depth in range(NDEPTH):
        for q in range(n_freq):
            @pl.when(f != q)
            def _():
                image_copy(depth, q, q, (t, q)).wait_send()
                image_copy(depth, q, q, (t, q)).wait_recv()

    total = None
    for q in range(n_freq):
        mine = img_out[:, :, q * block:(q + 1) * block]
        part = jnp.where(f == q, mine, got[q])
        total = part if total is None else total + part
    image_out[...] = total


def shards(n_tile, n_freq, source_field, receiver_field, slowness, frequency, order_table, filter_coeffs, aperture):
    nc, nfl, own, ncol = source_field.shape
    block = slowness.shape[2]
    ext_rows = own + 2 * HALO
    elements = nc * nfl * 2 * ext_rows * ncol * NDEPTH
    rec_out, image_out = pl.pallas_call(
        functools.partial(migrate_kernel, n_tile, n_freq),
        out_shape=(
            jax.ShapeDtypeStruct((nc, nfl, own, ncol), jnp.float32),
            jax.ShapeDtypeStruct((NDEPTH, own, block), jnp.float32),
        ),
        in_specs=[pl.BlockSpec(memory_space=SMEM)] * 3 + [pl.BlockSpec(memory_space=pl.ANY)] * 4,
        out_specs=(pl.BlockSpec(memory_space=VMEM), pl.BlockSpec(memory_space=VMEM)),
        scratch_shapes=[
            pltpu.VMEM((nc, nfl, own, ncol), jnp.float32),
            pltpu.VMEM((nc, nfl, own, ncol), jnp.float32),
            pltpu.VMEM((n_freq, NDEPTH, own, block), jnp.float32),
            pltpu.VMEM((n_freq, HALO, block), jnp.float32),
            pltpu.VMEM((n_freq, HALO, block), jnp.float32),
            pltpu.VMEM((2, nc, nfl, HALO, ncol), jnp.float32),
            pltpu.VMEM((2, nc, nfl, HALO, ncol), jnp.float32),
            pltpu.VMEM((2, nc, nfl, HALO, ncol), jnp.float32),
            pltpu.VMEM((HALO, block), jnp.float32),
            pltpu.VMEM((2, nc, nfl, ext_rows, ncol), jnp.float32),
            pltpu.VMEM((3, 4, ext_rows + 2 * PAD, ncol), jnp.float32),
            pltpu.VMEM((NDEPTH, own, ncol), jnp.float32),
            pltpu.VMEM((n_freq, NDEPTH, own, block), jnp.float32),
            pltpu.SMEM(filter_coeffs.shape, jnp.float32),
            pltpu.VMEM((nfl, ORDER + 1, 2, ext_rows, ncol), jnp.float32),
            pltpu.VMEM((nfl, ORDER + 1, 2, own, ncol), jnp.float32),
            pltpu.VMEM((2, ext_rows, ncol), jnp.float32),
            pltpu.VMEM((4, own, ncol), jnp.float32),
            pltpu.SemaphoreType.DMA((4,)),
            pltpu.SemaphoreType.DMA((3 * n_freq + 6 + NDEPTH * n_freq,)),
            pltpu.SemaphoreType.DMA((3 * n_freq + 6 + NDEPTH * n_freq,)),
        ],
        compiler_params=pltpu.CompilerParams(collective_id=0, has_side_effects=True),
        cost_estimate=pl.CostEstimate(flops=elements * 100, bytes_accessed=elements * 4, transcendentals=0),
    )(aperture, order_table, frequency, filter_coeffs, source_field, receiver_field, slowness)
    return (image_out, rec_out)


def solution(mesh):
    placed = (
        P(None, "freq", "tile", None),
        P(None, "freq", "tile", None),
        P(None, "tile", "freq"),
        P("freq"),
        P(None, "freq"),
        P(),
        P(),
    )
    return jax.shard_map(
        functools.partial(shards, mesh.shape["tile"], mesh.shape["freq"]),
        mesh=mesh,
        in_specs=placed,
        out_specs=(P(None, "tile", "freq"), P(None, "freq", "tile", None)),
        check_vma=False,
    )
```

```python
import functools

import jax
import jax.numpy as jnp
from jax import lax
from jax.experimental import pallas as pl
from jax.experimental.pallas import tpu as pltpu
from jax.sharding import PartitionSpec as P

ORDER = 4
NDEPTH = 2
POWERS = 3
HALO = 8
MESH = pl.DeviceIdType.MESH
VMEM = pltpu.MemorySpace.VMEM
SMEM = pltpu.MemorySpace.SMEM


def migrate_kernel(n_tile, n_freq, aperture, orders, frequency, coeffs_hbm, src_hbm, rec_hbm, slow_hbm,
                   rec_out, image_out, src_v, rec_v, g_slow, h_sa, h_sb, h_fa, h_fb, up_buf, s_up, s1, tb, img_out,
                   got, coeffs, cf0, cf1, local_sem, send_sem, recv_sem):
    t = lax.axis_index("tile")
    f = lax.axis_index("freq")
    nc, nfl, own, ncol = src_v.shape
    ext_rows = HALO + own + HALO
    block = slow_hbm.shape[2]
    ap = aperture[t]
    has_above = t > 0
    has_below = t < n_tile - 1

    loads = (
        pltpu.make_async_copy(src_hbm, src_v, local_sem.at[0]),
        pltpu.make_async_copy(rec_hbm, rec_v, local_sem.at[1]),
        pltpu.make_async_copy(slow_hbm, g_slow.at[f], local_sem.at[2]),
        pltpu.make_async_copy(coeffs_hbm, coeffs, local_sem.at[3]),
    )
    for copy in loads:
        copy.start()

    @pl.when(t == 0)
    def _():
        h_fa[...] = jnp.zeros_like(h_fa)
        h_sa[...] = jnp.zeros_like(h_sa)

    @pl.when(t == n_tile - 1)
    def _():
        h_fb[...] = jnp.zeros_like(h_fb)
        h_sb[...] = jnp.zeros_like(h_sb)

    barrier = pltpu.get_barrier_semaphore()
    for q in range(n_freq):
        @pl.when(f != q)
        def _():
            pl.semaphore_signal(barrier, 1, device_id=(t, q), device_id_type=MESH)

        @pl.when(has_above)
        def _():
            pl.semaphore_signal(barrier, 1, device_id=(t - 1, q), device_id_type=MESH)

        @pl.when(has_below)
        def _():
            pl.semaphore_signal(barrier, 1, device_id=(t + 1, q), device_id_type=MESH)

    expected = (n_freq - 1) + n_freq * has_above.astype(jnp.int32) + n_freq * has_below.astype(jnp.int32)

    for copy in loads:
        copy.wait()

    own_rows = lax.broadcasted_iota(jnp.int32, (own, ncol), 0)
    own_forward = pltpu.roll(own_rows, 1, 0) == (own_rows + own - 1) % own
    lift = (own + HALO - ap) % own
    drop = ap - HALO

    def last_rows(x, forward):
        return jnp.where(forward, pltpu.roll(x, lift, 0), pltpu.roll(x, drop, 0))[:HALO]

    s_up[...] = last_rows(g_slow[f, 0], own_forward[:, :block])
    fields_v = (src_v, rec_v)
    for fi in range(nfl):
        for x in range(2):
            for c in range(nc):
                up_buf[x, c, fi] = last_rows(fields_v[x][c, fi], own_forward)

    pl.semaphore_wait(barrier, expected)

    def remote(src, dst, slot_send, slot_recv, device):
        return pltpu.make_async_remote_copy(
            src_ref=src, dst_ref=dst, send_sem=send_sem.at[slot_send], recv_sem=recv_sem.at[slot_recv],
            device_id=device, device_id_type=MESH,
        )

    f_lo = (src_hbm.at[:, :, pl.ds(0, HALO), :], rec_hbm.at[:, :, pl.ds(0, HALO), :])
    s_lo = slow_hbm.at[0, pl.ds(0, HALO), :]
    for q in range(n_freq):
        @pl.when(f != q)
        def _():
            remote(slow_hbm, g_slow.at[f], q, f, (t, q)).start()

        @pl.when(has_above)
        def _():
            remote(s_lo, h_sb.at[f], 2 * n_freq + q, 2 * n_freq + f, (t - 1, q)).start()

    field_base = 3 * n_freq

    def lower_copy(x, fi, device):
        return remote(f_lo[x].at[:, fi], h_fb.at[x, :, fi], field_base + 2 + 2 * x + fi,
                      field_base + 2 + 2 * x + fi, device)

    def upper_copy(fi, device):
        return remote(up_buf.at[:, :, fi], h_fa.at[:, :, fi], field_base + fi, field_base + fi, device)

    for fi in range(2):
        @pl.when(has_above)
        def _():
            for x in range(2):
                lower_copy(x, fi, (t - 1, f)).start()

    for q in range(n_freq):
        @pl.when(has_below)
        def _():
            remote(s_up, h_sa.at[f], n_freq + q, n_freq + f, (t + 1, q)).start()

    for fi in range(nfl):
        @pl.when(has_below)
        def _():
            upper_copy(fi, (t + 1, f)).start()

    for q in range(n_freq):
        @pl.when(f != q)
        def _():
            remote(slow_hbm, g_slow.at[q], q, q, (t, q)).wait_send()
            remote(slow_hbm, g_slow.at[q], q, q, (t, q)).wait_recv()

        @pl.when(has_below)
        def _():
            remote(s_up, h_sa.at[q], n_freq + q, n_freq + q, (t + 1, q)).wait_send()
            remote(s_lo, h_sb.at[q], 2 * n_freq + q, 2 * n_freq + q, (t + 1, q)).wait_recv()

        @pl.when(has_above)
        def _():
            remote(s_lo, h_sb.at[q], 2 * n_freq + q, 2 * n_freq + q, (t - 1, q)).wait_send()
            remote(s_up, h_sa.at[q], n_freq + q, n_freq + q, (t - 1, q)).wait_recv()

    def await_fields(fi):
        @pl.when(has_below)
        def _():
            upper_copy(fi, (t + 1, f)).wait_send()
            for x in range(2):
                lower_copy(x, fi, (t + 1, f)).wait_recv()

        @pl.when(has_above)
        def _():
            for x in range(2):
                lower_copy(x, fi, (t - 1, f)).wait_send()
            upper_copy(fi, (t - 1, f)).wait_recv()

    rows = lax.broadcasted_iota(jnp.int32, (ext_rows, ncol), 0)
    cols = lax.broadcasted_iota(jnp.int32, (ext_rows, ncol), 1)
    left_ok = jnp.abs(pltpu.roll(cols, 1, 1) - cols) == 1
    right_ok = jnp.abs(pltpu.roll(cols, ncol - 1, 1) - cols) == 1
    forward = pltpu.roll(rows, 1, 0) == (rows + ext_rows - 1) % ext_rows
    lower_start = HALO + ap
    top_part = rows < lower_start

    def in_band(lo, hi):
        return (rows >= lo) & (rows < hi)

    valid0 = (in_band(0, HALO) & has_above) | in_band(HALO, lower_start) | (
        in_band(lower_start, lower_start + HALO) & has_below)
    reach = HALO // 2
    valid1 = (in_band(HALO - reach, HALO) & has_above) | in_band(HALO, lower_start) | (
        in_band(lower_start, lower_start + reach) & has_below)
    live = lax.broadcasted_iota(jnp.int32, (own, ncol), 0) < ap
    zeros_tail = jnp.zeros((ext_rows - HALO, ncol), jnp.float32)

    def place_lower(lower8):
        padded = jnp.concatenate([lower8, zeros_tail], axis=0)
        ahead = pltpu.roll(padded, lower_start, 0)
        behind = pltpu.roll(padded, ext_rows - lower_start, 0)
        return jnp.where(forward, ahead, behind)

    def joined(upper8, own_rows, lower8):
        top = jnp.concatenate([upper8, own_rows, jnp.zeros((HALO, ncol), jnp.float32)], axis=0)
        return jnp.where(top_part, top, place_lower(lower8))

    def columns_of(pieces):
        return jnp.concatenate(pieces, axis=1)

    slow0 = joined(
        columns_of([h_sa[q] for q in range(n_freq)]),
        columns_of([g_slow[q, 0] for q in range(n_freq)]),
        columns_of([h_sb[q] for q in range(n_freq)]),
    )
    slow0 = jnp.where(valid0, slow0, 0.0)
    slow1 = columns_of([g_slow[q, 1] for q in range(n_freq)])

    edge = 128

    def masked_side(b):
        ahead = pltpu.roll(b, 1, 1)
        behind = pltpu.roll(b, ncol - 1, 1)

        def guarded(lo, hi):
            return jnp.where(left_ok[:, lo:hi], ahead[:, lo:hi], 0.0) + jnp.where(
                right_ok[:, lo:hi], behind[:, lo:hi], 0.0)

        middle = ahead[:, edge:ncol - edge] + behind[:, edge:ncol - edge]
        return jnp.concatenate([guarded(0, edge), middle, guarded(ncol - edge, ncol)], axis=1)

    def chebyshev_step(v, prev):
        pair = pltpu.roll(v, 1, 0) + pltpu.roll(v, ext_rows - 1, 0)
        blur = 0.25 * pair + 0.5 * v
        side = masked_side(blur)
        if prev is None:
            return 0.5 * side + blur - v
        return side + 0.5 * pair - v - prev

    def coefficient_of(depth, fi, n, wavenumber):
        coef_re = coeffs[0, n, POWERS - 1] + 0.0 * wavenumber
        coef_im = coeffs[1, n, POWERS - 1] + 0.0 * wavenumber
        for m in range(POWERS - 2, -1, -1):
            coef_re = coef_re * wavenumber + coeffs[0, n, m]
            coef_im = coef_im * wavenumber + coeffs[1, n, m]
        active = (orders[depth, fi] >= n).astype(jnp.float32)
        return coef_re * active, coef_im * active

    for fi in range(nfl):
        for n in range(ORDER + 1):
            cf0[fi, n, 0], cf0[fi, n, 1] = coefficient_of(0, fi, n, frequency[fi] * slow0)
            cf1[fi, n, 0], cf1[fi, n, 1] = coefficient_of(1, fi, n, frequency[fi] * slow1)

    def coefficient(depth, fi, n, wavenumber):
        table = cf0 if depth == 0 else cf1
        return table[fi, n, 0], table[fi, n, 1]

    def extrapolate(depth, fi, wavenumber, valid, lo, hi, write):
        for n in range(ORDER + 1):
            slot = n % 3
            if n >= 1:
                cur, prev = (n - 1) % 3, (n - 2) % 3
                for p in range(4):
                    g = chebyshev_step(tb[cur, p], tb[prev, p] if n > 1 else None)
                    tb[slot, p] = jnp.where(valid, g, 0.0)
            coef_re, coef_im = coefficient(depth, fi, n, wavenumber)
            s_re = tb[slot, 0, lo:hi, :]
            s_im = tb[slot, 1, lo:hi, :]
            r_re = tb[slot, 2, lo:hi, :]
            r_im = tb[slot, 3, lo:hi, :]
            terms = (
                coef_re * s_re + coef_im * s_im,
                coef_re * s_im - coef_im * s_re,
                coef_re * r_re - coef_im * r_im,
                coef_re * r_im + coef_im * r_re,
            )
            write(n, terms)

    fields = (src_v, rec_v)
    for fi in range(nfl):
        await_fields(fi)
        for p in range(4):
            x, c = p // 2, p % 2
            tb[0, p] = jnp.where(valid0, joined(h_fa[x, c, fi], fields[x][c, fi], h_fb[x, c, fi]), 0.0)

        def write0(n, terms, fi=fi):
            for p in range(4):
                if n == 0:
                    s1[p // 2, p % 2, fi] = terms[p]
                else:
                    s1[p // 2, p % 2, fi] = s1[p // 2, p % 2, fi] + terms[p]

        extrapolate(0, fi, frequency[fi] * slow0, valid0, 0, ext_rows, write0)
        for p in range(4):
            s1[p // 2, p % 2, fi] = jnp.where(valid1, s1[p // 2, p % 2, fi], 0.0)
        mid = slice(HALO, HALO + own)
        term = s1[0, 0, fi, mid, :] * s1[1, 0, fi, mid, :] + s1[0, 1, fi, mid, :] * s1[1, 1, fi, mid, :]
        term = jnp.where(live, term, 0.0)
        if fi == 0:
            img_out[0] = term
        else:
            img_out[0] = img_out[0] + term

    image_base = 3 * n_freq + 6

    def image_copy(depth, q, slot_recv, device):
        return pltpu.make_async_remote_copy(
            src_ref=img_out.at[depth, :, pl.ds(q * block, block)], dst_ref=got.at[slot_recv, depth],
            send_sem=send_sem.at[image_base + depth * n_freq + q],
            recv_sem=recv_sem.at[image_base + depth * n_freq + slot_recv],
            device_id=device, device_id_type=MESH,
        )

    def send_image(depth):
        for q in range(n_freq):
            @pl.when(f != q)
            def _():
                image_copy(depth, q, f, (t, q)).start()

    send_image(0)

    for fi in range(nfl):
        for p in range(4):
            tb[0, p] = s1[p // 2, p % 2, fi]
        acc = {}

        def write1(n, terms, acc=acc):
            for p in range(4):
                acc[p] = terms[p] if n == 0 else acc[p] + terms[p]

        extrapolate(1, fi, frequency[fi] * slow1, valid1, HALO, HALO + own, write1)
        result = [jnp.where(live, acc[p], 0.0) for p in range(4)]
        rec_out[0, fi] = result[2]
        rec_out[1, fi] = result[3]
        term = result[0] * result[2] + result[1] * result[3]
        if fi == 0:
            img_out[1] = term
        else:
            img_out[1] = img_out[1] + term

    send_image(1)
    for depth in range(NDEPTH):
        for q in range(n_freq):
            @pl.when(f != q)
            def _():
                image_copy(depth, q, q, (t, q)).wait_send()
                image_copy(depth, q, q, (t, q)).wait_recv()

    total = None
    for q in range(n_freq):
        mine = img_out[:, :, q * block:(q + 1) * block]
        part = jnp.where(f == q, mine, got[q])
        total = part if total is None else total + part
    image_out[...] = total


def shards(n_tile, n_freq, source_field, receiver_field, slowness, frequency, order_table, filter_coeffs, aperture):
    nc, nfl, own, ncol = source_field.shape
    block = slowness.shape[2]
    ext_rows = own + 2 * HALO
    elements = nc * nfl * 2 * ext_rows * ncol * NDEPTH
    rec_out, image_out = pl.pallas_call(
        functools.partial(migrate_kernel, n_tile, n_freq),
        out_shape=(
            jax.ShapeDtypeStruct((nc, nfl, own, ncol), jnp.float32),
            jax.ShapeDtypeStruct((NDEPTH, own, block), jnp.float32),
        ),
        in_specs=[pl.BlockSpec(memory_space=SMEM)] * 3 + [pl.BlockSpec(memory_space=pl.ANY)] * 4,
        out_specs=(pl.BlockSpec(memory_space=VMEM), pl.BlockSpec(memory_space=VMEM)),
        scratch_shapes=[
            pltpu.VMEM((nc, nfl, own, ncol), jnp.float32),
            pltpu.VMEM((nc, nfl, own, ncol), jnp.float32),
            pltpu.VMEM((n_freq, NDEPTH, own, block), jnp.float32),
            pltpu.VMEM((n_freq, HALO, block), jnp.float32),
            pltpu.VMEM((n_freq, HALO, block), jnp.float32),
            pltpu.VMEM((2, nc, nfl, HALO, ncol), jnp.float32),
            pltpu.VMEM((2, nc, nfl, HALO, ncol), jnp.float32),
            pltpu.VMEM((2, nc, nfl, HALO, ncol), jnp.float32),
            pltpu.VMEM((HALO, block), jnp.float32),
            pltpu.VMEM((2, nc, nfl, ext_rows, ncol), jnp.float32),
            pltpu.VMEM((3, 4, ext_rows, ncol), jnp.float32),
            pltpu.VMEM((NDEPTH, own, ncol), jnp.float32),
            pltpu.VMEM((n_freq, NDEPTH, own, block), jnp.float32),
            pltpu.SMEM(filter_coeffs.shape, jnp.float32),
            pltpu.VMEM((nfl, ORDER + 1, 2, ext_rows, ncol), jnp.float32),
            pltpu.VMEM((nfl, ORDER + 1, 2, own, ncol), jnp.float32),
            pltpu.SemaphoreType.DMA((4,)),
            pltpu.SemaphoreType.DMA((3 * n_freq + 6 + NDEPTH * n_freq,)),
            pltpu.SemaphoreType.DMA((3 * n_freq + 6 + NDEPTH * n_freq,)),
        ],
        compiler_params=pltpu.CompilerParams(collective_id=0, has_side_effects=True),
        cost_estimate=pl.CostEstimate(flops=elements * 100, bytes_accessed=elements * 4, transcendentals=0),
    )(aperture, order_table, frequency, filter_coeffs, source_field, receiver_field, slowness)
    return (image_out, rec_out)


def solution(mesh):
    placed = (
        P(None, "freq", "tile", None),
        P(None, "freq", "tile", None),
        P(None, "tile", "freq"),
        P("freq"),
        P(None, "freq"),
        P(),
        P(),
    )
    return jax.shard_map(
        functools.partial(shards, mesh.shape["tile"], mesh.shape["freq"]),
        mesh=mesh,
        in_specs=placed,
        out_specs=(P(None, "tile", "freq"), P(None, "freq", "tile", None)),
        check_vma=False,
    )
```

```python
import functools

import jax
import jax.numpy as jnp
from jax import lax
from jax.experimental import pallas as pl
from jax.experimental.pallas import tpu as pltpu
from jax.sharding import PartitionSpec as P

ORDER = 4
NDEPTH = 2
POWERS = 3
HALO = 8
MESH = pl.DeviceIdType.MESH
VMEM = pltpu.MemorySpace.VMEM
SMEM = pltpu.MemorySpace.SMEM


def migrate_kernel(n_tile, n_freq, aperture, orders, frequency, coeffs_hbm, src_hbm, rec_hbm, slow_hbm,
                   rec_out, image_out, src_v, rec_v, g_slow, h_sa, h_sb, h_fa, h_fb, up_buf, s_up, s1, tb, img_out,
                   got, coeffs, cf0, cf1, local_sem, send_sem, recv_sem):
    t = lax.axis_index("tile")
    f = lax.axis_index("freq")
    nc, nfl, own, ncol = src_v.shape
    ext_rows = HALO + own + HALO
    block = slow_hbm.shape[2]
    ap = aperture[t]
    has_above = t > 0
    has_below = t < n_tile - 1

    loads = (
        pltpu.make_async_copy(src_hbm, src_v, local_sem.at[0]),
        pltpu.make_async_copy(rec_hbm, rec_v, local_sem.at[1]),
        pltpu.make_async_copy(slow_hbm, g_slow.at[f], local_sem.at[2]),
        pltpu.make_async_copy(coeffs_hbm, coeffs, local_sem.at[3]),
    )
    for copy in loads:
        copy.start()

    @pl.when(t == 0)
    def _():
        h_fa[...] = jnp.zeros_like(h_fa)
        h_sa[...] = jnp.zeros_like(h_sa)

    @pl.when(t == n_tile - 1)
    def _():
        h_fb[...] = jnp.zeros_like(h_fb)
        h_sb[...] = jnp.zeros_like(h_sb)

    barrier = pltpu.get_barrier_semaphore()
    for q in range(n_freq):
        @pl.when(f != q)
        def _():
            pl.semaphore_signal(barrier, 1, device_id=(t, q), device_id_type=MESH)

        @pl.when(has_above)
        def _():
            pl.semaphore_signal(barrier, 1, device_id=(t - 1, q), device_id_type=MESH)

        @pl.when(has_below)
        def _():
            pl.semaphore_signal(barrier, 1, device_id=(t + 1, q), device_id_type=MESH)

    expected = (n_freq - 1) + n_freq * has_above.astype(jnp.int32) + n_freq * has_below.astype(jnp.int32)

    for copy in loads:
        copy.wait()

    own_rows = lax.broadcasted_iota(jnp.int32, (own, ncol), 0)
    own_forward = pltpu.roll(own_rows, 1, 0) == (own_rows + own - 1) % own
    lift = (own + HALO - ap) % own
    drop = ap - HALO

    def last_rows(x, forward):
        return jnp.where(forward, pltpu.roll(x, lift, 0), pltpu.roll(x, drop, 0))[:HALO]

    s_up[...] = last_rows(g_slow[f, 0], own_forward[:, :block])
    fields_v = (src_v, rec_v)
    for fi in range(nfl):
        for x in range(2):
            for c in range(nc):
                up_buf[x, c, fi] = last_rows(fields_v[x][c, fi], own_forward)

    pl.semaphore_wait(barrier, expected)

    def remote(src, dst, slot_send, slot_recv, device):
        return pltpu.make_async_remote_copy(
            src_ref=src, dst_ref=dst, send_sem=send_sem.at[slot_send], recv_sem=recv_sem.at[slot_recv],
            device_id=device, device_id_type=MESH,
        )

    f_lo = (src_hbm.at[:, :, pl.ds(0, HALO), :], rec_hbm.at[:, :, pl.ds(0, HALO), :])
    s_lo = slow_hbm.at[0, pl.ds(0, HALO), :]
    for q in range(n_freq):
        @pl.when(f != q)
        def _():
            remote(slow_hbm, g_slow.at[f], q, f, (t, q)).start()

        @pl.when(has_above)
        def _():
            remote(s_lo, h_sb.at[f], 2 * n_freq + q, 2 * n_freq + f, (t - 1, q)).start()

    field_base = 3 * n_freq

    def lower_copy(x, fi, device):
        return remote(f_lo[x].at[:, fi], h_fb.at[x, :, fi], field_base + 2 + 2 * x + fi,
                      field_base + 2 + 2 * x + fi, device)

    def upper_copy(fi, device):
        return remote(up_buf.at[:, :, fi], h_fa.at[:, :, fi], field_base + fi, field_base + fi, device)

    for fi in range(2):
        @pl.when(has_above)
        def _():
            for x in range(2):
                lower_copy(x, fi, (t - 1, f)).start()

    for q in range(n_freq):
        @pl.when(has_below)
        def _():
            remote(s_up, h_sa.at[f], n_freq + q, n_freq + f, (t + 1, q)).start()

    for fi in range(nfl):
        @pl.when(has_below)
        def _():
            upper_copy(fi, (t + 1, f)).start()

    for q in range(n_freq):
        @pl.when(f != q)
        def _():
            remote(slow_hbm, g_slow.at[q], q, q, (t, q)).wait_send()
            remote(slow_hbm, g_slow.at[q], q, q, (t, q)).wait_recv()

        @pl.when(has_below)
        def _():
            remote(s_up, h_sa.at[q], n_freq + q, n_freq + q, (t + 1, q)).wait_send()
            remote(s_lo, h_sb.at[q], 2 * n_freq + q, 2 * n_freq + q, (t + 1, q)).wait_recv()

        @pl.when(has_above)
        def _():
            remote(s_lo, h_sb.at[q], 2 * n_freq + q, 2 * n_freq + q, (t - 1, q)).wait_send()
            remote(s_up, h_sa.at[q], n_freq + q, n_freq + q, (t - 1, q)).wait_recv()

    def await_fields(fi):
        @pl.when(has_below)
        def _():
            upper_copy(fi, (t + 1, f)).wait_send()
            for x in range(2):
                lower_copy(x, fi, (t + 1, f)).wait_recv()

        @pl.when(has_above)
        def _():
            for x in range(2):
                lower_copy(x, fi, (t - 1, f)).wait_send()
            upper_copy(fi, (t - 1, f)).wait_recv()

    rows = lax.broadcasted_iota(jnp.int32, (ext_rows, ncol), 0)
    cols = lax.broadcasted_iota(jnp.int32, (ext_rows, ncol), 1)
    left_ok = jnp.abs(pltpu.roll(cols, 1, 1) - cols) == 1
    right_ok = jnp.abs(pltpu.roll(cols, ncol - 1, 1) - cols) == 1
    forward = pltpu.roll(rows, 1, 0) == (rows + ext_rows - 1) % ext_rows
    lower_start = HALO + ap
    top_part = rows < lower_start

    def in_band(lo, hi):
        return (rows >= lo) & (rows < hi)

    valid0 = (in_band(0, HALO) & has_above) | in_band(HALO, lower_start) | (
        in_band(lower_start, lower_start + HALO) & has_below)
    reach = HALO // 2
    valid1 = (in_band(HALO - reach, HALO) & has_above) | in_band(HALO, lower_start) | (
        in_band(lower_start, lower_start + reach) & has_below)
    live = lax.broadcasted_iota(jnp.int32, (own, ncol), 0) < ap
    zeros_tail = jnp.zeros((ext_rows - HALO, ncol), jnp.float32)

    def place_lower(lower8):
        padded = jnp.concatenate([lower8, zeros_tail], axis=0)
        ahead = pltpu.roll(padded, lower_start, 0)
        behind = pltpu.roll(padded, ext_rows - lower_start, 0)
        return jnp.where(forward, ahead, behind)

    def joined(upper8, own_rows, lower8):
        top = jnp.concatenate([upper8, own_rows, jnp.zeros((HALO, ncol), jnp.float32)], axis=0)
        return jnp.where(top_part, top, place_lower(lower8))

    def columns_of(pieces):
        return jnp.concatenate(pieces, axis=1)

    slow0 = joined(
        columns_of([h_sa[q] for q in range(n_freq)]),
        columns_of([g_slow[q, 0] for q in range(n_freq)]),
        columns_of([h_sb[q] for q in range(n_freq)]),
    )
    slow0 = jnp.where(valid0, slow0, 0.0)
    slow1 = columns_of([g_slow[q, 1] for q in range(n_freq)])

    edge = 128

    def masked_side(b):
        ahead = pltpu.roll(b, 1, 1)
        behind = pltpu.roll(b, ncol - 1, 1)

        def guarded(lo, hi):
            return jnp.where(left_ok[:, lo:hi], ahead[:, lo:hi], 0.0) + jnp.where(
                right_ok[:, lo:hi], behind[:, lo:hi], 0.0)

        middle = ahead[:, edge:ncol - edge] + behind[:, edge:ncol - edge]
        return jnp.concatenate([guarded(0, edge), middle, guarded(ncol - edge, ncol)], axis=1)

    def chebyshev_step(v, prev):
        pair = pltpu.roll(v, 1, 0) + pltpu.roll(v, ext_rows - 1, 0)
        blur = 0.25 * pair + 0.5 * v
        side = masked_side(blur)
        if prev is None:
            return 0.5 * side + blur - v
        return side + 0.5 * pair - v - prev

    def coefficient_of(depth, fi, n, wavenumber):
        active = jnp.where(orders[depth, fi] >= n, 1.0, 0.0).astype(jnp.float32)
        scaled = [[coeffs[c, n, m] * active for m in range(POWERS)] for c in range(2)]
        coef_re = scaled[0][POWERS - 1] * wavenumber + scaled[0][POWERS - 2]
        coef_im = scaled[1][POWERS - 1] * wavenumber + scaled[1][POWERS - 2]
        for m in range(POWERS - 3, -1, -1):
            coef_re = coef_re * wavenumber + scaled[0][m]
            coef_im = coef_im * wavenumber + scaled[1][m]
        return coef_re, coef_im

    for fi in range(nfl):
        for n in range(ORDER + 1):
            cf0[fi, n, 0], cf0[fi, n, 1] = coefficient_of(0, fi, n, frequency[fi] * slow0)
            cf1[fi, n, 0], cf1[fi, n, 1] = coefficient_of(1, fi, n, frequency[fi] * slow1)

    def coefficient(depth, fi, n, wavenumber):
        table = cf0 if depth == 0 else cf1
        return table[fi, n, 0], table[fi, n, 1]

    def extrapolate(depth, fi, wavenumber, valid, lo, hi, write):
        for n in range(ORDER + 1):
            slot = n % 3
            if n >= 1:
                cur, prev = (n - 1) % 3, (n - 2) % 3
                for p in range(4):
                    tb[slot, p] = chebyshev_step(tb[cur, p], tb[prev, p] if n > 1 else None)

                @pl.when(jnp.logical_not(has_above & has_below))
                def _():
                    for p in range(4):
                        tb[slot, p] = jnp.where(valid, tb[slot, p], 0.0)
            coef_re, coef_im = coefficient(depth, fi, n, wavenumber)
            s_re = tb[slot, 0, lo:hi, :]
            s_im = tb[slot, 1, lo:hi, :]
            r_re = tb[slot, 2, lo:hi, :]
            r_im = tb[slot, 3, lo:hi, :]
            terms = (
                coef_re * s_re + coef_im * s_im,
                coef_re * s_im - coef_im * s_re,
                coef_re * r_re - coef_im * r_im,
                coef_re * r_im + coef_im * r_re,
            )
            write(n, terms)

    fields = (src_v, rec_v)
    for fi in range(nfl):
        await_fields(fi)
        for p in range(4):
            x, c = p // 2, p % 2
            tb[0, p] = jnp.where(valid0, joined(h_fa[x, c, fi], fields[x][c, fi], h_fb[x, c, fi]), 0.0)

        def write0(n, terms, fi=fi):
            for p in range(4):
                if n == 0:
                    s1[p // 2, p % 2, fi] = terms[p]
                else:
                    s1[p // 2, p % 2, fi] = s1[p // 2, p % 2, fi] + terms[p]

        extrapolate(0, fi, frequency[fi] * slow0, valid0, 0, ext_rows, write0)
        for p in range(4):
            s1[p // 2, p % 2, fi] = jnp.where(valid1, s1[p // 2, p % 2, fi], 0.0)
        mid = slice(HALO, HALO + own)
        term = s1[0, 0, fi, mid, :] * s1[1, 0, fi, mid, :] + s1[0, 1, fi, mid, :] * s1[1, 1, fi, mid, :]
        term = jnp.where(live, term, 0.0)
        if fi == 0:
            img_out[0] = term
        else:
            img_out[0] = img_out[0] + term

    image_base = 3 * n_freq + 6

    def image_copy(depth, q, slot_recv, device):
        return pltpu.make_async_remote_copy(
            src_ref=img_out.at[depth, :, pl.ds(q * block, block)], dst_ref=got.at[slot_recv, depth],
            send_sem=send_sem.at[image_base + depth * n_freq + q],
            recv_sem=recv_sem.at[image_base + depth * n_freq + slot_recv],
            device_id=device, device_id_type=MESH,
        )

    def send_image(depth):
        for q in range(n_freq):
            @pl.when(f != q)
            def _():
                image_copy(depth, q, f, (t, q)).start()

    send_image(0)

    for fi in range(nfl):
        for p in range(4):
            tb[0, p] = s1[p // 2, p % 2, fi]
        acc = {}

        def write1(n, terms, acc=acc):
            for p in range(4):
                acc[p] = terms[p] if n == 0 else acc[p] + terms[p]

        extrapolate(1, fi, frequency[fi] * slow1, valid1, HALO, HALO + own, write1)
        result = [jnp.where(live, acc[p], 0.0) for p in range(4)]
        rec_out[0, fi] = result[2]
        rec_out[1, fi] = result[3]
        term = result[0] * result[2] + result[1] * result[3]
        if fi == 0:
            img_out[1] = term
        else:
            img_out[1] = img_out[1] + term

    send_image(1)
    for depth in range(NDEPTH):
        for q in range(n_freq):
            @pl.when(f != q)
            def _():
                image_copy(depth, q, q, (t, q)).wait_send()
                image_copy(depth, q, q, (t, q)).wait_recv()

    total = None
    for q in range(n_freq):
        mine = img_out[:, :, q * block:(q + 1) * block]
        part = jnp.where(f == q, mine, got[q])
        total = part if total is None else total + part
    image_out[...] = total


def shards(n_tile, n_freq, source_field, receiver_field, slowness, frequency, order_table, filter_coeffs, aperture):
    nc, nfl, own, ncol = source_field.shape
    block = slowness.shape[2]
    ext_rows = own + 2 * HALO
    elements = nc * nfl * 2 * ext_rows * ncol * NDEPTH
    rec_out, image_out = pl.pallas_call(
        functools.partial(migrate_kernel, n_tile, n_freq),
        out_shape=(
            jax.ShapeDtypeStruct((nc, nfl, own, ncol), jnp.float32),
            jax.ShapeDtypeStruct((NDEPTH, own, block), jnp.float32),
        ),
        in_specs=[pl.BlockSpec(memory_space=SMEM)] * 3 + [pl.BlockSpec(memory_space=pl.ANY)] * 4,
        out_specs=(pl.BlockSpec(memory_space=VMEM), pl.BlockSpec(memory_space=VMEM)),
        scratch_shapes=[
            pltpu.VMEM((nc, nfl, own, ncol), jnp.float32),
            pltpu.VMEM((nc, nfl, own, ncol), jnp.float32),
            pltpu.VMEM((n_freq, NDEPTH, own, block), jnp.float32),
            pltpu.VMEM((n_freq, HALO, block), jnp.float32),
            pltpu.VMEM((n_freq, HALO, block), jnp.float32),
            pltpu.VMEM((2, nc, nfl, HALO, ncol), jnp.float32),
            pltpu.VMEM((2, nc, nfl, HALO, ncol), jnp.float32),
            pltpu.VMEM((2, nc, nfl, HALO, ncol), jnp.float32),
            pltpu.VMEM((HALO, block), jnp.float32),
            pltpu.VMEM((2, nc, nfl, ext_rows, ncol), jnp.float32),
            pltpu.VMEM((3, 4, ext_rows, ncol), jnp.float32),
            pltpu.VMEM((NDEPTH, own, ncol), jnp.float32),
            pltpu.VMEM((n_freq, NDEPTH, own, block), jnp.float32),
            pltpu.SMEM(filter_coeffs.shape, jnp.float32),
            pltpu.VMEM((nfl, ORDER + 1, 2, ext_rows, ncol), jnp.float32),
            pltpu.VMEM((nfl, ORDER + 1, 2, own, ncol), jnp.float32),
            pltpu.SemaphoreType.DMA((4,)),
            pltpu.SemaphoreType.DMA((3 * n_freq + 6 + NDEPTH * n_freq,)),
            pltpu.SemaphoreType.DMA((3 * n_freq + 6 + NDEPTH * n_freq,)),
        ],
        compiler_params=pltpu.CompilerParams(collective_id=0, has_side_effects=True),
        cost_estimate=pl.CostEstimate(flops=elements * 100, bytes_accessed=elements * 4, transcendentals=0),
    )(aperture, order_table, frequency, filter_coeffs, source_field, receiver_field, slowness)
    return (image_out, rec_out)


def solution(mesh):
    placed = (
        P(None, "freq", "tile", None),
        P(None, "freq", "tile", None),
        P(None, "tile", "freq"),
        P("freq"),
        P(None, "freq"),
        P(),
        P(),
    )
    return jax.shard_map(
        functools.partial(shards, mesh.shape["tile"], mesh.shape["freq"]),
        mesh=mesh,
        in_specs=placed,
        out_specs=(P(None, "tile", "freq"), P(None, "freq", "tile", None)),
        check_vma=False,
    )
```

```python
import functools

import jax
import jax.numpy as jnp
from jax import lax
from jax.experimental import pallas as pl
from jax.experimental.pallas import tpu as pltpu
from jax.sharding import PartitionSpec as P

ORDER = 4
NDEPTH = 2
POWERS = 3
HALO = 8
MESH = pl.DeviceIdType.MESH
VMEM = pltpu.MemorySpace.VMEM
SMEM = pltpu.MemorySpace.SMEM


def migrate_kernel(n_tile, n_freq, aperture, orders, frequency, coeffs_hbm, src_hbm, rec_hbm, slow_hbm,
                   rec_out, image_out, src_v, rec_v, g_slow, h_sa, h_sb, h_fa, h_fb, up_buf, s_up, s1, tb, img_out,
                   got, coeffs, cf0, cf1, local_sem, send_sem, recv_sem):
    t = lax.axis_index("tile")
    f = lax.axis_index("freq")
    nc, nfl, own, ncol = src_v.shape
    ext_rows = HALO + own + HALO
    block = slow_hbm.shape[2]
    ap = aperture[t]
    has_above = t > 0
    has_below = t < n_tile - 1

    loads = (
        pltpu.make_async_copy(src_hbm, src_v, local_sem.at[0]),
        pltpu.make_async_copy(rec_hbm, rec_v, local_sem.at[1]),
        pltpu.make_async_copy(slow_hbm, g_slow.at[f], local_sem.at[2]),
        pltpu.make_async_copy(coeffs_hbm, coeffs, local_sem.at[3]),
    )
    for copy in loads:
        copy.start()

    @pl.when(t == 0)
    def _():
        h_fa[...] = jnp.zeros_like(h_fa)
        h_sa[...] = jnp.zeros_like(h_sa)

    @pl.when(t == n_tile - 1)
    def _():
        h_fb[...] = jnp.zeros_like(h_fb)
        h_sb[...] = jnp.zeros_like(h_sb)

    barrier = pltpu.get_barrier_semaphore()
    for q in range(n_freq):
        @pl.when(f != q)
        def _():
            pl.semaphore_signal(barrier, 1, device_id=(t, q), device_id_type=MESH)

        @pl.when(has_above)
        def _():
            pl.semaphore_signal(barrier, 1, device_id=(t - 1, q), device_id_type=MESH)

        @pl.when(has_below)
        def _():
            pl.semaphore_signal(barrier, 1, device_id=(t + 1, q), device_id_type=MESH)

    expected = (n_freq - 1) + n_freq * has_above.astype(jnp.int32) + n_freq * has_below.astype(jnp.int32)

    for copy in loads:
        copy.wait()

    own_rows = lax.broadcasted_iota(jnp.int32, (own, ncol), 0)
    own_forward = pltpu.roll(own_rows, 1, 0) == (own_rows + own - 1) % own
    lift = (own + HALO - ap) % own
    drop = ap - HALO

    def last_rows(x, forward):
        return jnp.where(forward, pltpu.roll(x, lift, 0), pltpu.roll(x, drop, 0))[:HALO]

    s_up[...] = last_rows(g_slow[f, 0], own_forward[:, :block])
    fields_v = (src_v, rec_v)
    for fi in range(nfl):
        for x in range(2):
            for c in range(nc):
                up_buf[x, c, fi] = last_rows(fields_v[x][c, fi], own_forward)

    pl.semaphore_wait(barrier, expected)

    def remote(src, dst, slot_send, slot_recv, device):
        return pltpu.make_async_remote_copy(
            src_ref=src, dst_ref=dst, send_sem=send_sem.at[slot_send], recv_sem=recv_sem.at[slot_recv],
            device_id=device, device_id_type=MESH,
        )

    f_lo = (src_hbm.at[:, :, pl.ds(0, HALO), :], rec_hbm.at[:, :, pl.ds(0, HALO), :])
    s_lo = slow_hbm.at[0, pl.ds(0, HALO), :]
    for q in range(n_freq):
        @pl.when(f != q)
        def _():
            remote(slow_hbm, g_slow.at[f], q, f, (t, q)).start()

        @pl.when(has_above)
        def _():
            remote(s_lo, h_sb.at[f], 2 * n_freq + q, 2 * n_freq + f, (t - 1, q)).start()

    field_base = 3 * n_freq

    def lower_copy(x, fi, device):
        return remote(f_lo[x].at[:, fi], h_fb.at[x, :, fi], field_base + 2 + 2 * x + fi,
                      field_base + 2 + 2 * x + fi, device)

    def upper_copy(fi, device):
        return remote(up_buf.at[:, :, fi], h_fa.at[:, :, fi], field_base + fi, field_base + fi, device)

    for fi in range(2):
        @pl.when(has_above)
        def _():
            for x in range(2):
                lower_copy(x, fi, (t - 1, f)).start()

    for q in range(n_freq):
        @pl.when(has_below)
        def _():
            remote(s_up, h_sa.at[f], n_freq + q, n_freq + f, (t + 1, q)).start()

    for fi in range(nfl):
        @pl.when(has_below)
        def _():
            upper_copy(fi, (t + 1, f)).start()

    for q in range(n_freq):
        @pl.when(f != q)
        def _():
            remote(slow_hbm, g_slow.at[q], q, q, (t, q)).wait_send()
            remote(slow_hbm, g_slow.at[q], q, q, (t, q)).wait_recv()

        @pl.when(has_below)
        def _():
            remote(s_up, h_sa.at[q], n_freq + q, n_freq + q, (t + 1, q)).wait_send()
            remote(s_lo, h_sb.at[q], 2 * n_freq + q, 2 * n_freq + q, (t + 1, q)).wait_recv()

        @pl.when(has_above)
        def _():
            remote(s_lo, h_sb.at[q], 2 * n_freq + q, 2 * n_freq + q, (t - 1, q)).wait_send()
            remote(s_up, h_sa.at[q], n_freq + q, n_freq + q, (t - 1, q)).wait_recv()

    def await_fields(fi):
        @pl.when(has_below)
        def _():
            upper_copy(fi, (t + 1, f)).wait_send()
            for x in range(2):
                lower_copy(x, fi, (t + 1, f)).wait_recv()

        @pl.when(has_above)
        def _():
            for x in range(2):
                lower_copy(x, fi, (t - 1, f)).wait_send()
            upper_copy(fi, (t - 1, f)).wait_recv()

    rows = lax.broadcasted_iota(jnp.int32, (ext_rows, ncol), 0)
    cols = lax.broadcasted_iota(jnp.int32, (ext_rows, ncol), 1)
    left_ok = jnp.abs(pltpu.roll(cols, 1, 1) - cols) == 1
    right_ok = jnp.abs(pltpu.roll(cols, ncol - 1, 1) - cols) == 1
    forward = pltpu.roll(rows, 1, 0) == (rows + ext_rows - 1) % ext_rows
    lower_start = HALO + ap
    top_part = rows < lower_start

    def in_band(lo, hi):
        return (rows >= lo) & (rows < hi)

    valid0 = (in_band(0, HALO) & has_above) | in_band(HALO, lower_start) | (
        in_band(lower_start, lower_start + HALO) & has_below)
    reach = HALO // 2
    valid1 = (in_band(HALO - reach, HALO) & has_above) | in_band(HALO, lower_start) | (
        in_band(lower_start, lower_start + reach) & has_below)
    live = lax.broadcasted_iota(jnp.int32, (own, ncol), 0) < ap
    zeros_tail = jnp.zeros((ext_rows - HALO, ncol), jnp.float32)

    def place_lower(lower8):
        padded = jnp.concatenate([lower8, zeros_tail], axis=0)
        ahead = pltpu.roll(padded, lower_start, 0)
        behind = pltpu.roll(padded, ext_rows - lower_start, 0)
        return jnp.where(forward, ahead, behind)

    def joined(upper8, own_rows, lower8):
        top = jnp.concatenate([upper8, own_rows, jnp.zeros((HALO, ncol), jnp.float32)], axis=0)
        return jnp.where(top_part, top, place_lower(lower8))

    def columns_of(pieces):
        return jnp.concatenate(pieces, axis=1)

    slow0 = joined(
        columns_of([h_sa[q] for q in range(n_freq)]),
        columns_of([g_slow[q, 0] for q in range(n_freq)]),
        columns_of([h_sb[q] for q in range(n_freq)]),
    )
    slow0 = jnp.where(valid0, slow0, 0.0)
    slow1 = columns_of([g_slow[q, 1] for q in range(n_freq)])

    edge = 128

    def masked_side(b):
        ahead = pltpu.roll(b, 1, 1)
        behind = pltpu.roll(b, ncol - 1, 1)

        def guarded(lo, hi):
            return jnp.where(left_ok[:, lo:hi], ahead[:, lo:hi], 0.0) + jnp.where(
                right_ok[:, lo:hi], behind[:, lo:hi], 0.0)

        middle = ahead[:, edge:ncol - edge] + behind[:, edge:ncol - edge]
        return jnp.concatenate([guarded(0, edge), middle, guarded(ncol - edge, ncol)], axis=1)

    def chebyshev_step(v, prev):
        pair = pltpu.roll(v, 1, 0) + pltpu.roll(v, ext_rows - 1, 0)
        blur = 0.25 * pair + 0.5 * v
        side = masked_side(blur)
        if prev is None:
            return 0.5 * side + blur - v
        return side + 0.5 * pair - v - prev

    def coefficient_of(depth, fi, n, wavenumber):
        coef_re = coeffs[0, n, POWERS - 1] + 0.0 * wavenumber
        coef_im = coeffs[1, n, POWERS - 1] + 0.0 * wavenumber
        for m in range(POWERS - 2, -1, -1):
            coef_re = coef_re * wavenumber + coeffs[0, n, m]
            coef_im = coef_im * wavenumber + coeffs[1, n, m]
        active = (orders[depth, fi] >= n).astype(jnp.float32)
        return coef_re * active, coef_im * active

    for fi in range(nfl):
        for n in range(ORDER + 1):
            cf0[fi, n, 0], cf0[fi, n, 1] = coefficient_of(0, fi, n, frequency[fi] * slow0)
            cf1[fi, n, 0], cf1[fi, n, 1] = coefficient_of(1, fi, n, frequency[fi] * slow1)

    def coefficient(depth, fi, n, wavenumber):
        table = cf0 if depth == 0 else cf1
        return table[fi, n, 0], table[fi, n, 1]

    def extrapolate(depth, fi, wavenumber, valid, lo, hi, write):
        for n in range(ORDER + 1):
            slot = n % 3
            if n >= 1:
                cur, prev = (n - 1) % 3, (n - 2) % 3
                for p in range(4):
                    g = chebyshev_step(tb[cur, p], tb[prev, p] if n > 1 else None)
                    tb[slot, p] = jnp.where(valid, g, 0.0)
            coef_re, coef_im = coefficient(depth, fi, n, wavenumber)
            s_re = tb[slot, 0, lo:hi, :]
            s_im = tb[slot, 1, lo:hi, :]
            r_re = tb[slot, 2, lo:hi, :]
            r_im = tb[slot, 3, lo:hi, :]
            terms = (
                coef_re * s_re + coef_im * s_im,
                coef_re * s_im - coef_im * s_re,
                coef_re * r_re - coef_im * r_im,
                coef_re * r_im + coef_im * r_re,
            )
            write(n, terms)

    fields = (src_v, rec_v)
    for fi in range(nfl):
        await_fields(fi)
        for p in range(4):
            x, c = p // 2, p % 2
            tb[0, p] = jnp.where(valid0, joined(h_fa[x, c, fi], fields[x][c, fi], h_fb[x, c, fi]), 0.0)

        def write0(n, terms, fi=fi):
            for p in range(4):
                if n == 0:
                    s1[p // 2, p % 2, fi] = terms[p]
                else:
                    s1[p // 2, p % 2, fi] = s1[p // 2, p % 2, fi] + terms[p]

        extrapolate(0, fi, frequency[fi] * slow0, valid0, 0, ext_rows, write0)
        for p in range(4):
            s1[p // 2, p % 2, fi] = jnp.where(valid1, s1[p // 2, p % 2, fi], 0.0)
        mid = slice(HALO, HALO + own)
        term = s1[0, 0, fi, mid, :] * s1[1, 0, fi, mid, :] + s1[0, 1, fi, mid, :] * s1[1, 1, fi, mid, :]
        term = jnp.where(live, term, 0.0)
        if fi == 0:
            img_out[0] = term
        else:
            img_out[0] = img_out[0] + term

    image_base = 3 * n_freq + 6

    def image_copy(depth, q, slot_recv, device):
        return pltpu.make_async_remote_copy(
            src_ref=img_out.at[depth, :, pl.ds(q * block, block)], dst_ref=got.at[slot_recv, depth],
            send_sem=send_sem.at[image_base + depth * n_freq + q],
            recv_sem=recv_sem.at[image_base + depth * n_freq + slot_recv],
            device_id=device, device_id_type=MESH,
        )

    def send_image(depth):
        for q in range(n_freq):
            @pl.when(f != q)
            def _():
                image_copy(depth, q, f, (t, q)).start()

    send_image(0)

    for fi in range(nfl):
        for p in range(4):
            tb[0, p] = s1[p // 2, p % 2, fi]
        acc = {}

        def write1(n, terms, acc=acc):
            for p in range(4):
                acc[p] = terms[p] if n == 0 else acc[p] + terms[p]

        extrapolate(1, fi, frequency[fi] * slow1, valid1, HALO, HALO + own, write1)
        result = [jnp.where(live, acc[p], 0.0) for p in range(4)]
        rec_out[0, fi] = result[2]
        rec_out[1, fi] = result[3]
        term = result[0] * result[2] + result[1] * result[3]
        if fi == 0:
            img_out[1] = term
        else:
            img_out[1] = img_out[1] + term

    send_image(1)
    for depth in range(NDEPTH):
        for q in range(n_freq):
            @pl.when(f != q)
            def _():
                image_copy(depth, q, q, (t, q)).wait_send()
                image_copy(depth, q, q, (t, q)).wait_recv()

    total = None
    for q in range(n_freq):
        mine = img_out[:, :, q * block:(q + 1) * block]
        part = jnp.where(f == q, mine, got[q])
        total = part if total is None else total + part
    image_out[...] = total


def shards(n_tile, n_freq, source_field, receiver_field, slowness, frequency, order_table, filter_coeffs, aperture):
    nc, nfl, own, ncol = source_field.shape
    block = slowness.shape[2]
    ext_rows = own + 2 * HALO
    elements = nc * nfl * 2 * ext_rows * ncol * NDEPTH
    rec_out, image_out = pl.pallas_call(
        functools.partial(migrate_kernel, n_tile, n_freq),
        out_shape=(
            jax.ShapeDtypeStruct((nc, nfl, own, ncol), jnp.float32),
            jax.ShapeDtypeStruct((NDEPTH, own, block), jnp.float32),
        ),
        in_specs=[pl.BlockSpec(memory_space=SMEM)] * 3 + [pl.BlockSpec(memory_space=pl.ANY)] * 4,
        out_specs=(pl.BlockSpec(memory_space=VMEM), pl.BlockSpec(memory_space=VMEM)),
        scratch_shapes=[
            pltpu.VMEM((nc, nfl, own, ncol), jnp.float32),
            pltpu.VMEM((nc, nfl, own, ncol), jnp.float32),
            pltpu.VMEM((n_freq, NDEPTH, own, block), jnp.float32),
            pltpu.VMEM((n_freq, HALO, block), jnp.float32),
            pltpu.VMEM((n_freq, HALO, block), jnp.float32),
            pltpu.VMEM((2, nc, nfl, HALO, ncol), jnp.float32),
            pltpu.VMEM((2, nc, nfl, HALO, ncol), jnp.float32),
            pltpu.VMEM((2, nc, nfl, HALO, ncol), jnp.float32),
            pltpu.VMEM((HALO, block), jnp.float32),
            pltpu.VMEM((2, nc, nfl, ext_rows, ncol), jnp.float32),
            pltpu.VMEM((3, 4, ext_rows, ncol), jnp.float32),
            pltpu.VMEM((NDEPTH, own, ncol), jnp.float32),
            pltpu.VMEM((n_freq, NDEPTH, own, block), jnp.float32),
            pltpu.SMEM(filter_coeffs.shape, jnp.float32),
            pltpu.VMEM((nfl, ORDER + 1, 2, ext_rows, ncol), jnp.float32),
            pltpu.VMEM((nfl, ORDER + 1, 2, own, ncol), jnp.float32),
            pltpu.SemaphoreType.DMA((4,)),
            pltpu.SemaphoreType.DMA((3 * n_freq + 6 + NDEPTH * n_freq,)),
            pltpu.SemaphoreType.DMA((3 * n_freq + 6 + NDEPTH * n_freq,)),
        ],
        compiler_params=pltpu.CompilerParams(collective_id=0, has_side_effects=True),
        cost_estimate=pl.CostEstimate(flops=elements * 100, bytes_accessed=elements * 4, transcendentals=0),
    )(aperture, order_table, frequency, filter_coeffs, source_field, receiver_field, slowness)
    return pl.pallas_call(
        passthrough_kernel,
        out_shape=(
            jax.ShapeDtypeStruct(image_out.shape, jnp.float32),
            jax.ShapeDtypeStruct(rec_out.shape, jnp.float32),
        ),
        in_specs=[pl.BlockSpec(memory_space=VMEM)] * 2,
        out_specs=(pl.BlockSpec(memory_space=VMEM), pl.BlockSpec(memory_space=VMEM)),
    )(image_out, rec_out)


def passthrough_kernel(img_in, rec_in, img_out, rec_out):
    img_out[...] = img_in[...]
    rec_out[...] = rec_in[...]


def solution(mesh):
    placed = (
        P(None, "freq", "tile", None),
        P(None, "freq", "tile", None),
        P(None, "tile", "freq"),
        P("freq"),
        P(None, "freq"),
        P(),
        P(),
    )
    return jax.shard_map(
        functools.partial(shards, mesh.shape["tile"], mesh.shape["freq"]),
        mesh=mesh,
        in_specs=placed,
        out_specs=(P(None, "tile", "freq"), P(None, "freq", "tile", None)),
        check_vma=False,
    )
```

```python
import functools

import jax
import jax.numpy as jnp
from jax import lax
from jax.experimental import pallas as pl
from jax.experimental.pallas import tpu as pltpu
from jax.sharding import PartitionSpec as P

ORDER = 4
NDEPTH = 2
POWERS = 3
HALO = 8
MESH = pl.DeviceIdType.MESH
VMEM = pltpu.MemorySpace.VMEM
SMEM = pltpu.MemorySpace.SMEM


def migrate_kernel(n_tile, n_freq, aperture, orders, frequency, coeffs_hbm, src_hbm, rec_hbm, slow_hbm,
                   rec_out, image_out, src_v, rec_v, g_slow, h_sa, h_sb, h_fa, h_fb, up_buf, s_up, s1, tb, img_out,
                   got, coeffs, cf0, cf1, local_sem, send_sem, recv_sem):
    t = lax.axis_index("tile")
    f = lax.axis_index("freq")
    nc, nfl, own, ncol = src_v.shape
    ext_rows = HALO + own + HALO
    block = slow_hbm.shape[2]
    ap = aperture[t]
    has_above = t > 0
    has_below = t < n_tile - 1

    loads = (
        pltpu.make_async_copy(src_hbm, src_v, local_sem.at[0]),
        pltpu.make_async_copy(rec_hbm, rec_v, local_sem.at[1]),
        pltpu.make_async_copy(slow_hbm, g_slow.at[f], local_sem.at[2]),
        pltpu.make_async_copy(coeffs_hbm, coeffs, local_sem.at[3]),
    )
    for copy in loads:
        copy.start()

    @pl.when(t == 0)
    def _():
        h_fa[...] = jnp.zeros_like(h_fa)
        h_sa[...] = jnp.zeros_like(h_sa)

    @pl.when(t == n_tile - 1)
    def _():
        h_fb[...] = jnp.zeros_like(h_fb)
        h_sb[...] = jnp.zeros_like(h_sb)

    barrier = pltpu.get_barrier_semaphore()
    for q in range(n_freq):
        @pl.when(f != q)
        def _():
            pl.semaphore_signal(barrier, 1, device_id=(t, q), device_id_type=MESH)

        @pl.when(has_above)
        def _():
            pl.semaphore_signal(barrier, 1, device_id=(t - 1, q), device_id_type=MESH)

        @pl.when(has_below)
        def _():
            pl.semaphore_signal(barrier, 1, device_id=(t + 1, q), device_id_type=MESH)

    expected = (n_freq - 1) + n_freq * has_above.astype(jnp.int32) + n_freq * has_below.astype(jnp.int32)

    for copy in loads:
        copy.wait()

    own_rows = lax.broadcasted_iota(jnp.int32, (own, ncol), 0)
    own_forward = pltpu.roll(own_rows, 1, 0) == (own_rows + own - 1) % own
    lift = (own + HALO - ap) % own
    drop = ap - HALO

    def last_rows(x, forward):
        return jnp.where(forward, pltpu.roll(x, lift, 0), pltpu.roll(x, drop, 0))[:HALO]

    s_up[...] = last_rows(g_slow[f, 0], own_forward[:, :block])
    fields_v = (src_v, rec_v)
    for fi in range(nfl):
        for x in range(2):
            for c in range(nc):
                up_buf[x, c, fi] = last_rows(fields_v[x][c, fi], own_forward)

    pl.semaphore_wait(barrier, expected)

    def remote(src, dst, slot_send, slot_recv, device):
        return pltpu.make_async_remote_copy(
            src_ref=src, dst_ref=dst, send_sem=send_sem.at[slot_send], recv_sem=recv_sem.at[slot_recv],
            device_id=device, device_id_type=MESH,
        )

    f_lo = (src_hbm.at[:, :, pl.ds(0, HALO), :], rec_hbm.at[:, :, pl.ds(0, HALO), :])
    s_lo = slow_hbm.at[0, pl.ds(0, HALO), :]
    for q in range(n_freq):
        @pl.when(f != q)
        def _():
            remote(slow_hbm, g_slow.at[f], q, f, (t, q)).start()

        @pl.when(has_above)
        def _():
            remote(s_lo, h_sb.at[f], 2 * n_freq + q, 2 * n_freq + f, (t - 1, q)).start()

    field_base = 3 * n_freq

    def lower_copy(x, fi, device):
        return remote(f_lo[x].at[:, fi], h_fb.at[x, :, fi], field_base + 2 + 2 * x + fi,
                      field_base + 2 + 2 * x + fi, device)

    def upper_copy(fi, device):
        return remote(up_buf.at[:, :, fi], h_fa.at[:, :, fi], field_base + fi, field_base + fi, device)

    for fi in range(2):
        @pl.when(has_above)
        def _():
            for x in range(2):
                lower_copy(x, fi, (t - 1, f)).start()

    for q in range(n_freq):
        @pl.when(has_below)
        def _():
            remote(s_up, h_sa.at[f], n_freq + q, n_freq + f, (t + 1, q)).start()

    for fi in range(nfl):
        @pl.when(has_below)
        def _():
            upper_copy(fi, (t + 1, f)).start()

    for q in range(n_freq):
        @pl.when(f != q)
        def _():
            remote(slow_hbm, g_slow.at[q], q, q, (t, q)).wait_send()
            remote(slow_hbm, g_slow.at[q], q, q, (t, q)).wait_recv()

        @pl.when(has_below)
        def _():
            remote(s_up, h_sa.at[q], n_freq + q, n_freq + q, (t + 1, q)).wait_send()
            remote(s_lo, h_sb.at[q], 2 * n_freq + q, 2 * n_freq + q, (t + 1, q)).wait_recv()

        @pl.when(has_above)
        def _():
            remote(s_lo, h_sb.at[q], 2 * n_freq + q, 2 * n_freq + q, (t - 1, q)).wait_send()
            remote(s_up, h_sa.at[q], n_freq + q, n_freq + q, (t - 1, q)).wait_recv()

    def await_fields(fi):
        @pl.when(has_below)
        def _():
            upper_copy(fi, (t + 1, f)).wait_send()
            for x in range(2):
                lower_copy(x, fi, (t + 1, f)).wait_recv()

        @pl.when(has_above)
        def _():
            for x in range(2):
                lower_copy(x, fi, (t - 1, f)).wait_send()
            upper_copy(fi, (t - 1, f)).wait_recv()

    rows = lax.broadcasted_iota(jnp.int32, (ext_rows, ncol), 0)
    cols = lax.broadcasted_iota(jnp.int32, (ext_rows, ncol), 1)
    left_ok = jnp.abs(pltpu.roll(cols, 1, 1) - cols) == 1
    right_ok = jnp.abs(pltpu.roll(cols, ncol - 1, 1) - cols) == 1
    forward = pltpu.roll(rows, 1, 0) == (rows + ext_rows - 1) % ext_rows
    lower_start = HALO + ap
    top_part = rows < lower_start

    def in_band(lo, hi):
        return (rows >= lo) & (rows < hi)

    valid0 = (in_band(0, HALO) & has_above) | in_band(HALO, lower_start) | (
        in_band(lower_start, lower_start + HALO) & has_below)
    reach = HALO // 2
    valid1 = (in_band(HALO - reach, HALO) & has_above) | in_band(HALO, lower_start) | (
        in_band(lower_start, lower_start + reach) & has_below)
    live = lax.broadcasted_iota(jnp.int32, (own, ncol), 0) < ap
    zeros_tail = jnp.zeros((ext_rows - HALO, ncol), jnp.float32)

    def place_lower(lower8):
        padded = jnp.concatenate([lower8, zeros_tail], axis=0)
        ahead = pltpu.roll(padded, lower_start, 0)
        behind = pltpu.roll(padded, ext_rows - lower_start, 0)
        return jnp.where(forward, ahead, behind)

    def joined(upper8, own_rows, lower8):
        top = jnp.concatenate([upper8, own_rows, jnp.zeros((HALO, ncol), jnp.float32)], axis=0)
        return jnp.where(top_part, top, place_lower(lower8))

    def columns_of(pieces):
        return jnp.concatenate(pieces, axis=1)

    slow0 = joined(
        columns_of([h_sa[q] for q in range(n_freq)]),
        columns_of([g_slow[q, 0] for q in range(n_freq)]),
        columns_of([h_sb[q] for q in range(n_freq)]),
    )
    slow0 = jnp.where(valid0, slow0, 0.0)
    slow1 = columns_of([g_slow[q, 1] for q in range(n_freq)])

    edge = 128

    def masked_side(b):
        ahead = pltpu.roll(b, 1, 1)
        behind = pltpu.roll(b, ncol - 1, 1)

        def guarded(lo, hi):
            return jnp.where(left_ok[:, lo:hi], ahead[:, lo:hi], 0.0) + jnp.where(
                right_ok[:, lo:hi], behind[:, lo:hi], 0.0)

        middle = ahead[:, edge:ncol - edge] + behind[:, edge:ncol - edge]
        return jnp.concatenate([guarded(0, edge), middle, guarded(ncol - edge, ncol)], axis=1)

    def chebyshev_step(v, prev):
        pair = pltpu.roll(v, 1, 0) + pltpu.roll(v, ext_rows - 1, 0)
        blur = 0.25 * pair + 0.5 * v
        side = masked_side(blur)
        if prev is None:
            return 0.5 * side + blur - v
        return side + 0.5 * pair - v - prev

    def coefficient_of(depth, fi, n, wavenumber):
        active = jnp.where(orders[depth, fi] >= n, 1.0, 0.0).astype(jnp.float32)
        scaled = [[coeffs[c, n, m] * active for m in range(POWERS)] for c in range(2)]
        coef_re = scaled[0][POWERS - 1] * wavenumber + scaled[0][POWERS - 2]
        coef_im = scaled[1][POWERS - 1] * wavenumber + scaled[1][POWERS - 2]
        for m in range(POWERS - 3, -1, -1):
            coef_re = coef_re * wavenumber + scaled[0][m]
            coef_im = coef_im * wavenumber + scaled[1][m]
        return coef_re, coef_im

    for fi in range(nfl):
        wave0 = frequency[fi] * slow0
        wave1 = frequency[fi] * slow1
        for n in range(ORDER + 1):
            cf0[fi, n, 0], cf0[fi, n, 1] = coefficient_of(0, fi, n, wave0)
            cf1[fi, n, 0], cf1[fi, n, 1] = coefficient_of(1, fi, n, wave1)

    def coefficient(depth, fi, n, wavenumber):
        table = cf0 if depth == 0 else cf1
        return table[fi, n, 0], table[fi, n, 1]

    def extrapolate(depth, fi, wavenumber, valid, lo, hi, write):
        for n in range(ORDER + 1):
            slot = n % 3
            if n >= 1:
                cur, prev = (n - 1) % 3, (n - 2) % 3
                for p in range(4):
                    g = chebyshev_step(tb[cur, p], tb[prev, p] if n > 1 else None)
                    tb[slot, p] = jnp.where(valid, g, 0.0)
            coef_re, coef_im = coefficient(depth, fi, n, wavenumber)
            s_re = tb[slot, 0, lo:hi, :]
            s_im = tb[slot, 1, lo:hi, :]
            r_re = tb[slot, 2, lo:hi, :]
            r_im = tb[slot, 3, lo:hi, :]
            terms = (
                coef_re * s_re + coef_im * s_im,
                coef_re * s_im - coef_im * s_re,
                coef_re * r_re - coef_im * r_im,
                coef_re * r_im + coef_im * r_re,
            )
            write(n, terms)

    fields = (src_v, rec_v)
    for fi in range(nfl):
        await_fields(fi)
        for p in range(4):
            x, c = p // 2, p % 2
            tb[0, p] = jnp.where(valid0, joined(h_fa[x, c, fi], fields[x][c, fi], h_fb[x, c, fi]), 0.0)

        def write0(n, terms, fi=fi):
            for p in range(4):
                if n == 0:
                    s1[p // 2, p % 2, fi] = terms[p]
                else:
                    s1[p // 2, p % 2, fi] = s1[p // 2, p % 2, fi] + terms[p]

        extrapolate(0, fi, frequency[fi] * slow0, valid0, 0, ext_rows, write0)
        for p in range(4):
            s1[p // 2, p % 2, fi] = jnp.where(valid1, s1[p // 2, p % 2, fi], 0.0)
        mid = slice(HALO, HALO + own)
        term = s1[0, 0, fi, mid, :] * s1[1, 0, fi, mid, :] + s1[0, 1, fi, mid, :] * s1[1, 1, fi, mid, :]
        term = jnp.where(live, term, 0.0)
        if fi == 0:
            img_out[0] = term
        else:
            img_out[0] = img_out[0] + term

    image_base = 3 * n_freq + 6

    def image_copy(depth, q, slot_recv, device):
        return pltpu.make_async_remote_copy(
            src_ref=img_out.at[depth, :, pl.ds(q * block, block)], dst_ref=got.at[slot_recv, depth],
            send_sem=send_sem.at[image_base + depth * n_freq + q],
            recv_sem=recv_sem.at[image_base + depth * n_freq + slot_recv],
            device_id=device, device_id_type=MESH,
        )

    def send_image(depth):
        for q in range(n_freq):
            @pl.when(f != q)
            def _():
                image_copy(depth, q, f, (t, q)).start()

    send_image(0)

    for fi in range(nfl):
        for p in range(4):
            tb[0, p] = s1[p // 2, p % 2, fi]
        acc = {}

        def write1(n, terms, acc=acc):
            for p in range(4):
                acc[p] = terms[p] if n == 0 else acc[p] + terms[p]

        extrapolate(1, fi, frequency[fi] * slow1, valid1, HALO, HALO + own, write1)
        result = [jnp.where(live, acc[p], 0.0) for p in range(4)]
        rec_out[0, fi] = result[2]
        rec_out[1, fi] = result[3]
        term = result[0] * result[2] + result[1] * result[3]
        if fi == 0:
            img_out[1] = term
        else:
            img_out[1] = img_out[1] + term

    send_image(1)
    for depth in range(NDEPTH):
        for q in range(n_freq):
            @pl.when(f != q)
            def _():
                image_copy(depth, q, q, (t, q)).wait_send()
                image_copy(depth, q, q, (t, q)).wait_recv()

    total = None
    for q in range(n_freq):
        mine = img_out[:, :, q * block:(q + 1) * block]
        part = jnp.where(f == q, mine, got[q])
        total = part if total is None else total + part
    image_out[...] = total


def shards(n_tile, n_freq, source_field, receiver_field, slowness, frequency, order_table, filter_coeffs, aperture):
    nc, nfl, own, ncol = source_field.shape
    block = slowness.shape[2]
    ext_rows = own + 2 * HALO
    elements = nc * nfl * 2 * ext_rows * ncol * NDEPTH
    rec_out, image_out = pl.pallas_call(
        functools.partial(migrate_kernel, n_tile, n_freq),
        out_shape=(
            jax.ShapeDtypeStruct((nc, nfl, own, ncol), jnp.float32),
            jax.ShapeDtypeStruct((NDEPTH, own, block), jnp.float32),
        ),
        in_specs=[pl.BlockSpec(memory_space=SMEM)] * 3 + [pl.BlockSpec(memory_space=pl.ANY)] * 4,
        out_specs=(pl.BlockSpec(memory_space=VMEM), pl.BlockSpec(memory_space=VMEM)),
        scratch_shapes=[
            pltpu.VMEM((nc, nfl, own, ncol), jnp.float32),
            pltpu.VMEM((nc, nfl, own, ncol), jnp.float32),
            pltpu.VMEM((n_freq, NDEPTH, own, block), jnp.float32),
            pltpu.VMEM((n_freq, HALO, block), jnp.float32),
            pltpu.VMEM((n_freq, HALO, block), jnp.float32),
            pltpu.VMEM((2, nc, nfl, HALO, ncol), jnp.float32),
            pltpu.VMEM((2, nc, nfl, HALO, ncol), jnp.float32),
            pltpu.VMEM((2, nc, nfl, HALO, ncol), jnp.float32),
            pltpu.VMEM((HALO, block), jnp.float32),
            pltpu.VMEM((2, nc, nfl, ext_rows, ncol), jnp.float32),
            pltpu.VMEM((3, 4, ext_rows, ncol), jnp.float32),
            pltpu.VMEM((NDEPTH, own, ncol), jnp.float32),
            pltpu.VMEM((n_freq, NDEPTH, own, block), jnp.float32),
            pltpu.SMEM(filter_coeffs.shape, jnp.float32),
            pltpu.VMEM((nfl, ORDER + 1, 2, ext_rows, ncol), jnp.float32),
            pltpu.VMEM((nfl, ORDER + 1, 2, own, ncol), jnp.float32),
            pltpu.SemaphoreType.DMA((4,)),
            pltpu.SemaphoreType.DMA((3 * n_freq + 6 + NDEPTH * n_freq,)),
            pltpu.SemaphoreType.DMA((3 * n_freq + 6 + NDEPTH * n_freq,)),
        ],
        compiler_params=pltpu.CompilerParams(collective_id=0, has_side_effects=True),
        cost_estimate=pl.CostEstimate(flops=elements * 100, bytes_accessed=elements * 4, transcendentals=0),
    )(aperture, order_table, frequency, filter_coeffs, source_field, receiver_field, slowness)
    return pl.pallas_call(
        passthrough_kernel,
        out_shape=(
            jax.ShapeDtypeStruct(image_out.shape, jnp.float32),
            jax.ShapeDtypeStruct(rec_out.shape, jnp.float32),
        ),
        in_specs=[pl.BlockSpec(memory_space=VMEM)] * 2,
        out_specs=(pl.BlockSpec(memory_space=VMEM), pl.BlockSpec(memory_space=VMEM)),
    )(image_out, rec_out)


def passthrough_kernel(img_in, rec_in, img_out, rec_out):
    img_out[...] = img_in[...]
    rec_out[...] = rec_in[...]


def solution(mesh):
    placed = (
        P(None, "freq", "tile", None),
        P(None, "freq", "tile", None),
        P(None, "tile", "freq"),
        P("freq"),
        P(None, "freq"),
        P(),
        P(),
    )
    return jax.shard_map(
        functools.partial(shards, mesh.shape["tile"], mesh.shape["freq"]),
        mesh=mesh,
        in_specs=placed,
        out_specs=(P(None, "tile", "freq"), P(None, "freq", "tile", None)),
        check_vma=False,
    )
```

```python
import functools

import jax
import jax.numpy as jnp
from jax import lax
from jax.experimental import pallas as pl
from jax.experimental.pallas import tpu as pltpu
from jax.sharding import PartitionSpec as P

ORDER = 4
NDEPTH = 2
POWERS = 3
HALO = 8
MESH = pl.DeviceIdType.MESH
VMEM = pltpu.MemorySpace.VMEM
SMEM = pltpu.MemorySpace.SMEM


def migrate_kernel(n_tile, n_freq, aperture, orders, frequency, coeffs_hbm, src_hbm, rec_hbm, slow_hbm,
                   rec_out, image_out, src_v, rec_v, g_slow, h_sa, h_sb, h_fa, h_fb, up_buf, s_up, s1, tb, img_out,
                   got, coeffs, cf0, cf1, local_sem, send_sem, recv_sem):
    t = lax.axis_index("tile")
    f = lax.axis_index("freq")
    nc, nfl, own, ncol = src_v.shape
    ext_rows = HALO + own + HALO
    block = slow_hbm.shape[2]
    ap = aperture[t]
    has_above = t > 0
    has_below = t < n_tile - 1

    loads = (
        pltpu.make_async_copy(src_hbm, src_v, local_sem.at[0]),
        pltpu.make_async_copy(rec_hbm, rec_v, local_sem.at[1]),
        pltpu.make_async_copy(slow_hbm, g_slow.at[f], local_sem.at[2]),
        pltpu.make_async_copy(coeffs_hbm, coeffs, local_sem.at[3]),
    )
    for copy in loads:
        copy.start()

    @pl.when(t == 0)
    def _():
        h_fa[...] = jnp.zeros_like(h_fa)
        h_sa[...] = jnp.zeros_like(h_sa)

    @pl.when(t == n_tile - 1)
    def _():
        h_fb[...] = jnp.zeros_like(h_fb)
        h_sb[...] = jnp.zeros_like(h_sb)

    barrier = pltpu.get_barrier_semaphore()
    for q in range(n_freq):
        @pl.when(f != q)
        def _():
            pl.semaphore_signal(barrier, 1, device_id=(t, q), device_id_type=MESH)

        @pl.when(has_above)
        def _():
            pl.semaphore_signal(barrier, 1, device_id=(t - 1, q), device_id_type=MESH)

        @pl.when(has_below)
        def _():
            pl.semaphore_signal(barrier, 1, device_id=(t + 1, q), device_id_type=MESH)

    expected = (n_freq - 1) + n_freq * has_above.astype(jnp.int32) + n_freq * has_below.astype(jnp.int32)

    for copy in loads:
        copy.wait()

    own_rows = lax.broadcasted_iota(jnp.int32, (own, ncol), 0)
    own_forward = pltpu.roll(own_rows, 1, 0) == (own_rows + own - 1) % own
    lift = (own + HALO - ap) % own
    drop = ap - HALO

    def last_rows(x, forward):
        return jnp.where(forward, pltpu.roll(x, lift, 0), pltpu.roll(x, drop, 0))[:HALO]

    s_up[...] = last_rows(g_slow[f, 0], own_forward[:, :block])
    fields_v = (src_v, rec_v)
    for fi in range(nfl):
        for x in range(2):
            for c in range(nc):
                up_buf[x, c, fi] = last_rows(fields_v[x][c, fi], own_forward)

    pl.semaphore_wait(barrier, expected)

    def remote(src, dst, slot_send, slot_recv, device):
        return pltpu.make_async_remote_copy(
            src_ref=src, dst_ref=dst, send_sem=send_sem.at[slot_send], recv_sem=recv_sem.at[slot_recv],
            device_id=device, device_id_type=MESH,
        )

    f_lo = (src_hbm.at[:, :, pl.ds(0, HALO), :], rec_hbm.at[:, :, pl.ds(0, HALO), :])
    s_lo = slow_hbm.at[0, pl.ds(0, HALO), :]
    for q in range(n_freq):
        @pl.when(f != q)
        def _():
            remote(slow_hbm, g_slow.at[f], q, f, (t, q)).start()

        @pl.when(has_above)
        def _():
            remote(s_lo, h_sb.at[f], 2 * n_freq + q, 2 * n_freq + f, (t - 1, q)).start()

    field_base = 3 * n_freq

    def lower_copy(x, fi, device):
        return remote(f_lo[x].at[:, fi], h_fb.at[x, :, fi], field_base + 2 + 2 * x + fi,
                      field_base + 2 + 2 * x + fi, device)

    def upper_copy(fi, device):
        return remote(up_buf.at[:, :, fi], h_fa.at[:, :, fi], field_base + fi, field_base + fi, device)

    for fi in range(2):
        @pl.when(has_above)
        def _():
            for x in range(2):
                lower_copy(x, fi, (t - 1, f)).start()

    for q in range(n_freq):
        @pl.when(has_below)
        def _():
            remote(s_up, h_sa.at[f], n_freq + q, n_freq + f, (t + 1, q)).start()

    for fi in range(nfl):
        @pl.when(has_below)
        def _():
            upper_copy(fi, (t + 1, f)).start()

    for q in range(n_freq):
        @pl.when(f != q)
        def _():
            remote(slow_hbm, g_slow.at[q], q, q, (t, q)).wait_send()
            remote(slow_hbm, g_slow.at[q], q, q, (t, q)).wait_recv()

        @pl.when(has_below)
        def _():
            remote(s_up, h_sa.at[q], n_freq + q, n_freq + q, (t + 1, q)).wait_send()
            remote(s_lo, h_sb.at[q], 2 * n_freq + q, 2 * n_freq + q, (t + 1, q)).wait_recv()

        @pl.when(has_above)
        def _():
            remote(s_lo, h_sb.at[q], 2 * n_freq + q, 2 * n_freq + q, (t - 1, q)).wait_send()
            remote(s_up, h_sa.at[q], n_freq + q, n_freq + q, (t - 1, q)).wait_recv()

    def await_fields(fi):
        @pl.when(has_below)
        def _():
            upper_copy(fi, (t + 1, f)).wait_send()
            for x in range(2):
                lower_copy(x, fi, (t + 1, f)).wait_recv()

        @pl.when(has_above)
        def _():
            for x in range(2):
                lower_copy(x, fi, (t - 1, f)).wait_send()
            upper_copy(fi, (t - 1, f)).wait_recv()

    rows = lax.broadcasted_iota(jnp.int32, (ext_rows, ncol), 0)
    cols = lax.broadcasted_iota(jnp.int32, (ext_rows, ncol), 1)
    left_ok = jnp.abs(pltpu.roll(cols, 1, 1) - cols) == 1
    right_ok = jnp.abs(pltpu.roll(cols, ncol - 1, 1) - cols) == 1
    forward = pltpu.roll(rows, 1, 0) == (rows + ext_rows - 1) % ext_rows
    lower_start = HALO + ap
    top_part = rows < lower_start

    def in_band(lo, hi):
        return (rows >= lo) & (rows < hi)

    valid0 = (in_band(0, HALO) & has_above) | in_band(HALO, lower_start) | (
        in_band(lower_start, lower_start + HALO) & has_below)
    reach = HALO // 2
    valid1 = (in_band(HALO - reach, HALO) & has_above) | in_band(HALO, lower_start) | (
        in_band(lower_start, lower_start + reach) & has_below)
    live = lax.broadcasted_iota(jnp.int32, (own, ncol), 0) < ap
    zeros_tail = jnp.zeros((ext_rows - HALO, ncol), jnp.float32)

    def place_lower(lower8):
        padded = jnp.concatenate([lower8, zeros_tail], axis=0)
        ahead = pltpu.roll(padded, lower_start, 0)
        behind = pltpu.roll(padded, ext_rows - lower_start, 0)
        return jnp.where(forward, ahead, behind)

    def joined(upper8, own_rows, lower8):
        top = jnp.concatenate([upper8, own_rows, jnp.zeros((HALO, ncol), jnp.float32)], axis=0)
        return jnp.where(top_part, top, place_lower(lower8))

    def columns_of(pieces):
        return jnp.concatenate(pieces, axis=1)

    slow0 = joined(
        columns_of([h_sa[q] for q in range(n_freq)]),
        columns_of([g_slow[q, 0] for q in range(n_freq)]),
        columns_of([h_sb[q] for q in range(n_freq)]),
    )
    slow0 = jnp.where(valid0, slow0, 0.0)
    slow1 = columns_of([g_slow[q, 1] for q in range(n_freq)])

    edge = 128

    def masked_side(b):
        ahead = pltpu.roll(b, 1, 1)
        behind = pltpu.roll(b, ncol - 1, 1)

        def guarded(lo, hi):
            return jnp.where(left_ok[:, lo:hi], ahead[:, lo:hi], 0.0) + jnp.where(
                right_ok[:, lo:hi], behind[:, lo:hi], 0.0)

        middle = ahead[:, edge:ncol - edge] + behind[:, edge:ncol - edge]
        return jnp.concatenate([guarded(0, edge), middle, guarded(ncol - edge, ncol)], axis=1)

    def chebyshev_step(v, prev):
        pair = pltpu.roll(v, 1, 0) + pltpu.roll(v, ext_rows - 1, 0)
        blur = 0.25 * pair + 0.5 * v
        side = masked_side(blur)
        if prev is None:
            return 0.5 * side + blur - v
        return side + 0.5 * pair - v - prev

    def coefficient_of(depth, fi, n, wavenumber):
        active = jnp.where(orders[depth, fi] >= n, 1.0, 0.0).astype(jnp.float32)
        scaled = [[coeffs[m, c, n] * active for m in range(POWERS)] for c in range(2)]
        coef_re = scaled[0][POWERS - 1] * wavenumber + scaled[0][POWERS - 2]
        coef_im = scaled[1][POWERS - 1] * wavenumber + scaled[1][POWERS - 2]
        for m in range(POWERS - 3, -1, -1):
            coef_re = coef_re * wavenumber + scaled[0][m]
            coef_im = coef_im * wavenumber + scaled[1][m]
        return coef_re, coef_im

    for fi in range(nfl):
        wave0 = frequency[fi] * slow0
        wave1 = frequency[fi] * slow1
        for n in range(ORDER + 1):
            cf0[fi, n, 0], cf0[fi, n, 1] = coefficient_of(0, fi, n, wave0)
            cf1[fi, n, 0], cf1[fi, n, 1] = coefficient_of(1, fi, n, wave1)

    def coefficient(depth, fi, n, wavenumber):
        table = cf0 if depth == 0 else cf1
        return table[fi, n, 0], table[fi, n, 1]

    def extrapolate(depth, fi, wavenumber, valid, lo, hi, write):
        for n in range(ORDER + 1):
            slot = n % 3
            if n >= 1:
                cur, prev = (n - 1) % 3, (n - 2) % 3
                for p in range(4):
                    g = chebyshev_step(tb[cur, p], tb[prev, p] if n > 1 else None)
                    tb[slot, p] = jnp.where(valid, g, 0.0)
            coef_re, coef_im = coefficient(depth, fi, n, wavenumber)
            s_re = tb[slot, 0, lo:hi, :]
            s_im = tb[slot, 1, lo:hi, :]
            r_re = tb[slot, 2, lo:hi, :]
            r_im = tb[slot, 3, lo:hi, :]
            terms = (
                coef_re * s_re + coef_im * s_im,
                coef_re * s_im - coef_im * s_re,
                coef_re * r_re - coef_im * r_im,
                coef_re * r_im + coef_im * r_re,
            )
            write(n, terms)

    fields = (src_v, rec_v)
    for fi in range(nfl):
        await_fields(fi)
        for p in range(4):
            x, c = p // 2, p % 2
            tb[0, p] = jnp.where(valid0, joined(h_fa[x, c, fi], fields[x][c, fi], h_fb[x, c, fi]), 0.0)

        def write0(n, terms, fi=fi):
            for p in range(4):
                if n == 0:
                    s1[p // 2, p % 2, fi] = terms[p]
                else:
                    s1[p // 2, p % 2, fi] = s1[p // 2, p % 2, fi] + terms[p]

        extrapolate(0, fi, frequency[fi] * slow0, valid0, 0, ext_rows, write0)
        for p in range(4):
            s1[p // 2, p % 2, fi] = jnp.where(valid1, s1[p // 2, p % 2, fi], 0.0)
        mid = slice(HALO, HALO + own)
        term = s1[0, 0, fi, mid, :] * s1[1, 0, fi, mid, :] + s1[0, 1, fi, mid, :] * s1[1, 1, fi, mid, :]
        term = jnp.where(live, term, 0.0)
        if fi == 0:
            img_out[0] = term
        else:
            img_out[0] = img_out[0] + term

    image_base = 3 * n_freq + 6

    def image_copy(depth, q, slot_recv, device):
        return pltpu.make_async_remote_copy(
            src_ref=img_out.at[depth, :, pl.ds(q * block, block)], dst_ref=got.at[slot_recv, depth],
            send_sem=send_sem.at[image_base + depth * n_freq + q],
            recv_sem=recv_sem.at[image_base + depth * n_freq + slot_recv],
            device_id=device, device_id_type=MESH,
        )

    def send_image(depth):
        for q in range(n_freq):
            @pl.when(f != q)
            def _():
                image_copy(depth, q, f, (t, q)).start()

    send_image(0)

    for fi in range(nfl):
        for p in range(4):
            tb[0, p] = s1[p // 2, p % 2, fi]
        acc = {}

        def write1(n, terms, acc=acc):
            for p in range(4):
                acc[p] = terms[p] if n == 0 else acc[p] + terms[p]

        extrapolate(1, fi, frequency[fi] * slow1, valid1, HALO, HALO + own, write1)
        result = [jnp.where(live, acc[p], 0.0) for p in range(4)]
        rec_out[0, fi] = result[2]
        rec_out[1, fi] = result[3]
        term = result[0] * result[2] + result[1] * result[3]
        if fi == 0:
            img_out[1] = term
        else:
            img_out[1] = img_out[1] + term

    send_image(1)
    for depth in range(NDEPTH):
        for q in range(n_freq):
            @pl.when(f != q)
            def _():
                image_copy(depth, q, q, (t, q)).wait_send()
                image_copy(depth, q, q, (t, q)).wait_recv()

    total = None
    for q in range(n_freq):
        mine = img_out[:, :, q * block:(q + 1) * block]
        part = jnp.where(f == q, mine, got[q])
        total = part if total is None else total + part
    image_out[...] = total


def shards(n_tile, n_freq, source_field, receiver_field, slowness, frequency, order_table, filter_coeffs, aperture):
    nc, nfl, own, ncol = source_field.shape
    block = slowness.shape[2]
    ext_rows = own + 2 * HALO
    elements = nc * nfl * 2 * ext_rows * ncol * NDEPTH
    rec_out, image_out = pl.pallas_call(
        functools.partial(migrate_kernel, n_tile, n_freq),
        out_shape=(
            jax.ShapeDtypeStruct((nc, nfl, own, ncol), jnp.float32),
            jax.ShapeDtypeStruct((NDEPTH, own, block), jnp.float32),
        ),
        in_specs=[pl.BlockSpec(memory_space=SMEM)] * 3 + [pl.BlockSpec(memory_space=pl.ANY)] * 4,
        out_specs=(pl.BlockSpec(memory_space=VMEM), pl.BlockSpec(memory_space=VMEM)),
        scratch_shapes=[
            pltpu.VMEM((nc, nfl, own, ncol), jnp.float32),
            pltpu.VMEM((nc, nfl, own, ncol), jnp.float32),
            pltpu.VMEM((n_freq, NDEPTH, own, block), jnp.float32),
            pltpu.VMEM((n_freq, HALO, block), jnp.float32),
            pltpu.VMEM((n_freq, HALO, block), jnp.float32),
            pltpu.VMEM((2, nc, nfl, HALO, ncol), jnp.float32),
            pltpu.VMEM((2, nc, nfl, HALO, ncol), jnp.float32),
            pltpu.VMEM((2, nc, nfl, HALO, ncol), jnp.float32),
            pltpu.VMEM((HALO, block), jnp.float32),
            pltpu.VMEM((2, nc, nfl, ext_rows, ncol), jnp.float32),
            pltpu.VMEM((3, 4, ext_rows, ncol), jnp.float32),
            pltpu.VMEM((NDEPTH, own, ncol), jnp.float32),
            pltpu.VMEM((n_freq, NDEPTH, own, block), jnp.float32),
            pltpu.SMEM((filter_coeffs.shape[2], filter_coeffs.shape[0], filter_coeffs.shape[1]), jnp.float32),
            pltpu.VMEM((nfl, ORDER + 1, 2, ext_rows, ncol), jnp.float32),
            pltpu.VMEM((nfl, ORDER + 1, 2, own, ncol), jnp.float32),
            pltpu.SemaphoreType.DMA((4,)),
            pltpu.SemaphoreType.DMA((3 * n_freq + 6 + NDEPTH * n_freq,)),
            pltpu.SemaphoreType.DMA((3 * n_freq + 6 + NDEPTH * n_freq,)),
        ],
        compiler_params=pltpu.CompilerParams(collective_id=0, has_side_effects=True),
        cost_estimate=pl.CostEstimate(flops=elements * 100, bytes_accessed=elements * 4, transcendentals=0),
    )(aperture, order_table, frequency, jnp.transpose(filter_coeffs, (2, 0, 1)), source_field, receiver_field, slowness)
    return pl.pallas_call(
        passthrough_kernel,
        out_shape=(
            jax.ShapeDtypeStruct(image_out.shape, jnp.float32),
            jax.ShapeDtypeStruct(rec_out.shape, jnp.float32),
        ),
        in_specs=[pl.BlockSpec(memory_space=VMEM)] * 2,
        out_specs=(pl.BlockSpec(memory_space=VMEM), pl.BlockSpec(memory_space=VMEM)),
    )(image_out, rec_out)


def passthrough_kernel(img_in, rec_in, img_out, rec_out):
    img_out[...] = img_in[...]
    rec_out[...] = rec_in[...]


def solution(mesh):
    placed = (
        P(None, "freq", "tile", None),
        P(None, "freq", "tile", None),
        P(None, "tile", "freq"),
        P("freq"),
        P(None, "freq"),
        P(),
        P(),
    )
    return jax.shard_map(
        functools.partial(shards, mesh.shape["tile"], mesh.shape["freq"]),
        mesh=mesh,
        in_specs=placed,
        out_specs=(P(None, "tile", "freq"), P(None, "freq", "tile", None)),
        check_vma=False,
    )
```

```python
import functools

import jax
import jax.numpy as jnp
from jax import lax
from jax.experimental import pallas as pl
from jax.experimental.pallas import tpu as pltpu
from jax.sharding import PartitionSpec as P

ORDER = 4
NDEPTH = 2
POWERS = 3
HALO = 8
MESH = pl.DeviceIdType.MESH
VMEM = pltpu.MemorySpace.VMEM
SMEM = pltpu.MemorySpace.SMEM


def migrate_kernel(n_tile, n_freq, period, aperture, orders, frequency, coeffs_hbm, src_hbm, rec_hbm, slow_hbm,
                   rec_out, image_out, src_v, rec_v, g_slow, h_sa, h_sb, h_fa, h_fb, up_buf, s_up, s1, tb, img_out,
                   got, coeffs, cf0, cf1, local_sem, send_sem, recv_sem):
    t = lax.axis_index("tile")
    f = lax.axis_index("freq")
    nc, nfl, own, ncol = src_v.shape
    ext_rows = HALO + own + HALO
    block = slow_hbm.shape[2]
    ap = aperture[t]
    has_above = t > 0
    has_below = t < n_tile - 1

    loads = (
        pltpu.make_async_copy(src_hbm, src_v, local_sem.at[0]),
        pltpu.make_async_copy(rec_hbm, rec_v, local_sem.at[1]),
        pltpu.make_async_copy(slow_hbm, g_slow.at[f], local_sem.at[2]),
        pltpu.make_async_copy(coeffs_hbm, coeffs, local_sem.at[3]),
    )
    for copy in loads:
        copy.start()

    @pl.when(t == 0)
    def _():
        h_fa[...] = jnp.zeros_like(h_fa)
        h_sa[...] = jnp.zeros_like(h_sa)

    @pl.when(t == n_tile - 1)
    def _():
        h_fb[...] = jnp.zeros_like(h_fb)
        h_sb[...] = jnp.zeros_like(h_sb)

    barrier = pltpu.get_barrier_semaphore()
    for q in range(n_freq):
        @pl.when(f != q)
        def _():
            pl.semaphore_signal(barrier, 1, device_id=(t, q), device_id_type=MESH)

        @pl.when(has_above)
        def _():
            pl.semaphore_signal(barrier, 1, device_id=(t - 1, q), device_id_type=MESH)

        @pl.when(has_below)
        def _():
            pl.semaphore_signal(barrier, 1, device_id=(t + 1, q), device_id_type=MESH)

    expected = (n_freq - 1) + n_freq * has_above.astype(jnp.int32) + n_freq * has_below.astype(jnp.int32)

    for copy in loads:
        copy.wait()

    own_rows = lax.broadcasted_iota(jnp.int32, (own, ncol), 0)
    own_forward = pltpu.roll(own_rows, 1, 0) == (own_rows + own - 1) % own
    lift = (own + HALO - ap) % own
    drop = ap - HALO

    def last_rows(x, forward):
        return jnp.where(forward, pltpu.roll(x, lift, 0), pltpu.roll(x, drop, 0))[:HALO]

    s_up[...] = last_rows(g_slow[f, 0], own_forward[:, :block])
    fields_v = (src_v, rec_v)
    for fi in range(nfl):
        for x in range(2):
            for c in range(nc):
                up_buf[x, c, fi] = last_rows(fields_v[x][c, fi], own_forward)

    pl.semaphore_wait(barrier, expected)

    def remote(src, dst, slot_send, slot_recv, device):
        return pltpu.make_async_remote_copy(
            src_ref=src, dst_ref=dst, send_sem=send_sem.at[slot_send], recv_sem=recv_sem.at[slot_recv],
            device_id=device, device_id_type=MESH,
        )

    f_lo = (src_hbm.at[:, :, pl.ds(0, HALO), :], rec_hbm.at[:, :, pl.ds(0, HALO), :])
    s_lo = slow_hbm.at[0, pl.ds(0, HALO), :]
    for q in range(n_freq):
        @pl.when(f != q)
        def _():
            remote(slow_hbm, g_slow.at[f], q, f, (t, q)).start()

        @pl.when(has_above)
        def _():
            remote(s_lo, h_sb.at[f], 2 * n_freq + q, 2 * n_freq + f, (t - 1, q)).start()

    field_base = 3 * n_freq

    def lower_copy(x, fi, device):
        return remote(f_lo[x].at[:, fi], h_fb.at[x, :, fi], field_base + 2 + 2 * x + fi,
                      field_base + 2 + 2 * x + fi, device)

    def upper_copy(fi, device):
        return remote(up_buf.at[:, :, fi], h_fa.at[:, :, fi], field_base + fi, field_base + fi, device)

    def start_lower():
        for fi in range(nfl):
            @pl.when(has_above)
            def _():
                for x in range(2):
                    lower_copy(x, fi, (t - 1, f)).start()

    def start_upper():
        for q in range(n_freq):
            @pl.when(has_below)
            def _():
                remote(s_up, h_sa.at[f], n_freq + q, n_freq + f, (t + 1, q)).start()

        for fi in range(nfl):
            @pl.when(has_below)
            def _():
                upper_copy(fi, (t + 1, f)).start()

    far_above = (t % period == period - 1) if period else t < 0

    @pl.when(far_above)
    def _():
        start_upper()
        start_lower()

    @pl.when(jnp.logical_not(far_above))
    def _():
        start_lower()
        start_upper()

    for q in range(n_freq):
        @pl.when(f != q)
        def _():
            remote(slow_hbm, g_slow.at[q], q, q, (t, q)).wait_send()
            remote(slow_hbm, g_slow.at[q], q, q, (t, q)).wait_recv()

        @pl.when(has_below)
        def _():
            remote(s_up, h_sa.at[q], n_freq + q, n_freq + q, (t + 1, q)).wait_send()
            remote(s_lo, h_sb.at[q], 2 * n_freq + q, 2 * n_freq + q, (t + 1, q)).wait_recv()

        @pl.when(has_above)
        def _():
            remote(s_lo, h_sb.at[q], 2 * n_freq + q, 2 * n_freq + q, (t - 1, q)).wait_send()
            remote(s_up, h_sa.at[q], n_freq + q, n_freq + q, (t - 1, q)).wait_recv()

    def await_fields(fi):
        @pl.when(has_below)
        def _():
            upper_copy(fi, (t + 1, f)).wait_send()
            for x in range(2):
                lower_copy(x, fi, (t + 1, f)).wait_recv()

        @pl.when(has_above)
        def _():
            for x in range(2):
                lower_copy(x, fi, (t - 1, f)).wait_send()
            upper_copy(fi, (t - 1, f)).wait_recv()

    rows = lax.broadcasted_iota(jnp.int32, (ext_rows, ncol), 0)
    cols = lax.broadcasted_iota(jnp.int32, (ext_rows, ncol), 1)
    left_ok = jnp.abs(pltpu.roll(cols, 1, 1) - cols) == 1
    right_ok = jnp.abs(pltpu.roll(cols, ncol - 1, 1) - cols) == 1
    forward = pltpu.roll(rows, 1, 0) == (rows + ext_rows - 1) % ext_rows
    lower_start = HALO + ap
    top_part = rows < lower_start

    def in_band(lo, hi):
        return (rows >= lo) & (rows < hi)

    valid0 = (in_band(0, HALO) & has_above) | in_band(HALO, lower_start) | (
        in_band(lower_start, lower_start + HALO) & has_below)
    reach = HALO // 2
    valid1 = (in_band(HALO - reach, HALO) & has_above) | in_band(HALO, lower_start) | (
        in_band(lower_start, lower_start + reach) & has_below)
    live = lax.broadcasted_iota(jnp.int32, (own, ncol), 0) < ap
    zeros_tail = jnp.zeros((ext_rows - HALO, ncol), jnp.float32)

    def place_lower(lower8):
        padded = jnp.concatenate([lower8, zeros_tail], axis=0)
        ahead = pltpu.roll(padded, lower_start, 0)
        behind = pltpu.roll(padded, ext_rows - lower_start, 0)
        return jnp.where(forward, ahead, behind)

    def joined(upper8, own_rows, lower8):
        top = jnp.concatenate([upper8, own_rows, jnp.zeros((HALO, ncol), jnp.float32)], axis=0)
        return jnp.where(top_part, top, place_lower(lower8))

    def columns_of(pieces):
        return jnp.concatenate(pieces, axis=1)

    slow0 = joined(
        columns_of([h_sa[q] for q in range(n_freq)]),
        columns_of([g_slow[q, 0] for q in range(n_freq)]),
        columns_of([h_sb[q] for q in range(n_freq)]),
    )
    slow0 = jnp.where(valid0, slow0, 0.0)
    slow1 = columns_of([g_slow[q, 1] for q in range(n_freq)])

    edge = 128

    def masked_side(b):
        ahead = pltpu.roll(b, 1, 1)
        behind = pltpu.roll(b, ncol - 1, 1)

        def guarded(lo, hi):
            return jnp.where(left_ok[:, lo:hi], ahead[:, lo:hi], 0.0) + jnp.where(
                right_ok[:, lo:hi], behind[:, lo:hi], 0.0)

        middle = ahead[:, edge:ncol - edge] + behind[:, edge:ncol - edge]
        return jnp.concatenate([guarded(0, edge), middle, guarded(ncol - edge, ncol)], axis=1)

    def chebyshev_step(v, prev):
        pair = pltpu.roll(v, 1, 0) + pltpu.roll(v, ext_rows - 1, 0)
        blur = 0.25 * pair + 0.5 * v
        side = masked_side(blur)
        if prev is None:
            return 0.5 * side + blur - v
        return side + 0.5 * pair - v - prev

    def coefficient_of(depth, fi, n, wavenumber):
        active = jnp.where(orders[depth, fi] >= n, 1.0, 0.0).astype(jnp.float32)
        scaled = [[coeffs[m, c, n] * active for m in range(POWERS)] for c in range(2)]
        coef_re = scaled[0][POWERS - 1] * wavenumber + scaled[0][POWERS - 2]
        coef_im = scaled[1][POWERS - 1] * wavenumber + scaled[1][POWERS - 2]
        for m in range(POWERS - 3, -1, -1):
            coef_re = coef_re * wavenumber + scaled[0][m]
            coef_im = coef_im * wavenumber + scaled[1][m]
        return coef_re, coef_im

    for fi in range(nfl):
        wave0 = frequency[fi] * slow0
        wave1 = frequency[fi] * slow1
        for n in range(ORDER + 1):
            cf0[fi, n, 0], cf0[fi, n, 1] = coefficient_of(0, fi, n, wave0)
            cf1[fi, n, 0], cf1[fi, n, 1] = coefficient_of(1, fi, n, wave1)

    def coefficient(depth, fi, n, wavenumber):
        table = cf0 if depth == 0 else cf1
        return table[fi, n, 0], table[fi, n, 1]

    def extrapolate(depth, fi, wavenumber, valid, lo, hi, write):
        for n in range(ORDER + 1):
            slot = n % 3
            if n >= 1:
                cur, prev = (n - 1) % 3, (n - 2) % 3
                for p in range(4):
                    g = chebyshev_step(tb[cur, p], tb[prev, p] if n > 1 else None)
                    tb[slot, p] = jnp.where(valid, g, 0.0)
            coef_re, coef_im = coefficient(depth, fi, n, wavenumber)
            s_re = tb[slot, 0, lo:hi, :]
            s_im = tb[slot, 1, lo:hi, :]
            r_re = tb[slot, 2, lo:hi, :]
            r_im = tb[slot, 3, lo:hi, :]
            terms = (
                coef_re * s_re + coef_im * s_im,
                coef_re * s_im - coef_im * s_re,
                coef_re * r_re - coef_im * r_im,
                coef_re * r_im + coef_im * r_re,
            )
            write(n, terms)

    fields = (src_v, rec_v)
    for fi in range(nfl):
        await_fields(fi)
        for p in range(4):
            x, c = p // 2, p % 2
            tb[0, p] = jnp.where(valid0, joined(h_fa[x, c, fi], fields[x][c, fi], h_fb[x, c, fi]), 0.0)

        def write0(n, terms, fi=fi):
            for p in range(4):
                if n == 0:
                    s1[p // 2, p % 2, fi] = terms[p]
                else:
                    s1[p // 2, p % 2, fi] = s1[p // 2, p % 2, fi] + terms[p]

        extrapolate(0, fi, frequency[fi] * slow0, valid0, 0, ext_rows, write0)
        for p in range(4):
            s1[p // 2, p % 2, fi] = jnp.where(valid1, s1[p // 2, p % 2, fi], 0.0)
        mid = slice(HALO, HALO + own)
        term = s1[0, 0, fi, mid, :] * s1[1, 0, fi, mid, :] + s1[0, 1, fi, mid, :] * s1[1, 1, fi, mid, :]
        term = jnp.where(live, term, 0.0)
        if fi == 0:
            img_out[0] = term
        else:
            img_out[0] = img_out[0] + term

    image_base = 3 * n_freq + 6

    def image_copy(depth, q, slot_recv, device):
        return pltpu.make_async_remote_copy(
            src_ref=img_out.at[depth, :, pl.ds(q * block, block)], dst_ref=got.at[slot_recv, depth],
            send_sem=send_sem.at[image_base + depth * n_freq + q],
            recv_sem=recv_sem.at[image_base + depth * n_freq + slot_recv],
            device_id=device, device_id_type=MESH,
        )

    def send_image(depth):
        for q in range(n_freq):
            @pl.when(f != q)
            def _():
                image_copy(depth, q, f, (t, q)).start()

    send_image(0)

    for fi in range(nfl):
        for p in range(4):
            tb[0, p] = s1[p // 2, p % 2, fi]
        acc = {}

        def write1(n, terms, acc=acc):
            for p in range(4):
                acc[p] = terms[p] if n == 0 else acc[p] + terms[p]

        extrapolate(1, fi, frequency[fi] * slow1, valid1, HALO, HALO + own, write1)
        result = [jnp.where(live, acc[p], 0.0) for p in range(4)]
        rec_out[0, fi] = result[2]
        rec_out[1, fi] = result[3]
        term = result[0] * result[2] + result[1] * result[3]
        if fi == 0:
            img_out[1] = term
        else:
            img_out[1] = img_out[1] + term

    send_image(1)
    for depth in range(NDEPTH):
        for q in range(n_freq):
            @pl.when(f != q)
            def _():
                image_copy(depth, q, q, (t, q)).wait_send()
                image_copy(depth, q, q, (t, q)).wait_recv()

    total = None
    for q in range(n_freq):
        mine = img_out[:, :, q * block:(q + 1) * block]
        part = jnp.where(f == q, mine, got[q])
        total = part if total is None else total + part
    image_out[...] = total


def shards(n_tile, n_freq, period, source_field, receiver_field, slowness, frequency, order_table, filter_coeffs, aperture):
    nc, nfl, own, ncol = source_field.shape
    block = slowness.shape[2]
    ext_rows = own + 2 * HALO
    elements = nc * nfl * 2 * ext_rows * ncol * NDEPTH
    rec_out, image_out = pl.pallas_call(
        functools.partial(migrate_kernel, n_tile, n_freq, period),
        out_shape=(
            jax.ShapeDtypeStruct((nc, nfl, own, ncol), jnp.float32),
            jax.ShapeDtypeStruct((NDEPTH, own, block), jnp.float32),
        ),
        in_specs=[pl.BlockSpec(memory_space=SMEM)] * 3 + [pl.BlockSpec(memory_space=pl.ANY)] * 4,
        out_specs=(pl.BlockSpec(memory_space=VMEM), pl.BlockSpec(memory_space=VMEM)),
        scratch_shapes=[
            pltpu.VMEM((nc, nfl, own, ncol), jnp.float32),
            pltpu.VMEM((nc, nfl, own, ncol), jnp.float32),
            pltpu.VMEM((n_freq, NDEPTH, own, block), jnp.float32),
            pltpu.VMEM((n_freq, HALO, block), jnp.float32),
            pltpu.VMEM((n_freq, HALO, block), jnp.float32),
            pltpu.VMEM((2, nc, nfl, HALO, ncol), jnp.float32),
            pltpu.VMEM((2, nc, nfl, HALO, ncol), jnp.float32),
            pltpu.VMEM((2, nc, nfl, HALO, ncol), jnp.float32),
            pltpu.VMEM((HALO, block), jnp.float32),
            pltpu.VMEM((2, nc, nfl, ext_rows, ncol), jnp.float32),
            pltpu.VMEM((3, 4, ext_rows, ncol), jnp.float32),
            pltpu.VMEM((NDEPTH, own, ncol), jnp.float32),
            pltpu.VMEM((n_freq, NDEPTH, own, block), jnp.float32),
            pltpu.SMEM((filter_coeffs.shape[2], filter_coeffs.shape[0], filter_coeffs.shape[1]), jnp.float32),
            pltpu.VMEM((nfl, ORDER + 1, 2, ext_rows, ncol), jnp.float32),
            pltpu.VMEM((nfl, ORDER + 1, 2, own, ncol), jnp.float32),
            pltpu.SemaphoreType.DMA((4,)),
            pltpu.SemaphoreType.DMA((3 * n_freq + 6 + NDEPTH * n_freq,)),
            pltpu.SemaphoreType.DMA((3 * n_freq + 6 + NDEPTH * n_freq,)),
        ],
        compiler_params=pltpu.CompilerParams(collective_id=0, has_side_effects=True),
        cost_estimate=pl.CostEstimate(flops=elements * 100, bytes_accessed=elements * 4, transcendentals=0),
    )(aperture, order_table, frequency, jnp.transpose(filter_coeffs, (2, 0, 1)), source_field, receiver_field, slowness)
    return pl.pallas_call(
        passthrough_kernel,
        out_shape=(
            jax.ShapeDtypeStruct(image_out.shape, jnp.float32),
            jax.ShapeDtypeStruct(rec_out.shape, jnp.float32),
        ),
        in_specs=[pl.BlockSpec(memory_space=VMEM)] * 2,
        out_specs=(pl.BlockSpec(memory_space=VMEM), pl.BlockSpec(memory_space=VMEM)),
    )(image_out, rec_out)


def passthrough_kernel(img_in, rec_in, img_out, rec_out):
    img_out[...] = img_in[...]
    rec_out[...] = rec_in[...]


def relay_period(mesh):
    devices = mesh.devices
    n_tile, n_freq = devices.shape
    if n_freq % 2:
        return 0
    try:
        xs = [[d.coords[0] for d in row] for row in devices]
        cores = [[d.core_on_chip for d in row] for row in devices]
        ring = max(max(r) for r in xs) + 1
    except AttributeError:
        return 0
    crossing = []
    for t in range(n_tile - 1):
        gaps = {min((xs[t][q] - xs[t + 1][q]) % ring, (xs[t + 1][q] - xs[t][q]) % ring) for q in range(n_freq)}
        crossing.append(gaps == {2})
    if not any(crossing):
        return 0
    period = crossing.index(True) + 1
    if crossing != [t % period == period - 1 for t in range(n_tile - 1)]:
        return 0
    for t in range(n_tile):
        for q in range(n_freq):
            p = (q + n_freq // 2) % n_freq
            if cores[t][p] != cores[t][q] or xs[t][p] == xs[t][q]:
                return 0
    return period


def solution(mesh):
    placed = (
        P(None, "freq", "tile", None),
        P(None, "freq", "tile", None),
        P(None, "tile", "freq"),
        P("freq"),
        P(None, "freq"),
        P(),
        P(),
    )
    return jax.shard_map(
        functools.partial(shards, mesh.shape["tile"], mesh.shape["freq"], relay_period(mesh)),
        mesh=mesh,
        in_specs=placed,
        out_specs=(P(None, "tile", "freq"), P(None, "freq", "tile", None)),
        check_vma=False,
    )
```

```python
import functools

import jax
import jax.numpy as jnp
from jax import lax
from jax.experimental import pallas as pl
from jax.experimental.pallas import tpu as pltpu
from jax.sharding import PartitionSpec as P

ORDER = 4
NDEPTH = 2
POWERS = 3
HALO = 8
MESH = pl.DeviceIdType.MESH
VMEM = pltpu.MemorySpace.VMEM
SMEM = pltpu.MemorySpace.SMEM


def migrate_kernel(n_tile, n_freq, period, aperture, orders, frequency, coeffs_hbm, src_hbm, rec_hbm, slow_hbm,
                   rec_out, image_out, src_v, rec_v, g_slow, h_sa, h_sb, h_fa, h_fb, up_buf, s_up, s1, tb, img_out,
                   got, coeffs, cf0, cf1, local_sem, send_sem, recv_sem):
    t = lax.axis_index("tile")
    f = lax.axis_index("freq")
    nc, nfl, own, ncol = src_v.shape
    ext_rows = HALO + own + HALO
    block = slow_hbm.shape[2]
    ap = aperture[t]
    has_above = t > 0
    has_below = t < n_tile - 1

    loads = (
        pltpu.make_async_copy(src_hbm, src_v, local_sem.at[0]),
        pltpu.make_async_copy(rec_hbm, rec_v, local_sem.at[1]),
        pltpu.make_async_copy(slow_hbm, g_slow.at[f], local_sem.at[2]),
        pltpu.make_async_copy(coeffs_hbm, coeffs, local_sem.at[3]),
    )
    for copy in loads:
        copy.start()

    @pl.when(t == 0)
    def _():
        h_fa[...] = jnp.zeros_like(h_fa)
        h_sa[...] = jnp.zeros_like(h_sa)

    @pl.when(t == n_tile - 1)
    def _():
        h_fb[...] = jnp.zeros_like(h_fb)
        h_sb[...] = jnp.zeros_like(h_sb)

    barrier = pltpu.get_barrier_semaphore()
    for q in range(n_freq):
        @pl.when(f != q)
        def _():
            pl.semaphore_signal(barrier, 1, device_id=(t, q), device_id_type=MESH)

        @pl.when(has_above)
        def _():
            pl.semaphore_signal(barrier, 1, device_id=(t - 1, q), device_id_type=MESH)

        @pl.when(has_below)
        def _():
            pl.semaphore_signal(barrier, 1, device_id=(t + 1, q), device_id_type=MESH)

    expected = (n_freq - 1) + n_freq * has_above.astype(jnp.int32) + n_freq * has_below.astype(jnp.int32)

    for copy in loads:
        copy.wait()

    own_rows = lax.broadcasted_iota(jnp.int32, (own, ncol), 0)
    own_forward = pltpu.roll(own_rows, 1, 0) == (own_rows + own - 1) % own
    lift = (own + HALO - ap) % own
    drop = ap - HALO

    def last_rows(x, forward):
        return jnp.where(forward, pltpu.roll(x, lift, 0), pltpu.roll(x, drop, 0))[:HALO]

    s_up[...] = last_rows(g_slow[f, 0], own_forward[:, :block])
    fields_v = (src_v, rec_v)
    for fi in range(nfl):
        for x in range(2):
            for c in range(nc):
                up_buf[x, c, fi] = last_rows(fields_v[x][c, fi], own_forward)

    pl.semaphore_wait(barrier, expected)

    def remote(src, dst, slot_send, slot_recv, device):
        return pltpu.make_async_remote_copy(
            src_ref=src, dst_ref=dst, send_sem=send_sem.at[slot_send], recv_sem=recv_sem.at[slot_recv],
            device_id=device, device_id_type=MESH,
        )

    f_lo = (src_hbm.at[:, :, pl.ds(0, HALO), :], rec_hbm.at[:, :, pl.ds(0, HALO), :])
    s_lo = slow_hbm.at[0, pl.ds(0, HALO), :]
    for q in range(n_freq):
        @pl.when(f != q)
        def _():
            remote(slow_hbm, g_slow.at[f], q, f, (t, q)).start()

        @pl.when(has_above)
        def _():
            remote(s_lo, h_sb.at[f], 2 * n_freq + q, 2 * n_freq + f, (t - 1, q)).start()

    field_base = 3 * n_freq

    def lower_copy(x, fi, device):
        return remote(f_lo[x].at[:, fi], h_fb.at[x, :, fi], field_base + 2 + 2 * x + fi,
                      field_base + 2 + 2 * x + fi, device)

    def upper_copy(fi, device):
        return remote(up_buf.at[:, :, fi], h_fa.at[:, :, fi], field_base + fi, field_base + fi, device)

    def start_lower():
        for fi in range(nfl):
            @pl.when(has_above)
            def _():
                for x in range(2):
                    lower_copy(x, fi, (t - 1, f)).start()

    def start_upper():
        for q in range(n_freq):
            @pl.when(has_below)
            def _():
                remote(s_up, h_sa.at[f], n_freq + q, n_freq + f, (t + 1, q)).start()

        for fi in range(nfl):
            @pl.when(has_below)
            def _():
                upper_copy(fi, (t + 1, f)).start()

    far_above = (t % period == period - 1) if period else t < 0

    @pl.when(far_above)
    def _():
        start_upper()
        start_lower()

    @pl.when(jnp.logical_not(far_above))
    def _():
        start_lower()
        start_upper()

    for q in range(n_freq):
        @pl.when(f != q)
        def _():
            remote(slow_hbm, g_slow.at[q], q, q, (t, q)).wait_send()
            remote(slow_hbm, g_slow.at[q], q, q, (t, q)).wait_recv()

        @pl.when(has_below)
        def _():
            remote(s_up, h_sa.at[q], n_freq + q, n_freq + q, (t + 1, q)).wait_send()
            remote(s_lo, h_sb.at[q], 2 * n_freq + q, 2 * n_freq + q, (t + 1, q)).wait_recv()

        @pl.when(has_above)
        def _():
            remote(s_lo, h_sb.at[q], 2 * n_freq + q, 2 * n_freq + q, (t - 1, q)).wait_send()
            remote(s_up, h_sa.at[q], n_freq + q, n_freq + q, (t - 1, q)).wait_recv()

    def await_fields(fi):
        @pl.when(has_below)
        def _():
            upper_copy(fi, (t + 1, f)).wait_send()
            for x in range(2):
                lower_copy(x, fi, (t + 1, f)).wait_recv()

        @pl.when(has_above)
        def _():
            for x in range(2):
                lower_copy(x, fi, (t - 1, f)).wait_send()
            upper_copy(fi, (t - 1, f)).wait_recv()

    rows = lax.broadcasted_iota(jnp.int32, (ext_rows, ncol), 0)
    cols = lax.broadcasted_iota(jnp.int32, (ext_rows, ncol), 1)
    left_ok = jnp.abs(pltpu.roll(cols, 1, 1) - cols) == 1
    right_ok = jnp.abs(pltpu.roll(cols, ncol - 1, 1) - cols) == 1
    forward = pltpu.roll(rows, 1, 0) == (rows + ext_rows - 1) % ext_rows
    lower_start = HALO + ap
    top_part = rows < lower_start

    def in_band(lo, hi):
        return (rows >= lo) & (rows < hi)

    valid0 = (in_band(0, HALO) & has_above) | in_band(HALO, lower_start) | (
        in_band(lower_start, lower_start + HALO) & has_below)
    reach = HALO // 2
    valid1 = (in_band(HALO - reach, HALO) & has_above) | in_band(HALO, lower_start) | (
        in_band(lower_start, lower_start + reach) & has_below)
    live = lax.broadcasted_iota(jnp.int32, (own, ncol), 0) < ap
    zeros_tail = jnp.zeros((ext_rows - HALO, ncol), jnp.float32)

    def place_lower(lower8):
        padded = jnp.concatenate([lower8, zeros_tail], axis=0)
        ahead = pltpu.roll(padded, lower_start, 0)
        behind = pltpu.roll(padded, ext_rows - lower_start, 0)
        return jnp.where(forward, ahead, behind)

    def joined(upper8, own_rows, lower8):
        top = jnp.concatenate([upper8, own_rows, jnp.zeros((HALO, ncol), jnp.float32)], axis=0)
        return jnp.where(top_part, top, place_lower(lower8))

    def columns_of(pieces):
        return jnp.concatenate(pieces, axis=1)

    slow0 = joined(
        columns_of([h_sa[q] for q in range(n_freq)]),
        columns_of([g_slow[q, 0] for q in range(n_freq)]),
        columns_of([h_sb[q] for q in range(n_freq)]),
    )
    slow0 = jnp.where(valid0, slow0, 0.0)
    slow1 = columns_of([g_slow[q, 1] for q in range(n_freq)])

    edge = 128

    def masked_side(b):
        ahead = pltpu.roll(b, 1, 1)
        behind = pltpu.roll(b, ncol - 1, 1)

        def guarded(lo, hi):
            return jnp.where(left_ok[:, lo:hi], ahead[:, lo:hi], 0.0) + jnp.where(
                right_ok[:, lo:hi], behind[:, lo:hi], 0.0)

        middle = ahead[:, edge:ncol - edge] + behind[:, edge:ncol - edge]
        return jnp.concatenate([guarded(0, edge), middle, guarded(ncol - edge, ncol)], axis=1)

    def chebyshev_step(v, prev):
        pair = pltpu.roll(v, 1, 0) + pltpu.roll(v, ext_rows - 1, 0)
        blur = 0.25 * pair + 0.5 * v
        side = masked_side(blur)
        if prev is None:
            return 0.5 * side + blur - v
        return side + 0.5 * pair - v - prev

    def coefficient_of(depth, fi, n, wavenumber):
        active = jnp.where(orders[depth, fi] >= n, 1.0, 0.0).astype(jnp.float32)
        scaled = [[coeffs[m, c, n] * active for m in range(POWERS)] for c in range(2)]
        coef_re = scaled[0][POWERS - 1] * wavenumber + scaled[0][POWERS - 2]
        coef_im = scaled[1][POWERS - 1] * wavenumber + scaled[1][POWERS - 2]
        for m in range(POWERS - 3, -1, -1):
            coef_re = coef_re * wavenumber + scaled[0][m]
            coef_im = coef_im * wavenumber + scaled[1][m]
        return coef_re, coef_im

    for fi in range(nfl):
        wave0 = frequency[fi] * slow0
        wave1 = frequency[fi] * slow1
        for n in range(ORDER + 1):
            cf0[fi, n, 0], cf0[fi, n, 1] = coefficient_of(0, fi, n, wave0)
            cf1[fi, n, 0], cf1[fi, n, 1] = coefficient_of(1, fi, n, wave1)

    def coefficient(depth, fi, n, wavenumber):
        table = cf0 if depth == 0 else cf1
        return table[fi, n, 0], table[fi, n, 1]

    def extrapolate(depth, fi, wavenumber, valid, lo, hi, write):
        for n in range(ORDER + 1):
            slot = n % 3
            if n >= 1:
                cur, prev = (n - 1) % 3, (n - 2) % 3
                for p in range(4):
                    g = chebyshev_step(tb[cur, p], tb[prev, p] if n > 1 else None)
                    tb[slot, p] = jnp.where(valid, g, 0.0)
            coef_re, coef_im = coefficient(depth, fi, n, wavenumber)
            s_re = tb[slot, 0, lo:hi, :]
            s_im = tb[slot, 1, lo:hi, :]
            r_re = tb[slot, 2, lo:hi, :]
            r_im = tb[slot, 3, lo:hi, :]
            terms = (
                coef_re * s_re + coef_im * s_im,
                coef_re * s_im - coef_im * s_re,
                coef_re * r_re - coef_im * r_im,
                coef_re * r_im + coef_im * r_re,
            )
            write(n, terms)

    fields = (src_v, rec_v)
    for fi in range(nfl):
        await_fields(fi)
        for p in range(4):
            x, c = p // 2, p % 2
            tb[0, p] = jnp.where(valid0, joined(h_fa[x, c, fi], fields[x][c, fi], h_fb[x, c, fi]), 0.0)

        def write0(n, terms, fi=fi):
            for p in range(4):
                if n == 0:
                    s1[p // 2, p % 2, fi] = terms[p]
                else:
                    s1[p // 2, p % 2, fi] = s1[p // 2, p % 2, fi] + terms[p]

        extrapolate(0, fi, frequency[fi] * slow0, valid0, 0, ext_rows, write0)
        for p in range(4):
            s1[p // 2, p % 2, fi] = jnp.where(valid1, s1[p // 2, p % 2, fi], 0.0)
        mid = slice(HALO, HALO + own)
        term = s1[0, 0, fi, mid, :] * s1[1, 0, fi, mid, :] + s1[0, 1, fi, mid, :] * s1[1, 1, fi, mid, :]
        term = jnp.where(live, term, 0.0)
        if fi == 0:
            img_out[0] = term
        else:
            img_out[0] = img_out[0] + term

    image_base = 3 * n_freq + 6

    def image_copy(depth, q, slot_recv, device):
        return pltpu.make_async_remote_copy(
            src_ref=img_out.at[depth, :, pl.ds(q * block, block)], dst_ref=got.at[slot_recv, depth],
            send_sem=send_sem.at[image_base + depth * n_freq + q],
            recv_sem=recv_sem.at[image_base + depth * n_freq + slot_recv],
            device_id=device, device_id_type=MESH,
        )

    def send_image(depth):
        for q in range(n_freq):
            @pl.when(f != q)
            def _():
                image_copy(depth, q, f, (t, q)).start()

    send_image(0)

    for fi in range(nfl):
        for p in range(4):
            tb[0, p] = s1[p // 2, p % 2, fi]
        acc = {}

        def write1(n, terms, acc=acc):
            for p in range(4):
                acc[p] = terms[p] if n == 0 else acc[p] + terms[p]

        extrapolate(1, fi, frequency[fi] * slow1, valid1, HALO, HALO + own, write1)
        result = [jnp.where(live, acc[p], 0.0) for p in range(4)]
        rec_out[0, fi] = result[2]
        rec_out[1, fi] = result[3]
        term = result[0] * result[2] + result[1] * result[3]
        if fi == 0:
            img_out[1] = term
        else:
            img_out[1] = img_out[1] + term

    send_image(1)
    for depth in range(NDEPTH):
        for q in range(n_freq):
            @pl.when(f != q)
            def _():
                image_copy(depth, q, q, (t, q)).wait_send()
                image_copy(depth, q, q, (t, q)).wait_recv()

    total = None
    for q in range(n_freq):
        mine = img_out[:, :, q * block:(q + 1) * block]
        part = jnp.where(f == q, mine, got[q])
        total = part if total is None else total + part
    image_out[...] = total


def shards(n_tile, n_freq, period, source_field, receiver_field, slowness, frequency, order_table, filter_coeffs, aperture):
    nc, nfl, own, ncol = source_field.shape
    block = slowness.shape[2]
    ext_rows = own + 2 * HALO
    elements = nc * nfl * 2 * ext_rows * ncol * NDEPTH
    rec_out, image_out = pl.pallas_call(
        functools.partial(migrate_kernel, n_tile, n_freq, period),
        out_shape=(
            jax.ShapeDtypeStruct((nc, nfl, own, ncol), jnp.float32),
            jax.ShapeDtypeStruct((NDEPTH, own, block), jnp.float32),
        ),
        in_specs=[pl.BlockSpec(memory_space=SMEM)] * 3 + [pl.BlockSpec(memory_space=pl.ANY)] * 4,
        out_specs=(pl.BlockSpec(memory_space=VMEM), pl.BlockSpec(memory_space=VMEM)),
        scratch_shapes=[
            pltpu.VMEM((nc, nfl, own, ncol), jnp.float32),
            pltpu.VMEM((nc, nfl, own, ncol), jnp.float32),
            pltpu.VMEM((n_freq, NDEPTH, own, block), jnp.float32),
            pltpu.VMEM((n_freq, HALO, block), jnp.float32),
            pltpu.VMEM((n_freq, HALO, block), jnp.float32),
            pltpu.VMEM((2, nc, nfl, HALO, ncol), jnp.float32),
            pltpu.VMEM((2, nc, nfl, HALO, ncol), jnp.float32),
            pltpu.VMEM((2, nc, nfl, HALO, ncol), jnp.float32),
            pltpu.VMEM((HALO, block), jnp.float32),
            pltpu.VMEM((2, nc, nfl, ext_rows, ncol), jnp.float32),
            pltpu.VMEM((3, 4, ext_rows, ncol), jnp.float32),
            pltpu.VMEM((NDEPTH, own, ncol), jnp.float32),
            pltpu.VMEM((n_freq, NDEPTH, own, block), jnp.float32),
            pltpu.SMEM((filter_coeffs.shape[2], filter_coeffs.shape[0], filter_coeffs.shape[1]), jnp.float32),
            pltpu.VMEM((nfl, ORDER + 1, 2, ext_rows, ncol), jnp.float32),
            pltpu.VMEM((nfl, ORDER + 1, 2, own, ncol), jnp.float32),
            pltpu.SemaphoreType.DMA((4,)),
            pltpu.SemaphoreType.DMA((3 * n_freq + 6 + NDEPTH * n_freq,)),
            pltpu.SemaphoreType.DMA((3 * n_freq + 6 + NDEPTH * n_freq,)),
        ],
        compiler_params=pltpu.CompilerParams(collective_id=0, has_side_effects=True),
        cost_estimate=pl.CostEstimate(flops=elements * 100, bytes_accessed=elements * 4, transcendentals=0),
    )(aperture, order_table, frequency, jnp.transpose(filter_coeffs, (2, 0, 1)), source_field, receiver_field, slowness)
    return pl.pallas_call(
        passthrough_kernel,
        out_shape=(
            jax.ShapeDtypeStruct(image_out.shape, jnp.float32),
            jax.ShapeDtypeStruct(rec_out.shape, jnp.float32),
        ),
        in_specs=[pl.BlockSpec(memory_space=pl.ANY)] * 2,
        out_specs=(pl.BlockSpec(memory_space=VMEM), pl.BlockSpec(memory_space=VMEM)),
        scratch_shapes=[pltpu.SemaphoreType.DMA((2,))],
    )(image_out, rec_out)


def passthrough_kernel(img_in, rec_in, img_out, rec_out, sems):
    copies = (
        pltpu.make_async_copy(img_in, img_out, sems.at[0]),
        pltpu.make_async_copy(rec_in, rec_out, sems.at[1]),
    )
    for copy in copies:
        copy.start()
    for copy in copies:
        copy.wait()


def relay_period(mesh):
    devices = mesh.devices
    n_tile, n_freq = devices.shape
    if n_freq % 2:
        return 0
    try:
        xs = [[d.coords[0] for d in row] for row in devices]
        cores = [[d.core_on_chip for d in row] for row in devices]
        ring = max(max(r) for r in xs) + 1
    except AttributeError:
        return 0
    crossing = []
    for t in range(n_tile - 1):
        gaps = {min((xs[t][q] - xs[t + 1][q]) % ring, (xs[t + 1][q] - xs[t][q]) % ring) for q in range(n_freq)}
        crossing.append(gaps == {2})
    if not any(crossing):
        return 0
    period = crossing.index(True) + 1
    if crossing != [t % period == period - 1 for t in range(n_tile - 1)]:
        return 0
    for t in range(n_tile):
        for q in range(n_freq):
            p = (q + n_freq // 2) % n_freq
            if cores[t][p] != cores[t][q] or xs[t][p] == xs[t][q]:
                return 0
    return period


def solution(mesh):
    placed = (
        P(None, "freq", "tile", None),
        P(None, "freq", "tile", None),
        P(None, "tile", "freq"),
        P("freq"),
        P(None, "freq"),
        P(),
        P(),
    )
    return jax.shard_map(
        functools.partial(shards, mesh.shape["tile"], mesh.shape["freq"], relay_period(mesh)),
        mesh=mesh,
        in_specs=placed,
        out_specs=(P(None, "tile", "freq"), P(None, "freq", "tile", None)),
        check_vma=False,
    )
```

```python
import functools

import jax
import jax.numpy as jnp
from jax import lax
from jax.experimental import pallas as pl
from jax.experimental.pallas import tpu as pltpu
from jax.sharding import PartitionSpec as P

ORDER = 4
NDEPTH = 2
POWERS = 3
HALO = 8
MESH = pl.DeviceIdType.MESH
VMEM = pltpu.MemorySpace.VMEM
SMEM = pltpu.MemorySpace.SMEM


def migrate_kernel(n_tile, n_freq, period, aperture, orders, frequency, coeffs_hbm, src_hbm, rec_hbm, slow_hbm,
                   rec_out, image_out, src_v, rec_v, g_slow, h_sa, h_sb, h_fa, h_fb, up_buf, s_up, s1, tb, img_out,
                   got, coeffs, cf0, cf1, local_sem, send_sem, recv_sem):
    t = lax.axis_index("tile")
    f = lax.axis_index("freq")
    nc, nfl, own, ncol = src_v.shape
    ext_rows = HALO + own + HALO
    block = slow_hbm.shape[2]
    ap = aperture[t]
    has_above = t > 0
    has_below = t < n_tile - 1

    loads = (
        pltpu.make_async_copy(src_hbm, src_v, local_sem.at[0]),
        pltpu.make_async_copy(rec_hbm, rec_v, local_sem.at[1]),
        pltpu.make_async_copy(slow_hbm, g_slow.at[f], local_sem.at[2]),
        pltpu.make_async_copy(coeffs_hbm, coeffs, local_sem.at[3]),
    )
    for copy in loads:
        copy.start()

    @pl.when(t == 0)
    def _():
        h_fa[...] = jnp.zeros_like(h_fa)
        h_sa[...] = jnp.zeros_like(h_sa)

    @pl.when(t == n_tile - 1)
    def _():
        h_fb[...] = jnp.zeros_like(h_fb)
        h_sb[...] = jnp.zeros_like(h_sb)

    barrier = pltpu.get_barrier_semaphore()
    for q in range(n_freq):
        @pl.when(f != q)
        def _():
            pl.semaphore_signal(barrier, 1, device_id=(t, q), device_id_type=MESH)

        @pl.when(has_above)
        def _():
            pl.semaphore_signal(barrier, 1, device_id=(t - 1, q), device_id_type=MESH)

        @pl.when(has_below)
        def _():
            pl.semaphore_signal(barrier, 1, device_id=(t + 1, q), device_id_type=MESH)

    expected = (n_freq - 1) + n_freq * has_above.astype(jnp.int32) + n_freq * has_below.astype(jnp.int32)

    for copy in loads:
        copy.wait()

    own_rows = lax.broadcasted_iota(jnp.int32, (own, ncol), 0)
    own_forward = pltpu.roll(own_rows, 1, 0) == (own_rows + own - 1) % own
    lift = (own + HALO - ap) % own
    drop = ap - HALO

    def last_rows(x, forward):
        return jnp.where(forward, pltpu.roll(x, lift, 0), pltpu.roll(x, drop, 0))[:HALO]

    s_up[...] = last_rows(g_slow[f, 0], own_forward[:, :block])
    fields_v = (src_v, rec_v)
    for fi in range(nfl):
        for x in range(2):
            for c in range(nc):
                up_buf[x, c, fi] = last_rows(fields_v[x][c, fi], own_forward)

    pl.semaphore_wait(barrier, expected)

    def remote(src, dst, slot_send, slot_recv, device):
        return pltpu.make_async_remote_copy(
            src_ref=src, dst_ref=dst, send_sem=send_sem.at[slot_send], recv_sem=recv_sem.at[slot_recv],
            device_id=device, device_id_type=MESH,
        )

    f_lo = (src_hbm.at[:, :, pl.ds(0, HALO), :], rec_hbm.at[:, :, pl.ds(0, HALO), :])
    s_lo = slow_hbm.at[0, pl.ds(0, HALO), :]
    for q in range(n_freq):
        @pl.when(f != q)
        def _():
            remote(slow_hbm, g_slow.at[f], q, f, (t, q)).start()

        @pl.when(has_above)
        def _():
            remote(s_lo, h_sb.at[f], 2 * n_freq + q, 2 * n_freq + f, (t - 1, q)).start()

    field_base = 3 * n_freq

    def lower_copy(x, fi, device):
        return remote(f_lo[x].at[:, fi], h_fb.at[x, :, fi], field_base + 2 + 2 * x + fi,
                      field_base + 2 + 2 * x + fi, device)

    def upper_copy(fi, device):
        return remote(up_buf.at[:, :, fi], h_fa.at[:, :, fi], field_base + fi, field_base + fi, device)

    def start_lower():
        for fi in range(nfl):
            @pl.when(has_above)
            def _():
                for x in range(2):
                    lower_copy(x, fi, (t - 1, f)).start()

    def start_upper():
        for q in range(n_freq):
            @pl.when(has_below)
            def _():
                remote(s_up, h_sa.at[f], n_freq + q, n_freq + f, (t + 1, q)).start()

        for fi in range(nfl):
            @pl.when(has_below)
            def _():
                upper_copy(fi, (t + 1, f)).start()

    far_above = (t % period == period - 1) if period else t < 0

    @pl.when(far_above)
    def _():
        start_upper()
        start_lower()

    @pl.when(jnp.logical_not(far_above))
    def _():
        start_lower()
        start_upper()

    for q in range(n_freq):
        @pl.when(f != q)
        def _():
            remote(slow_hbm, g_slow.at[q], q, q, (t, q)).wait_send()
            remote(slow_hbm, g_slow.at[q], q, q, (t, q)).wait_recv()

        @pl.when(has_below)
        def _():
            remote(s_up, h_sa.at[q], n_freq + q, n_freq + q, (t + 1, q)).wait_send()
            remote(s_lo, h_sb.at[q], 2 * n_freq + q, 2 * n_freq + q, (t + 1, q)).wait_recv()

        @pl.when(has_above)
        def _():
            remote(s_lo, h_sb.at[q], 2 * n_freq + q, 2 * n_freq + q, (t - 1, q)).wait_send()
            remote(s_up, h_sa.at[q], n_freq + q, n_freq + q, (t - 1, q)).wait_recv()

    def await_fields(fi):
        @pl.when(has_below)
        def _():
            upper_copy(fi, (t + 1, f)).wait_send()
            for x in range(2):
                lower_copy(x, fi, (t + 1, f)).wait_recv()

        @pl.when(has_above)
        def _():
            for x in range(2):
                lower_copy(x, fi, (t - 1, f)).wait_send()
            upper_copy(fi, (t - 1, f)).wait_recv()

    rows = lax.broadcasted_iota(jnp.int32, (ext_rows, ncol), 0)
    cols = lax.broadcasted_iota(jnp.int32, (ext_rows, ncol), 1)
    left_ok = jnp.abs(pltpu.roll(cols, 1, 1) - cols) == 1
    right_ok = jnp.abs(pltpu.roll(cols, ncol - 1, 1) - cols) == 1
    forward = pltpu.roll(rows, 1, 0) == (rows + ext_rows - 1) % ext_rows
    lower_start = HALO + ap
    top_part = rows < lower_start

    def in_band(lo, hi):
        return (rows >= lo) & (rows < hi)

    valid0 = (in_band(0, HALO) & has_above) | in_band(HALO, lower_start) | (
        in_band(lower_start, lower_start + HALO) & has_below)
    reach = HALO // 2
    valid1 = (in_band(HALO - reach, HALO) & has_above) | in_band(HALO, lower_start) | (
        in_band(lower_start, lower_start + reach) & has_below)
    live = lax.broadcasted_iota(jnp.int32, (own, ncol), 0) < ap
    zeros_tail = jnp.zeros((ext_rows - HALO, ncol), jnp.float32)

    def place_lower(lower8):
        padded = jnp.concatenate([lower8, zeros_tail], axis=0)
        ahead = pltpu.roll(padded, lower_start, 0)
        behind = pltpu.roll(padded, ext_rows - lower_start, 0)
        return jnp.where(forward, ahead, behind)

    def joined(upper8, own_rows, lower8):
        top = jnp.concatenate([upper8, own_rows, jnp.zeros((HALO, ncol), jnp.float32)], axis=0)
        return jnp.where(top_part, top, place_lower(lower8))

    def columns_of(pieces):
        return jnp.concatenate(pieces, axis=1)

    slow0 = joined(
        columns_of([h_sa[q] for q in range(n_freq)]),
        columns_of([g_slow[q, 0] for q in range(n_freq)]),
        columns_of([h_sb[q] for q in range(n_freq)]),
    )
    slow0 = jnp.where(valid0, slow0, 0.0)
    slow1 = columns_of([g_slow[q, 1] for q in range(n_freq)])

    edge = 128

    def masked_side(b):
        ahead = pltpu.roll(b, 1, 1)
        behind = pltpu.roll(b, ncol - 1, 1)

        def guarded(lo, hi):
            return jnp.where(left_ok[:, lo:hi], ahead[:, lo:hi], 0.0) + jnp.where(
                right_ok[:, lo:hi], behind[:, lo:hi], 0.0)

        middle = ahead[:, edge:ncol - edge] + behind[:, edge:ncol - edge]
        return jnp.concatenate([guarded(0, edge), middle, guarded(ncol - edge, ncol)], axis=1)

    def chebyshev_step(v, prev):
        pair = pltpu.roll(v, 1, 0) + pltpu.roll(v, ext_rows - 1, 0)
        blur = 0.25 * pair + 0.5 * v
        side = masked_side(blur)
        if prev is None:
            return 0.5 * side + blur - v
        return side + 0.5 * pair - v - prev

    def coefficient_of(depth, fi, n, wavenumber):
        active = jnp.where(orders[depth, fi] >= n, 1.0, 0.0).astype(jnp.float32)
        scaled = [[coeffs[m, c, n] * active for m in range(POWERS)] for c in range(2)]
        coef_re = scaled[0][POWERS - 1] * wavenumber + scaled[0][POWERS - 2]
        coef_im = scaled[1][POWERS - 1] * wavenumber + scaled[1][POWERS - 2]
        for m in range(POWERS - 3, -1, -1):
            coef_re = coef_re * wavenumber + scaled[0][m]
            coef_im = coef_im * wavenumber + scaled[1][m]
        return coef_re, coef_im

    for fi in range(nfl):
        wave0 = frequency[fi] * slow0
        wave1 = frequency[fi] * slow1
        for n in range(ORDER + 1):
            cf0[fi, n, 0], cf0[fi, n, 1] = coefficient_of(0, fi, n, wave0)
            cf1[fi, n, 0], cf1[fi, n, 1] = coefficient_of(1, fi, n, wave1)

    def coefficient(depth, fi, n, wavenumber):
        table = cf0 if depth == 0 else cf1
        return table[fi, n, 0], table[fi, n, 1]

    def extrapolate(depth, fi, wavenumber, valid, lo, hi, write):
        for n in range(ORDER + 1):
            slot = n % 3
            if n >= 1:
                cur, prev = (n - 1) % 3, (n - 2) % 3
                for p in range(4):
                    g = chebyshev_step(tb[cur, p], tb[prev, p] if n > 1 else None)
                    tb[slot, p] = jnp.where(valid, g, 0.0)
            coef_re, coef_im = coefficient(depth, fi, n, wavenumber)
            s_re = tb[slot, 0, lo:hi, :]
            s_im = tb[slot, 1, lo:hi, :]
            r_re = tb[slot, 2, lo:hi, :]
            r_im = tb[slot, 3, lo:hi, :]
            terms = (
                coef_re * s_re + coef_im * s_im,
                coef_re * s_im - coef_im * s_re,
                coef_re * r_re - coef_im * r_im,
                coef_re * r_im + coef_im * r_re,
            )
            write(n, terms)

    fields = (src_v, rec_v)
    for fi in range(nfl):
        await_fields(fi)
        for p in range(4):
            x, c = p // 2, p % 2
            tb[0, p] = jnp.where(valid0, joined(h_fa[x, c, fi], fields[x][c, fi], h_fb[x, c, fi]), 0.0)

        def write0(n, terms, fi=fi):
            for p in range(4):
                if n == 0:
                    s1[p // 2, p % 2, fi] = terms[p]
                else:
                    s1[p // 2, p % 2, fi] = s1[p // 2, p % 2, fi] + terms[p]

        extrapolate(0, fi, frequency[fi] * slow0, valid0, 0, ext_rows, write0)
        for p in range(4):
            s1[p // 2, p % 2, fi] = jnp.where(valid1, s1[p // 2, p % 2, fi], 0.0)
        mid = slice(HALO, HALO + own)
        term = s1[0, 0, fi, mid, :] * s1[1, 0, fi, mid, :] + s1[0, 1, fi, mid, :] * s1[1, 1, fi, mid, :]
        term = jnp.where(live, term, 0.0)
        if fi == 0:
            img_out[0] = term
        else:
            img_out[0] = img_out[0] + term

    image_base = 3 * n_freq + 6

    def image_copy(depth, q, slot_recv, device):
        return pltpu.make_async_remote_copy(
            src_ref=img_out.at[depth, :, pl.ds(q * block, block)], dst_ref=got.at[slot_recv, depth],
            send_sem=send_sem.at[image_base + depth * n_freq + q],
            recv_sem=recv_sem.at[image_base + depth * n_freq + slot_recv],
            device_id=device, device_id_type=MESH,
        )

    def send_image(depth):
        for q in range(n_freq):
            @pl.when(f != q)
            def _():
                image_copy(depth, q, f, (t, q)).start()

    send_image(0)

    for fi in range(nfl):
        for p in range(4):
            tb[0, p] = s1[p // 2, p % 2, fi]
        acc = {}

        def write1(n, terms, acc=acc):
            for p in range(4):
                acc[p] = terms[p] if n == 0 else acc[p] + terms[p]

        extrapolate(1, fi, frequency[fi] * slow1, valid1, HALO, HALO + own, write1)
        result = [jnp.where(live, acc[p], 0.0) for p in range(4)]
        rec_out[0, fi] = result[2]
        rec_out[1, fi] = result[3]
        term = result[0] * result[2] + result[1] * result[3]
        if fi == 0:
            img_out[1] = term
        else:
            img_out[1] = img_out[1] + term

    send_image(1)
    for depth in range(NDEPTH):
        for q in range(n_freq):
            @pl.when(f != q)
            def _():
                image_copy(depth, q, q, (t, q)).wait_send()
                image_copy(depth, q, q, (t, q)).wait_recv()

    total = None
    for q in range(n_freq):
        mine = img_out[:, :, q * block:(q + 1) * block]
        part = jnp.where(f == q, mine, got[q])
        total = part if total is None else total + part
    image_out[...] = total


def shards(n_tile, n_freq, period, source_field, receiver_field, slowness, frequency, order_table, filter_coeffs, aperture):
    nc, nfl, own, ncol = source_field.shape
    block = slowness.shape[2]
    ext_rows = own + 2 * HALO
    elements = nc * nfl * 2 * ext_rows * ncol * NDEPTH
    rec_out, image_out = pl.pallas_call(
        functools.partial(migrate_kernel, n_tile, n_freq, period),
        out_shape=(
            jax.ShapeDtypeStruct((nc, nfl, own, ncol), jnp.float32),
            jax.ShapeDtypeStruct((NDEPTH, own, block), jnp.float32),
        ),
        in_specs=[pl.BlockSpec(memory_space=SMEM)] * 3 + [pl.BlockSpec(memory_space=pl.ANY)] * 4,
        out_specs=(pl.BlockSpec(memory_space=VMEM), pl.BlockSpec(memory_space=VMEM)),
        scratch_shapes=[
            pltpu.VMEM((nc, nfl, own, ncol), jnp.float32),
            pltpu.VMEM((nc, nfl, own, ncol), jnp.float32),
            pltpu.VMEM((n_freq, NDEPTH, own, block), jnp.float32),
            pltpu.VMEM((n_freq, HALO, block), jnp.float32),
            pltpu.VMEM((n_freq, HALO, block), jnp.float32),
            pltpu.VMEM((2, nc, nfl, HALO, ncol), jnp.float32),
            pltpu.VMEM((2, nc, nfl, HALO, ncol), jnp.float32),
            pltpu.VMEM((2, nc, nfl, HALO, ncol), jnp.float32),
            pltpu.VMEM((HALO, block), jnp.float32),
            pltpu.VMEM((2, nc, nfl, ext_rows, ncol), jnp.float32),
            pltpu.VMEM((3, 4, ext_rows, ncol), jnp.float32),
            pltpu.VMEM((NDEPTH, own, ncol), jnp.float32),
            pltpu.VMEM((n_freq, NDEPTH, own, block), jnp.float32),
            pltpu.SMEM((filter_coeffs.shape[2], filter_coeffs.shape[0], filter_coeffs.shape[1]), jnp.float32),
            pltpu.VMEM((nfl, ORDER + 1, 2, ext_rows, ncol), jnp.float32),
            pltpu.VMEM((nfl, ORDER + 1, 2, own, ncol), jnp.float32),
            pltpu.SemaphoreType.DMA((4,)),
            pltpu.SemaphoreType.DMA((3 * n_freq + 6 + NDEPTH * n_freq,)),
            pltpu.SemaphoreType.DMA((3 * n_freq + 6 + NDEPTH * n_freq,)),
        ],
        compiler_params=pltpu.CompilerParams(collective_id=0, has_side_effects=True),
        cost_estimate=pl.CostEstimate(flops=elements * 100, bytes_accessed=elements * 4, transcendentals=0),
    )(aperture, order_table, frequency, jnp.transpose(filter_coeffs, (2, 0, 1)), source_field, receiver_field, slowness)
    return pl.pallas_call(
        passthrough_kernel,
        out_shape=(
            jax.ShapeDtypeStruct(image_out.shape, jnp.float32),
            jax.ShapeDtypeStruct(rec_out.shape, jnp.float32),
        ),
        in_specs=[pl.BlockSpec(memory_space=pl.ANY)] * 2,
        out_specs=(pl.BlockSpec(memory_space=pl.ANY), pl.BlockSpec(memory_space=pl.ANY)),
        scratch_shapes=[pltpu.SemaphoreType.DMA((2,))],
    )(image_out, rec_out)


def passthrough_kernel(img_in, rec_in, img_out, rec_out, sems):
    copies = (
        pltpu.make_async_copy(img_in, img_out, sems.at[0]),
        pltpu.make_async_copy(rec_in, rec_out, sems.at[1]),
    )
    for copy in copies:
        copy.start()
    for copy in copies:
        copy.wait()


def relay_period(mesh):
    devices = mesh.devices
    n_tile, n_freq = devices.shape
    if n_freq % 2:
        return 0
    try:
        xs = [[d.coords[0] for d in row] for row in devices]
        cores = [[d.core_on_chip for d in row] for row in devices]
        ring = max(max(r) for r in xs) + 1
    except AttributeError:
        return 0
    crossing = []
    for t in range(n_tile - 1):
        gaps = {min((xs[t][q] - xs[t + 1][q]) % ring, (xs[t + 1][q] - xs[t][q]) % ring) for q in range(n_freq)}
        crossing.append(gaps == {2})
    if not any(crossing):
        return 0
    period = crossing.index(True) + 1
    if crossing != [t % period == period - 1 for t in range(n_tile - 1)]:
        return 0
    for t in range(n_tile):
        for q in range(n_freq):
            p = (q + n_freq // 2) % n_freq
            if cores[t][p] != cores[t][q] or xs[t][p] == xs[t][q]:
                return 0
    return period


def solution(mesh):
    placed = (
        P(None, "freq", "tile", None),
        P(None, "freq", "tile", None),
        P(None, "tile", "freq"),
        P("freq"),
        P(None, "freq"),
        P(),
        P(),
    )
    return jax.shard_map(
        functools.partial(shards, mesh.shape["tile"], mesh.shape["freq"], relay_period(mesh)),
        mesh=mesh,
        in_specs=placed,
        out_specs=(P(None, "tile", "freq"), P(None, "freq", "tile", None)),
        check_vma=False,
    )
```

```python
import functools

import jax
import jax.numpy as jnp
from jax import lax
from jax.experimental import pallas as pl
from jax.experimental.pallas import tpu as pltpu
from jax.sharding import PartitionSpec as P

ORDER = 4
NDEPTH = 2
POWERS = 3
HALO = 8
MESH = pl.DeviceIdType.MESH
VMEM = pltpu.MemorySpace.VMEM
SMEM = pltpu.MemorySpace.SMEM


def migrate_kernel(n_tile, n_freq, aperture, orders, frequency, coeffs_hbm, src_hbm, rec_hbm, slow_hbm,
                   rec_out, image_out, src_v, rec_v, g_slow, h_sa, h_sb, h_fa, h_fb, up_buf, s_up, s1, tb, img_out,
                   got, coeffs, cf0, cf1, ws, acc1, local_sem, send_sem, recv_sem):
    t = lax.axis_index("tile")
    f = lax.axis_index("freq")
    nc, nfl, own, ncol = src_v.shape
    ext_rows = HALO + own + HALO
    block = slow_hbm.shape[2]
    ap = aperture[t]
    has_above = t > 0
    has_below = t < n_tile - 1

    loads = (
        pltpu.make_async_copy(src_hbm, src_v, local_sem.at[0]),
        pltpu.make_async_copy(rec_hbm, rec_v, local_sem.at[1]),
        pltpu.make_async_copy(slow_hbm, g_slow.at[f], local_sem.at[2]),
        pltpu.make_async_copy(coeffs_hbm, coeffs, local_sem.at[3]),
    )
    for copy in loads:
        copy.start()

    @pl.when(t == 0)
    def _():
        h_fa[...] = jnp.zeros_like(h_fa)
        h_sa[...] = jnp.zeros_like(h_sa)

    @pl.when(t == n_tile - 1)
    def _():
        h_fb[...] = jnp.zeros_like(h_fb)
        h_sb[...] = jnp.zeros_like(h_sb)

    barrier = pltpu.get_barrier_semaphore()
    for q in range(n_freq):
        @pl.when(f != q)
        def _():
            pl.semaphore_signal(barrier, 1, device_id=(t, q), device_id_type=MESH)

        @pl.when(has_above)
        def _():
            pl.semaphore_signal(barrier, 1, device_id=(t - 1, q), device_id_type=MESH)

        @pl.when(has_below)
        def _():
            pl.semaphore_signal(barrier, 1, device_id=(t + 1, q), device_id_type=MESH)

    expected = (n_freq - 1) + n_freq * has_above.astype(jnp.int32) + n_freq * has_below.astype(jnp.int32)

    for copy in loads:
        copy.wait()

    own_rows = lax.broadcasted_iota(jnp.int32, (own, ncol), 0)
    own_forward = pltpu.roll(own_rows, 1, 0) == (own_rows + own - 1) % own
    lift = (own + HALO - ap) % own
    drop = ap - HALO

    def last_rows(x, forward):
        return jnp.where(forward, pltpu.roll(x, lift, 0), pltpu.roll(x, drop, 0))[:HALO]

    s_up[...] = last_rows(g_slow[f, 0], own_forward[:, :block])
    fields_v = (src_v, rec_v)
    for fi in range(nfl):
        for x in range(2):
            for c in range(nc):
                up_buf[x, c, fi] = last_rows(fields_v[x][c, fi], own_forward)

    pl.semaphore_wait(barrier, expected)

    def remote(src, dst, slot_send, slot_recv, device):
        return pltpu.make_async_remote_copy(
            src_ref=src, dst_ref=dst, send_sem=send_sem.at[slot_send], recv_sem=recv_sem.at[slot_recv],
            device_id=device, device_id_type=MESH,
        )

    f_lo = (src_hbm.at[:, :, pl.ds(0, HALO), :], rec_hbm.at[:, :, pl.ds(0, HALO), :])
    s_lo = slow_hbm.at[0, pl.ds(0, HALO), :]
    for q in range(n_freq):
        @pl.when(f != q)
        def _():
            remote(slow_hbm, g_slow.at[f], q, f, (t, q)).start()

        @pl.when(has_above)
        def _():
            remote(s_lo, h_sb.at[f], 2 * n_freq + q, 2 * n_freq + f, (t - 1, q)).start()

    field_base = 3 * n_freq

    def lower_copy(x, fi, device):
        return remote(f_lo[x].at[:, fi], h_fb.at[x, :, fi], field_base + 2 + 2 * x + fi,
                      field_base + 2 + 2 * x + fi, device)

    def upper_copy(fi, device):
        return remote(up_buf.at[:, :, fi], h_fa.at[:, :, fi], field_base + fi, field_base + fi, device)

    for fi in range(2):
        @pl.when(has_above)
        def _():
            for x in range(2):
                lower_copy(x, fi, (t - 1, f)).start()

    for q in range(n_freq):
        @pl.when(has_below)
        def _():
            remote(s_up, h_sa.at[f], n_freq + q, n_freq + f, (t + 1, q)).start()

    for fi in range(nfl):
        @pl.when(has_below)
        def _():
            upper_copy(fi, (t + 1, f)).start()

    for q in range(n_freq):
        @pl.when(f != q)
        def _():
            remote(slow_hbm, g_slow.at[q], q, q, (t, q)).wait_send()
            remote(slow_hbm, g_slow.at[q], q, q, (t, q)).wait_recv()

        @pl.when(has_below)
        def _():
            remote(s_up, h_sa.at[q], n_freq + q, n_freq + q, (t + 1, q)).wait_send()
            remote(s_lo, h_sb.at[q], 2 * n_freq + q, 2 * n_freq + q, (t + 1, q)).wait_recv()

        @pl.when(has_above)
        def _():
            remote(s_lo, h_sb.at[q], 2 * n_freq + q, 2 * n_freq + q, (t - 1, q)).wait_send()
            remote(s_up, h_sa.at[q], n_freq + q, n_freq + q, (t - 1, q)).wait_recv()

    def await_fields(fi):
        @pl.when(has_below)
        def _():
            upper_copy(fi, (t + 1, f)).wait_send()
            for x in range(2):
                lower_copy(x, fi, (t + 1, f)).wait_recv()

        @pl.when(has_above)
        def _():
            for x in range(2):
                lower_copy(x, fi, (t - 1, f)).wait_send()
            upper_copy(fi, (t - 1, f)).wait_recv()

    rows = lax.broadcasted_iota(jnp.int32, (ext_rows, ncol), 0)
    cols = lax.broadcasted_iota(jnp.int32, (ext_rows, ncol), 1)
    left_ok = jnp.abs(pltpu.roll(cols, 1, 1) - cols) == 1
    right_ok = jnp.abs(pltpu.roll(cols, ncol - 1, 1) - cols) == 1
    forward = pltpu.roll(rows, 1, 0) == (rows + ext_rows - 1) % ext_rows
    lower_start = HALO + ap
    top_part = rows < lower_start

    def in_band(lo, hi):
        return (rows >= lo) & (rows < hi)

    valid0 = (in_band(0, HALO) & has_above) | in_band(HALO, lower_start) | (
        in_band(lower_start, lower_start + HALO) & has_below)
    reach = HALO // 2
    valid1 = (in_band(HALO - reach, HALO) & has_above) | in_band(HALO, lower_start) | (
        in_band(lower_start, lower_start + reach) & has_below)
    live = lax.broadcasted_iota(jnp.int32, (own, ncol), 0) < ap
    zeros_tail = jnp.zeros((ext_rows - HALO, ncol), jnp.float32)

    def place_lower(lower8):
        padded = jnp.concatenate([lower8, zeros_tail], axis=0)
        ahead = pltpu.roll(padded, lower_start, 0)
        behind = pltpu.roll(padded, ext_rows - lower_start, 0)
        return jnp.where(forward, ahead, behind)

    def joined(upper8, own_rows, lower8):
        top = jnp.concatenate([upper8, own_rows, jnp.zeros((HALO, ncol), jnp.float32)], axis=0)
        return jnp.where(top_part, top, place_lower(lower8))

    def columns_of(pieces):
        return jnp.concatenate(pieces, axis=1)

    slow0 = joined(
        columns_of([h_sa[q] for q in range(n_freq)]),
        columns_of([g_slow[q, 0] for q in range(n_freq)]),
        columns_of([h_sb[q] for q in range(n_freq)]),
    )
    slow0 = jnp.where(valid0, slow0, 0.0)
    slow1 = columns_of([g_slow[q, 1] for q in range(n_freq)])

    edge = 128

    def masked_side(b):
        ahead = pltpu.roll(b, 1, 1)
        behind = pltpu.roll(b, ncol - 1, 1)

        def guarded(lo, hi):
            height = b.shape[0]
            return jnp.where(left_ok[:height, lo:hi], ahead[:, lo:hi], 0.0) + jnp.where(
                right_ok[:height, lo:hi], behind[:, lo:hi], 0.0)

        middle = ahead[:, edge:ncol - edge] + behind[:, edge:ncol - edge]
        return jnp.concatenate([guarded(0, edge), middle, guarded(ncol - edge, ncol)], axis=1)

    def chebyshev_step(v, prev):
        pair = pltpu.roll(v, 1, 0) + pltpu.roll(v, v.shape[0] - 1, 0)
        blur = 0.25 * pair + 0.5 * v
        side = masked_side(blur)
        if prev is None:
            return 0.5 * side + blur - v
        return side + 0.5 * pair - v - prev

    def coefficient_of(depth, fi, n, wavenumber):
        active = jnp.where(orders[depth, fi] >= n, 1.0, 0.0).astype(jnp.float32)
        scaled = [[coeffs[m, c, n] * active for m in range(POWERS)] for c in range(2)]
        coef_re = scaled[0][POWERS - 1] * wavenumber + scaled[0][POWERS - 2]
        coef_im = scaled[1][POWERS - 1] * wavenumber + scaled[1][POWERS - 2]
        for m in range(POWERS - 3, -1, -1):
            coef_re = coef_re * wavenumber + scaled[0][m]
            coef_im = coef_im * wavenumber + scaled[1][m]
        return coef_re, coef_im

    reach = HALO // 2
    win = ext_rows - 2 * reach
    ws[...] = jnp.concatenate([jnp.zeros((HALO, ncol), jnp.float32), slow1,
                               jnp.zeros((HALO, ncol), jnp.float32)], axis=0)
    slow1w = ws[reach:reach + win]
    pos = lax.broadcasted_iota(jnp.int32, (win, ncol), 0) + reach
    valid1w = ((pos >= HALO - reach) & (pos < HALO) & has_above) | ((pos >= HALO) & (pos < lower_start)) | (
        (pos >= lower_start) & (pos < lower_start + reach) & has_below)
    for fi in range(nfl):
        wave0 = frequency[fi] * slow0
        wave1 = frequency[fi] * slow1w
        for n in range(ORDER + 1):
            cf0[fi, n, 0], cf0[fi, n, 1] = coefficient_of(0, fi, n, wave0)
            cf1[fi, n, 0], cf1[fi, n, 1] = coefficient_of(1, fi, n, wave1)

    def coefficient(depth, fi, n, wavenumber):
        table = cf0 if depth == 0 else cf1
        return table[fi, n, 0], table[fi, n, 1]

    def extrapolate(depth, fi, wavenumber, valid, lo, hi, write):
        height = valid.shape[0]
        for n in range(ORDER + 1):
            slot = n % 3
            if n >= 1:
                cur, prev = (n - 1) % 3, (n - 2) % 3
                for p in range(4):
                    g = chebyshev_step(tb[cur, p, :height], tb[prev, p, :height] if n > 1 else None)
                    tb[slot, p, :height] = jnp.where(valid, g, 0.0)
            coef_re, coef_im = coefficient(depth, fi, n, wavenumber)
            s_re = tb[slot, 0, lo:hi, :]
            s_im = tb[slot, 1, lo:hi, :]
            r_re = tb[slot, 2, lo:hi, :]
            r_im = tb[slot, 3, lo:hi, :]
            terms = (
                coef_re * s_re + coef_im * s_im,
                coef_re * s_im - coef_im * s_re,
                coef_re * r_re - coef_im * r_im,
                coef_re * r_im + coef_im * r_re,
            )
            write(n, terms)

    fields = (src_v, rec_v)
    for fi in range(nfl):
        await_fields(fi)
        for p in range(4):
            x, c = p // 2, p % 2
            tb[0, p] = jnp.where(valid0, joined(h_fa[x, c, fi], fields[x][c, fi], h_fb[x, c, fi]), 0.0)

        def write0(n, terms, fi=fi):
            for p in range(4):
                if n == 0:
                    s1[p // 2, p % 2, fi] = terms[p]
                else:
                    s1[p // 2, p % 2, fi] = s1[p // 2, p % 2, fi] + terms[p]

        extrapolate(0, fi, frequency[fi] * slow0, valid0, 0, ext_rows, write0)
        for p in range(4):
            s1[p // 2, p % 2, fi] = jnp.where(valid1, s1[p // 2, p % 2, fi], 0.0)
        mid = slice(HALO, HALO + own)
        term = s1[0, 0, fi, mid, :] * s1[1, 0, fi, mid, :] + s1[0, 1, fi, mid, :] * s1[1, 1, fi, mid, :]
        term = jnp.where(live, term, 0.0)
        if fi == 0:
            img_out[0] = term
        else:
            img_out[0] = img_out[0] + term

    image_base = 3 * n_freq + 6

    def image_copy(depth, q, slot_recv, device):
        return pltpu.make_async_remote_copy(
            src_ref=img_out.at[depth, :, pl.ds(q * block, block)], dst_ref=got.at[slot_recv, depth],
            send_sem=send_sem.at[image_base + depth * n_freq + q],
            recv_sem=recv_sem.at[image_base + depth * n_freq + slot_recv],
            device_id=device, device_id_type=MESH,
        )

    def send_image(depth):
        for q in range(n_freq):
            @pl.when(f != q)
            def _():
                image_copy(depth, q, f, (t, q)).start()

    send_image(0)

    for fi in range(nfl):
        for p in range(4):
            tb[0, p, :win] = s1[p // 2, p % 2, fi, reach:reach + win]

        def write1(n, terms):
            for p in range(4):
                if n == 0:
                    acc1[p] = terms[p]
                else:
                    acc1[p] = acc1[p] + terms[p]

        extrapolate(1, fi, None, valid1w, 0, win, write1)
        result = [jnp.where(live, acc1[p, HALO - reach:HALO - reach + own], 0.0) for p in range(4)]
        rec_out[0, fi] = result[2]
        rec_out[1, fi] = result[3]
        term = result[0] * result[2] + result[1] * result[3]
        if fi == 0:
            img_out[1] = term
        else:
            img_out[1] = img_out[1] + term

    send_image(1)
    for depth in range(NDEPTH):
        for q in range(n_freq):
            @pl.when(f != q)
            def _():
                image_copy(depth, q, q, (t, q)).wait_send()
                image_copy(depth, q, q, (t, q)).wait_recv()

    total = None
    for q in range(n_freq):
        mine = img_out[:, :, q * block:(q + 1) * block]
        part = jnp.where(f == q, mine, got[q])
        total = part if total is None else total + part
    image_out[...] = total


def shards(n_tile, n_freq, source_field, receiver_field, slowness, frequency, order_table, filter_coeffs, aperture):
    nc, nfl, own, ncol = source_field.shape
    block = slowness.shape[2]
    ext_rows = own + 2 * HALO
    elements = nc * nfl * 2 * ext_rows * ncol * NDEPTH
    rec_out, image_out = pl.pallas_call(
        functools.partial(migrate_kernel, n_tile, n_freq),
        out_shape=(
            jax.ShapeDtypeStruct((nc, nfl, own, ncol), jnp.float32),
            jax.ShapeDtypeStruct((NDEPTH, own, block), jnp.float32),
        ),
        in_specs=[pl.BlockSpec(memory_space=SMEM)] * 3 + [pl.BlockSpec(memory_space=pl.ANY)] * 4,
        out_specs=(pl.BlockSpec(memory_space=VMEM), pl.BlockSpec(memory_space=VMEM)),
        scratch_shapes=[
            pltpu.VMEM((nc, nfl, own, ncol), jnp.float32),
            pltpu.VMEM((nc, nfl, own, ncol), jnp.float32),
            pltpu.VMEM((n_freq, NDEPTH, own, block), jnp.float32),
            pltpu.VMEM((n_freq, HALO, block), jnp.float32),
            pltpu.VMEM((n_freq, HALO, block), jnp.float32),
            pltpu.VMEM((2, nc, nfl, HALO, ncol), jnp.float32),
            pltpu.VMEM((2, nc, nfl, HALO, ncol), jnp.float32),
            pltpu.VMEM((2, nc, nfl, HALO, ncol), jnp.float32),
            pltpu.VMEM((HALO, block), jnp.float32),
            pltpu.VMEM((2, nc, nfl, ext_rows, ncol), jnp.float32),
            pltpu.VMEM((3, 4, ext_rows, ncol), jnp.float32),
            pltpu.VMEM((NDEPTH, own, ncol), jnp.float32),
            pltpu.VMEM((n_freq, NDEPTH, own, block), jnp.float32),
            pltpu.SMEM((filter_coeffs.shape[2], filter_coeffs.shape[0], filter_coeffs.shape[1]), jnp.float32),
            pltpu.VMEM((nfl, ORDER + 1, 2, ext_rows, ncol), jnp.float32),
            pltpu.VMEM((nfl, ORDER + 1, 2, own + HALO, ncol), jnp.float32),
            pltpu.VMEM((own + 2 * HALO, ncol), jnp.float32),
            pltpu.VMEM((4, own + HALO, ncol), jnp.float32),
            pltpu.SemaphoreType.DMA((4,)),
            pltpu.SemaphoreType.DMA((3 * n_freq + 6 + NDEPTH * n_freq,)),
            pltpu.SemaphoreType.DMA((3 * n_freq + 6 + NDEPTH * n_freq,)),
        ],
        compiler_params=pltpu.CompilerParams(collective_id=0, has_side_effects=True),
        cost_estimate=pl.CostEstimate(flops=elements * 100, bytes_accessed=elements * 4, transcendentals=0),
    )(aperture, order_table, frequency, jnp.transpose(filter_coeffs, (2, 0, 1)), source_field, receiver_field, slowness)
    return pl.pallas_call(
        passthrough_kernel,
        out_shape=(
            jax.ShapeDtypeStruct(image_out.shape, jnp.float32),
            jax.ShapeDtypeStruct(rec_out.shape, jnp.float32),
        ),
        in_specs=[pl.BlockSpec(memory_space=VMEM)] * 2,
        out_specs=(pl.BlockSpec(memory_space=VMEM), pl.BlockSpec(memory_space=VMEM)),
    )(image_out, rec_out)


def passthrough_kernel(img_in, rec_in, img_out, rec_out):
    img_out[...] = img_in[...]
    rec_out[...] = rec_in[...]


def solution(mesh):
    placed = (
        P(None, "freq", "tile", None),
        P(None, "freq", "tile", None),
        P(None, "tile", "freq"),
        P("freq"),
        P(None, "freq"),
        P(),
        P(),
    )
    return jax.shard_map(
        functools.partial(shards, mesh.shape["tile"], mesh.shape["freq"]),
        mesh=mesh,
        in_specs=placed,
        out_specs=(P(None, "tile", "freq"), P(None, "freq", "tile", None)),
        check_vma=False,
    )
```

```python
import functools

import jax
import jax.numpy as jnp
from jax import lax
from jax.experimental import pallas as pl
from jax.experimental.pallas import tpu as pltpu
from jax.sharding import PartitionSpec as P

ORDER = 4
NDEPTH = 2
POWERS = 3
HALO = 8
MESH = pl.DeviceIdType.MESH
VMEM = pltpu.MemorySpace.VMEM
SMEM = pltpu.MemorySpace.SMEM


def migrate_kernel(n_tile, n_freq, aperture, orders, frequency, coeffs_hbm, src_hbm, rec_hbm, slow_hbm,
                   rec_out, image_out, src_v, rec_v, g_slow, h_sa, h_sb, h_fa, h_fb, up_buf, s_up, s1, tb, img_out,
                   got, coeffs, cf0, cf1, local_sem, send_sem, recv_sem):
    t = lax.axis_index("tile")
    f = lax.axis_index("freq")
    nc, nfl, own, ncol = src_v.shape
    ext_rows = HALO + own + HALO
    block = slow_hbm.shape[2]
    ap = aperture[t]
    has_above = t > 0
    has_below = t < n_tile - 1

    loads = (
        pltpu.make_async_copy(src_hbm, src_v, local_sem.at[0]),
        pltpu.make_async_copy(rec_hbm, rec_v, local_sem.at[1]),
        pltpu.make_async_copy(slow_hbm, g_slow.at[f], local_sem.at[2]),
        pltpu.make_async_copy(coeffs_hbm, coeffs, local_sem.at[3]),
    )
    for copy in loads:
        copy.start()

    @pl.when(t == 0)
    def _():
        h_fa[...] = jnp.zeros_like(h_fa)
        h_sa[...] = jnp.zeros_like(h_sa)

    @pl.when(t == n_tile - 1)
    def _():
        h_fb[...] = jnp.zeros_like(h_fb)
        h_sb[...] = jnp.zeros_like(h_sb)

    barrier = pltpu.get_barrier_semaphore()
    for q in range(n_freq):
        @pl.when(f != q)
        def _():
            pl.semaphore_signal(barrier, 1, device_id=(t, q), device_id_type=MESH)

        @pl.when(has_above)
        def _():
            pl.semaphore_signal(barrier, 1, device_id=(t - 1, q), device_id_type=MESH)

        @pl.when(has_below)
        def _():
            pl.semaphore_signal(barrier, 1, device_id=(t + 1, q), device_id_type=MESH)

    expected = (n_freq - 1) + n_freq * has_above.astype(jnp.int32) + n_freq * has_below.astype(jnp.int32)

    for copy in loads:
        copy.wait()

    own_rows = lax.broadcasted_iota(jnp.int32, (own, ncol), 0)
    own_forward = pltpu.roll(own_rows, 1, 0) == (own_rows + own - 1) % own
    lift = (own + HALO - ap) % own
    drop = ap - HALO

    def last_rows(x, forward):
        return jnp.where(forward, pltpu.roll(x, lift, 0), pltpu.roll(x, drop, 0))[:HALO]

    s_up[...] = last_rows(g_slow[f, 0], own_forward[:, :block])
    fields_v = (src_v, rec_v)
    for fi in range(nfl):
        for x in range(2):
            for c in range(nc):
                up_buf[x, c, fi] = last_rows(fields_v[x][c, fi], own_forward)

    pl.semaphore_wait(barrier, expected)

    def remote(src, dst, slot_send, slot_recv, device):
        return pltpu.make_async_remote_copy(
            src_ref=src, dst_ref=dst, send_sem=send_sem.at[slot_send], recv_sem=recv_sem.at[slot_recv],
            device_id=device, device_id_type=MESH,
        )

    f_lo = (src_hbm.at[:, :, pl.ds(0, HALO), :], rec_hbm.at[:, :, pl.ds(0, HALO), :])
    s_lo = slow_hbm.at[0, pl.ds(0, HALO), :]
    for q in range(n_freq):
        @pl.when(f != q)
        def _():
            remote(slow_hbm, g_slow.at[f], q, f, (t, q)).start()

        @pl.when(has_above)
        def _():
            remote(s_lo, h_sb.at[f], 2 * n_freq + q, 2 * n_freq + f, (t - 1, q)).start()

    field_base = 3 * n_freq

    def lower_copy(x, fi, device):
        return remote(f_lo[x].at[:, fi], h_fb.at[x, :, fi], field_base + 2 + 2 * x + fi,
                      field_base + 2 + 2 * x + fi, device)

    def upper_copy(fi, device):
        return remote(up_buf.at[:, :, fi], h_fa.at[:, :, fi], field_base + fi, field_base + fi, device)

    for fi in range(2):
        @pl.when(has_above)
        def _():
            for x in range(2):
                lower_copy(x, fi, (t - 1, f)).start()

    for q in range(n_freq):
        @pl.when(has_below)
        def _():
            remote(s_up, h_sa.at[f], n_freq + q, n_freq + f, (t + 1, q)).start()

    for fi in range(nfl):
        @pl.when(has_below)
        def _():
            upper_copy(fi, (t + 1, f)).start()

    for q in range(n_freq):
        @pl.when(f != q)
        def _():
            remote(slow_hbm, g_slow.at[q], q, q, (t, q)).wait_recv()

        @pl.when(has_below)
        def _():
            remote(s_lo, h_sb.at[q], 2 * n_freq + q, 2 * n_freq + q, (t + 1, q)).wait_recv()

        @pl.when(has_above)
        def _():
            remote(s_up, h_sa.at[q], n_freq + q, n_freq + q, (t - 1, q)).wait_recv()

    def await_fields(fi):
        @pl.when(has_below)
        def _():
            for x in range(2):
                lower_copy(x, fi, (t + 1, f)).wait_recv()

        @pl.when(has_above)
        def _():
            upper_copy(fi, (t - 1, f)).wait_recv()

    def await_sends():
        for q in range(n_freq):
            @pl.when(f != q)
            def _():
                remote(slow_hbm, g_slow.at[q], q, q, (t, q)).wait_send()

            @pl.when(has_below)
            def _():
                remote(s_up, h_sa.at[q], n_freq + q, n_freq + q, (t + 1, q)).wait_send()

            @pl.when(has_above)
            def _():
                remote(s_lo, h_sb.at[q], 2 * n_freq + q, 2 * n_freq + q, (t - 1, q)).wait_send()

        for fi in range(nfl):
            @pl.when(has_below)
            def _():
                upper_copy(fi, (t + 1, f)).wait_send()

            @pl.when(has_above)
            def _():
                for x in range(2):
                    lower_copy(x, fi, (t - 1, f)).wait_send()

    rows = lax.broadcasted_iota(jnp.int32, (ext_rows, ncol), 0)
    cols = lax.broadcasted_iota(jnp.int32, (ext_rows, ncol), 1)
    left_ok = jnp.abs(pltpu.roll(cols, 1, 1) - cols) == 1
    right_ok = jnp.abs(pltpu.roll(cols, ncol - 1, 1) - cols) == 1
    forward = pltpu.roll(rows, 1, 0) == (rows + ext_rows - 1) % ext_rows
    lower_start = HALO + ap
    top_part = rows < lower_start

    def in_band(lo, hi):
        return (rows >= lo) & (rows < hi)

    valid0 = (in_band(0, HALO) & has_above) | in_band(HALO, lower_start) | (
        in_band(lower_start, lower_start + HALO) & has_below)
    reach = HALO // 2
    valid1 = (in_band(HALO - reach, HALO) & has_above) | in_band(HALO, lower_start) | (
        in_band(lower_start, lower_start + reach) & has_below)
    live = lax.broadcasted_iota(jnp.int32, (own, ncol), 0) < ap
    zeros_tail = jnp.zeros((ext_rows - HALO, ncol), jnp.float32)

    def place_lower(lower8):
        padded = jnp.concatenate([lower8, zeros_tail], axis=0)
        ahead = pltpu.roll(padded, lower_start, 0)
        behind = pltpu.roll(padded, ext_rows - lower_start, 0)
        return jnp.where(forward, ahead, behind)

    def joined(upper8, own_rows, lower8):
        top = jnp.concatenate([upper8, own_rows, jnp.zeros((HALO, ncol), jnp.float32)], axis=0)
        return jnp.where(top_part, top, place_lower(lower8))

    def columns_of(pieces):
        return jnp.concatenate(pieces, axis=1)

    slow0 = joined(
        columns_of([h_sa[q] for q in range(n_freq)]),
        columns_of([g_slow[q, 0] for q in range(n_freq)]),
        columns_of([h_sb[q] for q in range(n_freq)]),
    )
    slow0 = jnp.where(valid0, slow0, 0.0)
    slow1 = columns_of([g_slow[q, 1] for q in range(n_freq)])

    edge = 128

    def masked_side(b):
        ahead = pltpu.roll(b, 1, 1)
        behind = pltpu.roll(b, ncol - 1, 1)

        def guarded(lo, hi):
            return jnp.where(left_ok[:, lo:hi], ahead[:, lo:hi], 0.0) + jnp.where(
                right_ok[:, lo:hi], behind[:, lo:hi], 0.0)

        middle = ahead[:, edge:ncol - edge] + behind[:, edge:ncol - edge]
        return jnp.concatenate([guarded(0, edge), middle, guarded(ncol - edge, ncol)], axis=1)

    def chebyshev_step(v, prev):
        pair = pltpu.roll(v, 1, 0) + pltpu.roll(v, ext_rows - 1, 0)
        blur = 0.25 * pair + 0.5 * v
        side = masked_side(blur)
        if prev is None:
            return 0.5 * side + blur - v
        return side + 0.5 * pair - v - prev

    def coefficient_of(depth, fi, n, wavenumber):
        active = jnp.where(orders[depth, fi] >= n, 1.0, 0.0).astype(jnp.float32)
        scaled = [[coeffs[m, c, n] * active for m in range(POWERS)] for c in range(2)]
        coef_re = scaled[0][POWERS - 1] * wavenumber + scaled[0][POWERS - 2]
        coef_im = scaled[1][POWERS - 1] * wavenumber + scaled[1][POWERS - 2]
        for m in range(POWERS - 3, -1, -1):
            coef_re = coef_re * wavenumber + scaled[0][m]
            coef_im = coef_im * wavenumber + scaled[1][m]
        return coef_re, coef_im

    for fi in range(nfl):
        wave0 = frequency[fi] * slow0
        wave1 = frequency[fi] * slow1
        for n in range(ORDER + 1):
            cf0[fi, n, 0], cf0[fi, n, 1] = coefficient_of(0, fi, n, wave0)
            cf1[fi, n, 0], cf1[fi, n, 1] = coefficient_of(1, fi, n, wave1)

    def coefficient(depth, fi, n, wavenumber):
        table = cf0 if depth == 0 else cf1
        return table[fi, n, 0], table[fi, n, 1]

    def extrapolate(depth, fi, wavenumber, valid, lo, hi, write):
        for n in range(ORDER + 1):
            slot = n % 3
            if n >= 1:
                cur, prev = (n - 1) % 3, (n - 2) % 3
                for p in range(4):
                    g = chebyshev_step(tb[cur, p], tb[prev, p] if n > 1 else None)
                    tb[slot, p] = jnp.where(valid, g, 0.0)
            coef_re, coef_im = coefficient(depth, fi, n, wavenumber)
            s_re = tb[slot, 0, lo:hi, :]
            s_im = tb[slot, 1, lo:hi, :]
            r_re = tb[slot, 2, lo:hi, :]
            r_im = tb[slot, 3, lo:hi, :]
            terms = (
                coef_re * s_re + coef_im * s_im,
                coef_re * s_im - coef_im * s_re,
                coef_re * r_re - coef_im * r_im,
                coef_re * r_im + coef_im * r_re,
            )
            write(n, terms)

    fields = (src_v, rec_v)
    for fi in range(nfl):
        await_fields(fi)
        for p in range(4):
            x, c = p // 2, p % 2
            tb[0, p] = jnp.where(valid0, joined(h_fa[x, c, fi], fields[x][c, fi], h_fb[x, c, fi]), 0.0)

        def write0(n, terms, fi=fi):
            for p in range(4):
                if n == 0:
                    s1[p // 2, p % 2, fi] = terms[p]
                else:
                    s1[p // 2, p % 2, fi] = s1[p // 2, p % 2, fi] + terms[p]

        extrapolate(0, fi, frequency[fi] * slow0, valid0, 0, ext_rows, write0)
        for p in range(4):
            s1[p // 2, p % 2, fi] = jnp.where(valid1, s1[p // 2, p % 2, fi], 0.0)
        mid = slice(HALO, HALO + own)
        term = s1[0, 0, fi, mid, :] * s1[1, 0, fi, mid, :] + s1[0, 1, fi, mid, :] * s1[1, 1, fi, mid, :]
        term = jnp.where(live, term, 0.0)
        if fi == 0:
            img_out[0] = term
        else:
            img_out[0] = img_out[0] + term

    image_base = 3 * n_freq + 6

    def image_copy(depth, q, slot_recv, device):
        return pltpu.make_async_remote_copy(
            src_ref=img_out.at[depth, :, pl.ds(q * block, block)], dst_ref=got.at[slot_recv, depth],
            send_sem=send_sem.at[image_base + depth * n_freq + q],
            recv_sem=recv_sem.at[image_base + depth * n_freq + slot_recv],
            device_id=device, device_id_type=MESH,
        )

    def send_image(depth):
        for q in range(n_freq):
            @pl.when(f != q)
            def _():
                image_copy(depth, q, f, (t, q)).start()

    send_image(0)

    for fi in range(nfl):
        for p in range(4):
            tb[0, p] = s1[p // 2, p % 2, fi]
        acc = {}

        def write1(n, terms, acc=acc):
            for p in range(4):
                acc[p] = terms[p] if n == 0 else acc[p] + terms[p]

        extrapolate(1, fi, frequency[fi] * slow1, valid1, HALO, HALO + own, write1)
        result = [jnp.where(live, acc[p], 0.0) for p in range(4)]
        rec_out[0, fi] = result[2]
        rec_out[1, fi] = result[3]
        term = result[0] * result[2] + result[1] * result[3]
        if fi == 0:
            img_out[1] = term
        else:
            img_out[1] = img_out[1] + term

    send_image(1)
    await_sends()
    for depth in range(NDEPTH):
        for q in range(n_freq):
            @pl.when(f != q)
            def _():
                image_copy(depth, q, q, (t, q)).wait_send()
                image_copy(depth, q, q, (t, q)).wait_recv()

    total = None
    for q in range(n_freq):
        mine = img_out[:, :, q * block:(q + 1) * block]
        part = jnp.where(f == q, mine, got[q])
        total = part if total is None else total + part
    image_out[...] = total


def shards(n_tile, n_freq, source_field, receiver_field, slowness, frequency, order_table, filter_coeffs, aperture):
    nc, nfl, own, ncol = source_field.shape
    block = slowness.shape[2]
    ext_rows = own + 2 * HALO
    elements = nc * nfl * 2 * ext_rows * ncol * NDEPTH
    rec_out, image_out = pl.pallas_call(
        functools.partial(migrate_kernel, n_tile, n_freq),
        out_shape=(
            jax.ShapeDtypeStruct((nc, nfl, own, ncol), jnp.float32),
            jax.ShapeDtypeStruct((NDEPTH, own, block), jnp.float32),
        ),
        in_specs=[pl.BlockSpec(memory_space=SMEM)] * 3 + [pl.BlockSpec(memory_space=pl.ANY)] * 4,
        out_specs=(pl.BlockSpec(memory_space=VMEM), pl.BlockSpec(memory_space=VMEM)),
        scratch_shapes=[
            pltpu.VMEM((nc, nfl, own, ncol), jnp.float32),
            pltpu.VMEM((nc, nfl, own, ncol), jnp.float32),
            pltpu.VMEM((n_freq, NDEPTH, own, block), jnp.float32),
            pltpu.VMEM((n_freq, HALO, block), jnp.float32),
            pltpu.VMEM((n_freq, HALO, block), jnp.float32),
            pltpu.VMEM((2, nc, nfl, HALO, ncol), jnp.float32),
            pltpu.VMEM((2, nc, nfl, HALO, ncol), jnp.float32),
            pltpu.VMEM((2, nc, nfl, HALO, ncol), jnp.float32),
            pltpu.VMEM((HALO, block), jnp.float32),
            pltpu.VMEM((2, nc, nfl, ext_rows, ncol), jnp.float32),
            pltpu.VMEM((3, 4, ext_rows, ncol), jnp.float32),
            pltpu.VMEM((NDEPTH, own, ncol), jnp.float32),
            pltpu.VMEM((n_freq, NDEPTH, own, block), jnp.float32),
            pltpu.SMEM((filter_coeffs.shape[2], filter_coeffs.shape[0], filter_coeffs.shape[1]), jnp.float32),
            pltpu.VMEM((nfl, ORDER + 1, 2, ext_rows, ncol), jnp.float32),
            pltpu.VMEM((nfl, ORDER + 1, 2, own, ncol), jnp.float32),
            pltpu.SemaphoreType.DMA((4,)),
            pltpu.SemaphoreType.DMA((3 * n_freq + 6 + NDEPTH * n_freq,)),
            pltpu.SemaphoreType.DMA((3 * n_freq + 6 + NDEPTH * n_freq,)),
        ],
        compiler_params=pltpu.CompilerParams(collective_id=0, has_side_effects=True),
        cost_estimate=pl.CostEstimate(flops=elements * 100, bytes_accessed=elements * 4, transcendentals=0),
    )(aperture, order_table, frequency, jnp.transpose(filter_coeffs, (2, 0, 1)), source_field, receiver_field, slowness)
    return pl.pallas_call(
        passthrough_kernel,
        out_shape=(
            jax.ShapeDtypeStruct(image_out.shape, jnp.float32),
            jax.ShapeDtypeStruct(rec_out.shape, jnp.float32),
        ),
        in_specs=[pl.BlockSpec(memory_space=VMEM)] * 2,
        out_specs=(pl.BlockSpec(memory_space=VMEM), pl.BlockSpec(memory_space=VMEM)),
    )(image_out, rec_out)


def passthrough_kernel(img_in, rec_in, img_out, rec_out):
    img_out[...] = img_in[...]
    rec_out[...] = rec_in[...]


def solution(mesh):
    placed = (
        P(None, "freq", "tile", None),
        P(None, "freq", "tile", None),
        P(None, "tile", "freq"),
        P("freq"),
        P(None, "freq"),
        P(),
        P(),
    )
    return jax.shard_map(
        functools.partial(shards, mesh.shape["tile"], mesh.shape["freq"]),
        mesh=mesh,
        in_specs=placed,
        out_specs=(P(None, "tile", "freq"), P(None, "freq", "tile", None)),
        check_vma=False,
    )
```

```python
import functools

import jax
import jax.numpy as jnp
from jax import lax
from jax.experimental import pallas as pl
from jax.experimental.pallas import tpu as pltpu
from jax.sharding import PartitionSpec as P

ORDER = 4
NDEPTH = 2
POWERS = 3
HALO = 8
MESH = pl.DeviceIdType.MESH
VMEM = pltpu.MemorySpace.VMEM
SMEM = pltpu.MemorySpace.SMEM


def migrate_kernel(n_tile, n_freq, aperture, orders, frequency, coeffs_hbm, src_hbm, rec_hbm, slow_hbm,
                   rec_out, image_out, src_v, rec_v, g_slow, h_sa, h_sb, h_fa, h_fb, up_buf, s_up, s1, tb, img_out,
                   got, coeffs, cf0, cf1, local_sem, send_sem, recv_sem):
    t = lax.axis_index("tile")
    f = lax.axis_index("freq")
    nc, nfl, own, ncol = src_v.shape
    ext_rows = HALO + own + HALO
    block = slow_hbm.shape[2]
    ap = aperture[t]
    has_above = t > 0
    has_below = t < n_tile - 1

    loads = (
        pltpu.make_async_copy(src_hbm, src_v, local_sem.at[0]),
        pltpu.make_async_copy(rec_hbm, rec_v, local_sem.at[1]),
        pltpu.make_async_copy(slow_hbm, g_slow.at[f], local_sem.at[2]),
        pltpu.make_async_copy(coeffs_hbm, coeffs, local_sem.at[3]),
    )
    for copy in loads:
        copy.start()

    @pl.when(t == 0)
    def _():
        h_fa[...] = jnp.zeros_like(h_fa)
        h_sa[...] = jnp.zeros_like(h_sa)

    @pl.when(t == n_tile - 1)
    def _():
        h_fb[...] = jnp.zeros_like(h_fb)
        h_sb[...] = jnp.zeros_like(h_sb)

    barrier = pltpu.get_barrier_semaphore()
    for q in range(n_freq):
        @pl.when(f != q)
        def _():
            pl.semaphore_signal(barrier, 1, device_id=(t, q), device_id_type=MESH)

        @pl.when(has_above)
        def _():
            pl.semaphore_signal(barrier, 1, device_id=(t - 1, q), device_id_type=MESH)

        @pl.when(has_below)
        def _():
            pl.semaphore_signal(barrier, 1, device_id=(t + 1, q), device_id_type=MESH)

    expected = (n_freq - 1) + n_freq * has_above.astype(jnp.int32) + n_freq * has_below.astype(jnp.int32)

    for copy in loads:
        copy.wait()

    own_rows = lax.broadcasted_iota(jnp.int32, (own, ncol), 0)
    own_forward = pltpu.roll(own_rows, 1, 0) == (own_rows + own - 1) % own
    lift = (own + HALO - ap) % own
    drop = ap - HALO

    def last_rows(x, forward):
        return jnp.where(forward, pltpu.roll(x, lift, 0), pltpu.roll(x, drop, 0))[:HALO]

    s_up[...] = last_rows(g_slow[f, 0], own_forward[:, :block])
    fields_v = (src_v, rec_v)
    for fi in range(nfl):
        for x in range(2):
            for c in range(nc):
                up_buf[x, c, fi] = last_rows(fields_v[x][c, fi], own_forward)

    pl.semaphore_wait(barrier, expected)

    def remote(src, dst, slot_send, slot_recv, device):
        return pltpu.make_async_remote_copy(
            src_ref=src, dst_ref=dst, send_sem=send_sem.at[slot_send], recv_sem=recv_sem.at[slot_recv],
            device_id=device, device_id_type=MESH,
        )

    f_lo = (src_hbm.at[:, :, pl.ds(0, HALO), :], rec_hbm.at[:, :, pl.ds(0, HALO), :])
    s_lo = slow_hbm.at[0, pl.ds(0, HALO), :]
    for q in range(n_freq):
        @pl.when(f != q)
        def _():
            remote(slow_hbm, g_slow.at[f], q, f, (t, q)).start()

        @pl.when(has_above)
        def _():
            remote(s_lo, h_sb.at[f], 2 * n_freq + q, 2 * n_freq + f, (t - 1, q)).start()

    field_base = 3 * n_freq

    def lower_copy(x, fi, device):
        return remote(f_lo[x].at[:, fi], h_fb.at[x, :, fi], field_base + 2 + 2 * x + fi,
                      field_base + 2 + 2 * x + fi, device)

    def upper_copy(fi, device):
        return remote(up_buf.at[:, :, fi], h_fa.at[:, :, fi], field_base + fi, field_base + fi, device)

    for fi in range(2):
        @pl.when(has_above)
        def _():
            for x in range(2):
                lower_copy(x, fi, (t - 1, f)).start()

    for q in range(n_freq):
        @pl.when(has_below)
        def _():
            remote(s_up, h_sa.at[f], n_freq + q, n_freq + f, (t + 1, q)).start()

    for fi in range(nfl):
        @pl.when(has_below)
        def _():
            upper_copy(fi, (t + 1, f)).start()

    for q in range(n_freq):
        @pl.when(f != q)
        def _():
            remote(slow_hbm, g_slow.at[q], q, q, (t, q)).wait_recv()

        @pl.when(has_below)
        def _():
            remote(s_lo, h_sb.at[q], 2 * n_freq + q, 2 * n_freq + q, (t + 1, q)).wait_recv()

        @pl.when(has_above)
        def _():
            remote(s_up, h_sa.at[q], n_freq + q, n_freq + q, (t - 1, q)).wait_recv()

    def await_fields(fi):
        @pl.when(has_below)
        def _():
            for x in range(2):
                lower_copy(x, fi, (t + 1, f)).wait_recv()

        @pl.when(has_above)
        def _():
            upper_copy(fi, (t - 1, f)).wait_recv()

    def await_sends():
        for q in range(n_freq):
            @pl.when(f != q)
            def _():
                remote(slow_hbm, g_slow.at[q], q, q, (t, q)).wait_send()

            @pl.when(has_below)
            def _():
                remote(s_up, h_sa.at[q], n_freq + q, n_freq + q, (t + 1, q)).wait_send()

            @pl.when(has_above)
            def _():
                remote(s_lo, h_sb.at[q], 2 * n_freq + q, 2 * n_freq + q, (t - 1, q)).wait_send()

        for fi in range(nfl):
            @pl.when(has_below)
            def _():
                upper_copy(fi, (t + 1, f)).wait_send()

            @pl.when(has_above)
            def _():
                for x in range(2):
                    lower_copy(x, fi, (t - 1, f)).wait_send()

    rows = lax.broadcasted_iota(jnp.int32, (ext_rows, ncol), 0)
    cols = lax.broadcasted_iota(jnp.int32, (ext_rows, ncol), 1)
    left_ok = jnp.abs(pltpu.roll(cols, 1, 1) - cols) == 1
    right_ok = jnp.abs(pltpu.roll(cols, ncol - 1, 1) - cols) == 1
    forward = pltpu.roll(rows, 1, 0) == (rows + ext_rows - 1) % ext_rows
    lower_start = HALO + ap
    top_part = rows < lower_start

    def in_band(lo, hi):
        return (rows >= lo) & (rows < hi)

    valid0 = (in_band(0, HALO) & has_above) | in_band(HALO, lower_start) | (
        in_band(lower_start, lower_start + HALO) & has_below)
    reach = HALO // 2
    valid1 = (in_band(HALO - reach, HALO) & has_above) | in_band(HALO, lower_start) | (
        in_band(lower_start, lower_start + reach) & has_below)
    live = lax.broadcasted_iota(jnp.int32, (own, ncol), 0) < ap
    zeros_tail = jnp.zeros((ext_rows - HALO, ncol), jnp.float32)

    def place_lower(lower8):
        padded = jnp.concatenate([lower8, zeros_tail], axis=0)
        ahead = pltpu.roll(padded, lower_start, 0)
        behind = pltpu.roll(padded, ext_rows - lower_start, 0)
        return jnp.where(forward, ahead, behind)

    def joined(upper8, own_rows, lower8):
        top = jnp.concatenate([upper8, own_rows, jnp.zeros((HALO, ncol), jnp.float32)], axis=0)
        return jnp.where(top_part, top, place_lower(lower8))

    def columns_of(pieces):
        return jnp.concatenate(pieces, axis=1)

    slow0 = joined(
        columns_of([h_sa[q] for q in range(n_freq)]),
        columns_of([g_slow[q, 0] for q in range(n_freq)]),
        columns_of([h_sb[q] for q in range(n_freq)]),
    )
    slow0 = jnp.where(valid0, slow0, 0.0)
    slow1 = columns_of([g_slow[q, 1] for q in range(n_freq)])

    edge = 128

    def masked_side(b):
        ahead = pltpu.roll(b, 1, 1)
        behind = pltpu.roll(b, ncol - 1, 1)

        def guarded(lo, hi):
            return jnp.where(left_ok[:, lo:hi], ahead[:, lo:hi], 0.0) + jnp.where(
                right_ok[:, lo:hi], behind[:, lo:hi], 0.0)

        middle = ahead[:, edge:ncol - edge] + behind[:, edge:ncol - edge]
        return jnp.concatenate([guarded(0, edge), middle, guarded(ncol - edge, ncol)], axis=1)

    def chebyshev_step(v, prev):
        pair = pltpu.roll(v, 1, 0) + pltpu.roll(v, ext_rows - 1, 0)
        blur = 0.25 * pair + 0.5 * v
        side = masked_side(blur)
        if prev is None:
            return 0.5 * side + blur - v
        return side + 0.5 * pair - v - prev

    def coefficient_of(depth, fi, n, wavenumber):
        active = jnp.where(orders[depth, fi] >= n, 1.0, 0.0).astype(jnp.float32)
        scaled = [[coeffs[m, c, n] * active for m in range(POWERS)] for c in range(2)]
        coef_re = scaled[0][POWERS - 1] * wavenumber + scaled[0][POWERS - 2]
        coef_im = scaled[1][POWERS - 1] * wavenumber + scaled[1][POWERS - 2]
        for m in range(POWERS - 3, -1, -1):
            coef_re = coef_re * wavenumber + scaled[0][m]
            coef_im = coef_im * wavenumber + scaled[1][m]
        return coef_re, coef_im

    for fi in range(nfl):
        wave0 = frequency[fi] * slow0
        wave1 = frequency[fi] * slow1
        for n in range(ORDER + 1):
            cf0[fi, n, 0], cf0[fi, n, 1] = coefficient_of(0, fi, n, wave0)
            cf1[fi, n, 0], cf1[fi, n, 1] = coefficient_of(1, fi, n, wave1)

    def coefficient(depth, fi, n, wavenumber):
        table = cf0 if depth == 0 else cf1
        return table[fi, n, 0], table[fi, n, 1]

    def extrapolate(depth, fi, wavenumber, valid, lo, hi, write):
        for n in range(ORDER + 1):
            slot = n % 3
            if n >= 1:
                cur, prev = (n - 1) % 3, (n - 2) % 3
                for p in range(4):
                    g = chebyshev_step(tb[cur, p], tb[prev, p] if n > 1 else None)
                    tb[slot, p] = jnp.where(valid, g, 0.0)
            coef_re, coef_im = coefficient(depth, fi, n, wavenumber)
            s_re = tb[slot, 0, lo:hi, :]
            s_im = tb[slot, 1, lo:hi, :]
            r_re = tb[slot, 2, lo:hi, :]
            r_im = tb[slot, 3, lo:hi, :]
            terms = (
                coef_re * s_re + coef_im * s_im,
                coef_re * s_im - coef_im * s_re,
                coef_re * r_re - coef_im * r_im,
                coef_re * r_im + coef_im * r_re,
            )
            write(n, terms)

    fields = (src_v, rec_v)
    for fi in range(nfl):
        await_fields(fi)
        for p in range(4):
            x, c = p // 2, p % 2
            tb[0, p] = jnp.where(valid0, joined(h_fa[x, c, fi], fields[x][c, fi], h_fb[x, c, fi]), 0.0)

        def write0(n, terms, fi=fi):
            for p in range(4):
                if n == 0:
                    s1[p // 2, p % 2, fi] = terms[p]
                else:
                    s1[p // 2, p % 2, fi] = s1[p // 2, p % 2, fi] + terms[p]

        extrapolate(0, fi, frequency[fi] * slow0, valid0, 0, ext_rows, write0)
        for p in range(4):
            s1[p // 2, p % 2, fi] = jnp.where(valid1, s1[p // 2, p % 2, fi], 0.0)
        mid = slice(HALO, HALO + own)
        term = s1[0, 0, fi, mid, :] * s1[1, 0, fi, mid, :] + s1[0, 1, fi, mid, :] * s1[1, 1, fi, mid, :]
        term = jnp.where(live, term, 0.0)
        if fi == 0:
            img_out[0] = term
        else:
            img_out[0] = img_out[0] + term

    image_base = 3 * n_freq + 6

    def image_copy(depth, q, slot_recv, device):
        return pltpu.make_async_remote_copy(
            src_ref=img_out.at[depth, :, pl.ds(q * block, block)], dst_ref=got.at[slot_recv, depth],
            send_sem=send_sem.at[image_base + depth * n_freq + q],
            recv_sem=recv_sem.at[image_base + depth * n_freq + slot_recv],
            device_id=device, device_id_type=MESH,
        )

    def send_image(depth):
        for q in range(n_freq):
            @pl.when(f != q)
            def _():
                image_copy(depth, q, f, (t, q)).start()

    send_image(0)

    for fi in range(nfl):
        for p in range(4):
            tb[0, p] = s1[p // 2, p % 2, fi]
        acc = {}

        def write1(n, terms, acc=acc):
            for p in range(4):
                acc[p] = terms[p] if n == 0 else acc[p] + terms[p]

        extrapolate(1, fi, frequency[fi] * slow1, valid1, HALO, HALO + own, write1)
        result = [jnp.where(live, acc[p], 0.0) for p in range(4)]
        rec_out[0, fi] = result[2]
        rec_out[1, fi] = result[3]
        term = result[0] * result[2] + result[1] * result[3]
        if fi == 0:
            img_out[1] = term
        else:
            img_out[1] = img_out[1] + term

    send_image(1)
    for depth in range(NDEPTH):
        for q in range(n_freq):
            @pl.when(f != q)
            def _():
                image_copy(depth, q, q, (t, q)).wait_recv()

        total = None
        for q in range(n_freq):
            mine = img_out[depth, :, q * block:(q + 1) * block]
            part = jnp.where(f == q, mine, got[q, depth])
            total = part if total is None else total + part
        image_out[depth] = total

    for depth in range(NDEPTH):
        for q in range(n_freq):
            @pl.when(f != q)
            def _():
                image_copy(depth, q, q, (t, q)).wait_send()
    await_sends()


def shards(n_tile, n_freq, source_field, receiver_field, slowness, frequency, order_table, filter_coeffs, aperture):
    nc, nfl, own, ncol = source_field.shape
    block = slowness.shape[2]
    ext_rows = own + 2 * HALO
    elements = nc * nfl * 2 * ext_rows * ncol * NDEPTH
    rec_out, image_out = pl.pallas_call(
        functools.partial(migrate_kernel, n_tile, n_freq),
        out_shape=(
            jax.ShapeDtypeStruct((nc, nfl, own, ncol), jnp.float32),
            jax.ShapeDtypeStruct((NDEPTH, own, block), jnp.float32),
        ),
        in_specs=[pl.BlockSpec(memory_space=SMEM)] * 3 + [pl.BlockSpec(memory_space=pl.ANY)] * 4,
        out_specs=(pl.BlockSpec(memory_space=VMEM), pl.BlockSpec(memory_space=VMEM)),
        scratch_shapes=[
            pltpu.VMEM((nc, nfl, own, ncol), jnp.float32),
            pltpu.VMEM((nc, nfl, own, ncol), jnp.float32),
            pltpu.VMEM((n_freq, NDEPTH, own, block), jnp.float32),
            pltpu.VMEM((n_freq, HALO, block), jnp.float32),
            pltpu.VMEM((n_freq, HALO, block), jnp.float32),
            pltpu.VMEM((2, nc, nfl, HALO, ncol), jnp.float32),
            pltpu.VMEM((2, nc, nfl, HALO, ncol), jnp.float32),
            pltpu.VMEM((2, nc, nfl, HALO, ncol), jnp.float32),
            pltpu.VMEM((HALO, block), jnp.float32),
            pltpu.VMEM((2, nc, nfl, ext_rows, ncol), jnp.float32),
            pltpu.VMEM((3, 4, ext_rows, ncol), jnp.float32),
            pltpu.VMEM((NDEPTH, own, ncol), jnp.float32),
            pltpu.VMEM((n_freq, NDEPTH, own, block), jnp.float32),
            pltpu.SMEM((filter_coeffs.shape[2], filter_coeffs.shape[0], filter_coeffs.shape[1]), jnp.float32),
            pltpu.VMEM((nfl, ORDER + 1, 2, ext_rows, ncol), jnp.float32),
            pltpu.VMEM((nfl, ORDER + 1, 2, own, ncol), jnp.float32),
            pltpu.SemaphoreType.DMA((4,)),
            pltpu.SemaphoreType.DMA((3 * n_freq + 6 + NDEPTH * n_freq,)),
            pltpu.SemaphoreType.DMA((3 * n_freq + 6 + NDEPTH * n_freq,)),
        ],
        compiler_params=pltpu.CompilerParams(collective_id=0, has_side_effects=True),
        cost_estimate=pl.CostEstimate(flops=elements * 100, bytes_accessed=elements * 4, transcendentals=0),
    )(aperture, order_table, frequency, jnp.transpose(filter_coeffs, (2, 0, 1)), source_field, receiver_field, slowness)
    return pl.pallas_call(
        passthrough_kernel,
        out_shape=(
            jax.ShapeDtypeStruct(image_out.shape, jnp.float32),
            jax.ShapeDtypeStruct(rec_out.shape, jnp.float32),
        ),
        in_specs=[pl.BlockSpec(memory_space=VMEM)] * 2,
        out_specs=(pl.BlockSpec(memory_space=VMEM), pl.BlockSpec(memory_space=VMEM)),
    )(image_out, rec_out)


def passthrough_kernel(img_in, rec_in, img_out, rec_out):
    img_out[...] = img_in[...]
    rec_out[...] = rec_in[...]


def solution(mesh):
    placed = (
        P(None, "freq", "tile", None),
        P(None, "freq", "tile", None),
        P(None, "tile", "freq"),
        P("freq"),
        P(None, "freq"),
        P(),
        P(),
    )
    return jax.shard_map(
        functools.partial(shards, mesh.shape["tile"], mesh.shape["freq"]),
        mesh=mesh,
        in_specs=placed,
        out_specs=(P(None, "tile", "freq"), P(None, "freq", "tile", None)),
        check_vma=False,
    )
```

```python
import functools

import jax
import jax.numpy as jnp
from jax import lax
from jax.experimental import pallas as pl
from jax.experimental.pallas import tpu as pltpu
from jax.sharding import PartitionSpec as P

ORDER = 4
NDEPTH = 2
POWERS = 3
HALO = 8
MESH = pl.DeviceIdType.MESH
VMEM = pltpu.MemorySpace.VMEM
SMEM = pltpu.MemorySpace.SMEM


def migrate_kernel(n_tile, n_freq, aperture, orders, frequency, coeffs_hbm, src_hbm, rec_hbm, slow_hbm,
                   rec_out, image_out, src_v, rec_v, g_slow, h_sa, h_sb, h_fa, h_fb, up_buf, s_up, s1, tb, img_out,
                   got, coeffs, cf0, cf1, local_sem, send_sem, recv_sem):
    t = lax.axis_index("tile")
    f = lax.axis_index("freq")
    nc, nfl, own, ncol = src_v.shape
    ext_rows = HALO + own + HALO
    block = slow_hbm.shape[2]
    ap = aperture[t]
    has_above = t > 0
    has_below = t < n_tile - 1

    loads = (
        pltpu.make_async_copy(src_hbm, src_v, local_sem.at[0]),
        pltpu.make_async_copy(rec_hbm, rec_v, local_sem.at[1]),
        pltpu.make_async_copy(slow_hbm, g_slow.at[f], local_sem.at[2]),
        pltpu.make_async_copy(coeffs_hbm, coeffs, local_sem.at[3]),
    )
    for copy in loads:
        copy.start()

    @pl.when(t == 0)
    def _():
        h_fa[...] = jnp.zeros_like(h_fa)
        h_sa[...] = jnp.zeros_like(h_sa)

    @pl.when(t == n_tile - 1)
    def _():
        h_fb[...] = jnp.zeros_like(h_fb)
        h_sb[...] = jnp.zeros_like(h_sb)

    barrier = pltpu.get_barrier_semaphore()
    for q in range(n_freq):
        @pl.when(f != q)
        def _():
            pl.semaphore_signal(barrier, 1, device_id=(t, q), device_id_type=MESH)

        @pl.when(has_above)
        def _():
            pl.semaphore_signal(barrier, 1, device_id=(t - 1, q), device_id_type=MESH)

        @pl.when(has_below)
        def _():
            pl.semaphore_signal(barrier, 1, device_id=(t + 1, q), device_id_type=MESH)

    expected = (n_freq - 1) + n_freq * has_above.astype(jnp.int32) + n_freq * has_below.astype(jnp.int32)

    for copy in loads:
        copy.wait()

    own_rows = lax.broadcasted_iota(jnp.int32, (own, ncol), 0)
    own_forward = pltpu.roll(own_rows, 1, 0) == (own_rows + own - 1) % own
    lift = (own + HALO - ap) % own
    drop = ap - HALO

    def last_rows(x, forward):
        return jnp.where(forward, pltpu.roll(x, lift, 0), pltpu.roll(x, drop, 0))[:HALO]

    s_up[...] = last_rows(g_slow[f, 0], own_forward[:, :block])
    fields_v = (src_v, rec_v)
    for fi in range(nfl):
        for x in range(2):
            for c in range(nc):
                up_buf[x, c, fi] = last_rows(fields_v[x][c, fi], own_forward)

    pl.semaphore_wait(barrier, expected)

    def remote(src, dst, slot_send, slot_recv, device):
        return pltpu.make_async_remote_copy(
            src_ref=src, dst_ref=dst, send_sem=send_sem.at[slot_send], recv_sem=recv_sem.at[slot_recv],
            device_id=device, device_id_type=MESH,
        )

    f_lo = (src_hbm.at[:, :, pl.ds(0, HALO), :], rec_hbm.at[:, :, pl.ds(0, HALO), :])
    s_lo = slow_hbm.at[0, pl.ds(0, HALO), :]
    for q in range(n_freq):
        @pl.when(f != q)
        def _():
            remote(slow_hbm, g_slow.at[f], q, f, (t, q)).start()

        @pl.when(has_above)
        def _():
            remote(s_lo, h_sb.at[f], 2 * n_freq + q, 2 * n_freq + f, (t - 1, q)).start()

    field_base = 3 * n_freq

    def lower_copy(x, fi, device):
        return remote(f_lo[x].at[:, fi], h_fb.at[x, :, fi], field_base + 2 + 2 * x + fi,
                      field_base + 2 + 2 * x + fi, device)

    def upper_copy(fi, device):
        return remote(up_buf.at[:, :, fi], h_fa.at[:, :, fi], field_base + fi, field_base + fi, device)

    for fi in range(2):
        @pl.when(has_above)
        def _():
            for x in range(2):
                lower_copy(x, fi, (t - 1, f)).start()

    for q in range(n_freq):
        @pl.when(has_below)
        def _():
            remote(s_up, h_sa.at[f], n_freq + q, n_freq + f, (t + 1, q)).start()

    for fi in range(nfl):
        @pl.when(has_below)
        def _():
            upper_copy(fi, (t + 1, f)).start()

    for q in range(n_freq):
        @pl.when(f != q)
        def _():
            remote(slow_hbm, g_slow.at[q], q, q, (t, q)).wait_recv()

    def await_slowness_halos():
        for q in range(n_freq):
            @pl.when(has_below)
            def _():
                remote(s_lo, h_sb.at[q], 2 * n_freq + q, 2 * n_freq + q, (t + 1, q)).wait_recv()

            @pl.when(has_above)
            def _():
                remote(s_up, h_sa.at[q], n_freq + q, n_freq + q, (t - 1, q)).wait_recv()

    def await_fields(fi):
        @pl.when(has_below)
        def _():
            for x in range(2):
                lower_copy(x, fi, (t + 1, f)).wait_recv()

        @pl.when(has_above)
        def _():
            upper_copy(fi, (t - 1, f)).wait_recv()

    def await_sends():
        for q in range(n_freq):
            @pl.when(f != q)
            def _():
                remote(slow_hbm, g_slow.at[q], q, q, (t, q)).wait_send()

            @pl.when(has_below)
            def _():
                remote(s_up, h_sa.at[q], n_freq + q, n_freq + q, (t + 1, q)).wait_send()

            @pl.when(has_above)
            def _():
                remote(s_lo, h_sb.at[q], 2 * n_freq + q, 2 * n_freq + q, (t - 1, q)).wait_send()

        for fi in range(nfl):
            @pl.when(has_below)
            def _():
                upper_copy(fi, (t + 1, f)).wait_send()

            @pl.when(has_above)
            def _():
                for x in range(2):
                    lower_copy(x, fi, (t - 1, f)).wait_send()

    rows = lax.broadcasted_iota(jnp.int32, (ext_rows, ncol), 0)
    cols = lax.broadcasted_iota(jnp.int32, (ext_rows, ncol), 1)
    left_ok = jnp.abs(pltpu.roll(cols, 1, 1) - cols) == 1
    right_ok = jnp.abs(pltpu.roll(cols, ncol - 1, 1) - cols) == 1
    forward = pltpu.roll(rows, 1, 0) == (rows + ext_rows - 1) % ext_rows
    lower_start = HALO + ap
    top_part = rows < lower_start

    def in_band(lo, hi):
        return (rows >= lo) & (rows < hi)

    valid0 = (in_band(0, HALO) & has_above) | in_band(HALO, lower_start) | (
        in_band(lower_start, lower_start + HALO) & has_below)
    reach = HALO // 2
    valid1 = (in_band(HALO - reach, HALO) & has_above) | in_band(HALO, lower_start) | (
        in_band(lower_start, lower_start + reach) & has_below)
    live = lax.broadcasted_iota(jnp.int32, (own, ncol), 0) < ap
    zeros_tail = jnp.zeros((ext_rows - HALO, ncol), jnp.float32)

    def place_lower(lower8):
        padded = jnp.concatenate([lower8, zeros_tail], axis=0)
        ahead = pltpu.roll(padded, lower_start, 0)
        behind = pltpu.roll(padded, ext_rows - lower_start, 0)
        return jnp.where(forward, ahead, behind)

    def joined(upper8, own_rows, lower8):
        top = jnp.concatenate([upper8, own_rows, jnp.zeros((HALO, ncol), jnp.float32)], axis=0)
        return jnp.where(top_part, top, place_lower(lower8))

    def columns_of(pieces):
        return jnp.concatenate(pieces, axis=1)

    def coefficient_of(depth, fi, n, wavenumber):
        active = jnp.where(orders[depth, fi] >= n, 1.0, 0.0).astype(jnp.float32)
        scaled = [[coeffs[m, c, n] * active for m in range(POWERS)] for c in range(2)]
        coef_re = scaled[0][POWERS - 1] * wavenumber + scaled[0][POWERS - 2]
        coef_im = scaled[1][POWERS - 1] * wavenumber + scaled[1][POWERS - 2]
        for m in range(POWERS - 3, -1, -1):
            coef_re = coef_re * wavenumber + scaled[0][m]
            coef_im = coef_im * wavenumber + scaled[1][m]
        return coef_re, coef_im

    slow1 = columns_of([g_slow[q, 1] for q in range(n_freq)])
    for fi in range(nfl):
        wave1 = frequency[fi] * slow1
        for n in range(ORDER + 1):
            cf1[fi, n, 0], cf1[fi, n, 1] = coefficient_of(1, fi, n, wave1)

    await_slowness_halos()
    slow0 = joined(
        columns_of([h_sa[q] for q in range(n_freq)]),
        columns_of([g_slow[q, 0] for q in range(n_freq)]),
        columns_of([h_sb[q] for q in range(n_freq)]),
    )
    slow0 = jnp.where(valid0, slow0, 0.0)

    edge = 128

    def masked_side(b):
        ahead = pltpu.roll(b, 1, 1)
        behind = pltpu.roll(b, ncol - 1, 1)

        def guarded(lo, hi):
            return jnp.where(left_ok[:, lo:hi], ahead[:, lo:hi], 0.0) + jnp.where(
                right_ok[:, lo:hi], behind[:, lo:hi], 0.0)

        middle = ahead[:, edge:ncol - edge] + behind[:, edge:ncol - edge]
        return jnp.concatenate([guarded(0, edge), middle, guarded(ncol - edge, ncol)], axis=1)

    def chebyshev_step(v, prev):
        pair = pltpu.roll(v, 1, 0) + pltpu.roll(v, ext_rows - 1, 0)
        blur = 0.25 * pair + 0.5 * v
        side = masked_side(blur)
        if prev is None:
            return 0.5 * side + blur - v
        return side + 0.5 * pair - v - prev

    for fi in range(nfl):
        wave0 = frequency[fi] * slow0
        for n in range(ORDER + 1):
            cf0[fi, n, 0], cf0[fi, n, 1] = coefficient_of(0, fi, n, wave0)

    def coefficient(depth, fi, n, wavenumber):
        table = cf0 if depth == 0 else cf1
        return table[fi, n, 0], table[fi, n, 1]

    def extrapolate(depth, fi, wavenumber, valid, lo, hi, write):
        for n in range(ORDER + 1):
            slot = n % 3
            if n >= 1:
                cur, prev = (n - 1) % 3, (n - 2) % 3
                for p in range(4):
                    g = chebyshev_step(tb[cur, p], tb[prev, p] if n > 1 else None)
                    tb[slot, p] = jnp.where(valid, g, 0.0)
            coef_re, coef_im = coefficient(depth, fi, n, wavenumber)
            s_re = tb[slot, 0, lo:hi, :]
            s_im = tb[slot, 1, lo:hi, :]
            r_re = tb[slot, 2, lo:hi, :]
            r_im = tb[slot, 3, lo:hi, :]
            terms = (
                coef_re * s_re + coef_im * s_im,
                coef_re * s_im - coef_im * s_re,
                coef_re * r_re - coef_im * r_im,
                coef_re * r_im + coef_im * r_re,
            )
            write(n, terms)

    fields = (src_v, rec_v)
    for fi in range(nfl):
        await_fields(fi)
        for p in range(4):
            x, c = p // 2, p % 2
            tb[0, p] = jnp.where(valid0, joined(h_fa[x, c, fi], fields[x][c, fi], h_fb[x, c, fi]), 0.0)

        def write0(n, terms, fi=fi):
            for p in range(4):
                if n == 0:
                    s1[p // 2, p % 2, fi] = terms[p]
                else:
                    s1[p // 2, p % 2, fi] = s1[p // 2, p % 2, fi] + terms[p]

        extrapolate(0, fi, frequency[fi] * slow0, valid0, 0, ext_rows, write0)
        for p in range(4):
            s1[p // 2, p % 2, fi] = jnp.where(valid1, s1[p // 2, p % 2, fi], 0.0)
        mid = slice(HALO, HALO + own)
        term = s1[0, 0, fi, mid, :] * s1[1, 0, fi, mid, :] + s1[0, 1, fi, mid, :] * s1[1, 1, fi, mid, :]
        term = jnp.where(live, term, 0.0)
        if fi == 0:
            img_out[0] = term
        else:
            img_out[0] = img_out[0] + term

    image_base = 3 * n_freq + 6

    def image_copy(depth, q, slot_recv, device):
        return pltpu.make_async_remote_copy(
            src_ref=img_out.at[depth, :, pl.ds(q * block, block)], dst_ref=got.at[slot_recv, depth],
            send_sem=send_sem.at[image_base + depth * n_freq + q],
            recv_sem=recv_sem.at[image_base + depth * n_freq + slot_recv],
            device_id=device, device_id_type=MESH,
        )

    def send_image(depth):
        for q in range(n_freq):
            @pl.when(f != q)
            def _():
                image_copy(depth, q, f, (t, q)).start()

    send_image(0)

    for fi in range(nfl):
        for p in range(4):
            tb[0, p] = s1[p // 2, p % 2, fi]
        acc = {}

        def write1(n, terms, acc=acc):
            for p in range(4):
                acc[p] = terms[p] if n == 0 else acc[p] + terms[p]

        extrapolate(1, fi, frequency[fi] * slow1, valid1, HALO, HALO + own, write1)
        result = [jnp.where(live, acc[p], 0.0) for p in range(4)]
        rec_out[0, fi] = result[2]
        rec_out[1, fi] = result[3]
        term = result[0] * result[2] + result[1] * result[3]
        if fi == 0:
            img_out[1] = term
        else:
            img_out[1] = img_out[1] + term

    send_image(1)
    for depth in range(NDEPTH):
        for q in range(n_freq):
            @pl.when(f != q)
            def _():
                image_copy(depth, q, q, (t, q)).wait_recv()

        total = None
        for q in range(n_freq):
            mine = img_out[depth, :, q * block:(q + 1) * block]
            part = jnp.where(f == q, mine, got[q, depth])
            total = part if total is None else total + part
        image_out[depth] = total

    for depth in range(NDEPTH):
        for q in range(n_freq):
            @pl.when(f != q)
            def _():
                image_copy(depth, q, q, (t, q)).wait_send()
    await_sends()


def shards(n_tile, n_freq, source_field, receiver_field, slowness, frequency, order_table, filter_coeffs, aperture):
    nc, nfl, own, ncol = source_field.shape
    block = slowness.shape[2]
    ext_rows = own + 2 * HALO
    elements = nc * nfl * 2 * ext_rows * ncol * NDEPTH
    rec_out, image_out = pl.pallas_call(
        functools.partial(migrate_kernel, n_tile, n_freq),
        out_shape=(
            jax.ShapeDtypeStruct((nc, nfl, own, ncol), jnp.float32),
            jax.ShapeDtypeStruct((NDEPTH, own, block), jnp.float32),
        ),
        in_specs=[pl.BlockSpec(memory_space=SMEM)] * 3 + [pl.BlockSpec(memory_space=pl.ANY)] * 4,
        out_specs=(pl.BlockSpec(memory_space=VMEM), pl.BlockSpec(memory_space=VMEM)),
        scratch_shapes=[
            pltpu.VMEM((nc, nfl, own, ncol), jnp.float32),
            pltpu.VMEM((nc, nfl, own, ncol), jnp.float32),
            pltpu.VMEM((n_freq, NDEPTH, own, block), jnp.float32),
            pltpu.VMEM((n_freq, HALO, block), jnp.float32),
            pltpu.VMEM((n_freq, HALO, block), jnp.float32),
            pltpu.VMEM((2, nc, nfl, HALO, ncol), jnp.float32),
            pltpu.VMEM((2, nc, nfl, HALO, ncol), jnp.float32),
            pltpu.VMEM((2, nc, nfl, HALO, ncol), jnp.float32),
            pltpu.VMEM((HALO, block), jnp.float32),
            pltpu.VMEM((2, nc, nfl, ext_rows, ncol), jnp.float32),
            pltpu.VMEM((3, 4, ext_rows, ncol), jnp.float32),
            pltpu.VMEM((NDEPTH, own, ncol), jnp.float32),
            pltpu.VMEM((n_freq, NDEPTH, own, block), jnp.float32),
            pltpu.SMEM((filter_coeffs.shape[2], filter_coeffs.shape[0], filter_coeffs.shape[1]), jnp.float32),
            pltpu.VMEM((nfl, ORDER + 1, 2, ext_rows, ncol), jnp.float32),
            pltpu.VMEM((nfl, ORDER + 1, 2, own, ncol), jnp.float32),
            pltpu.SemaphoreType.DMA((4,)),
            pltpu.SemaphoreType.DMA((3 * n_freq + 6 + NDEPTH * n_freq,)),
            pltpu.SemaphoreType.DMA((3 * n_freq + 6 + NDEPTH * n_freq,)),
        ],
        compiler_params=pltpu.CompilerParams(collective_id=0, has_side_effects=True),
        cost_estimate=pl.CostEstimate(flops=elements * 100, bytes_accessed=elements * 4, transcendentals=0),
    )(aperture, order_table, frequency, jnp.transpose(filter_coeffs, (2, 0, 1)), source_field, receiver_field, slowness)
    return pl.pallas_call(
        passthrough_kernel,
        out_shape=(
            jax.ShapeDtypeStruct(image_out.shape, jnp.float32),
            jax.ShapeDtypeStruct(rec_out.shape, jnp.float32),
        ),
        in_specs=[pl.BlockSpec(memory_space=VMEM)] * 2,
        out_specs=(pl.BlockSpec(memory_space=VMEM), pl.BlockSpec(memory_space=VMEM)),
    )(image_out, rec_out)


def passthrough_kernel(img_in, rec_in, img_out, rec_out):
    img_out[...] = img_in[...]
    rec_out[...] = rec_in[...]


def solution(mesh):
    placed = (
        P(None, "freq", "tile", None),
        P(None, "freq", "tile", None),
        P(None, "tile", "freq"),
        P("freq"),
        P(None, "freq"),
        P(),
        P(),
    )
    return jax.shard_map(
        functools.partial(shards, mesh.shape["tile"], mesh.shape["freq"]),
        mesh=mesh,
        in_specs=placed,
        out_specs=(P(None, "tile", "freq"), P(None, "freq", "tile", None)),
        check_vma=False,
    )
```
